32 devices in a mesh: dp: 8 (over y, x, core), shard: 4 (over z).
Axes of the slice: x: 2, y: 2, z: 4, core: 2. Of those that a mesh axis runs over, the one named last changes fastest.
Arguments:
- tokens: bfloat16 [16384, 1024], P(('dp', 'shard')), may hold values from -9 to 9
- lengths: int32 [32, 2], P(('dp', 'shard')), may hold values from 8 to 256, as said below
- w_qkv: bfloat16 [2, 1024, 3072], P(None, ('dp', 'shard')), may hold values from -0.1875 to 0.1875
- w_out: bfloat16 [2, 1024, 1024], P(None, ('dp', 'shard')), may hold values from -2 to 2
- w_up: bfloat16 [2, 1024, 4096], P(None, ('dp', 'shard')), may hold values from -0.1875 to 0.1875
- w_down: bfloat16 [2, 4096, 1024], P(None, ('dp', 'shard')), may hold values from -0.09375 to 0.09375
- ln_gain: float32 [2, 2, 1024], replicated, may hold values from 0.5 to 1.5
- bias_qv: float32 [2, 2, 1024], replicated, may hold values from -3 to 3
- bias_out: float32 [2, 1024], replicated, may hold values from -3 to 3
- ln_bias: float32 [2, 2, 1024], replicated, may hold values from -3 to 3
- bias_up: float32 [2, 4096], replicated, may hold values from -3 to 3
- bias_down: float32 [2, 1024], replicated, may hold values from -3 to 3
- cotangent: bfloat16 [16384, 1024], P(('dp', 'shard')), may hold values from -6 to 6
Outputs:
- activations: bfloat16 [16384, 1024], P(('dp', 'shard'))
- input_grad: float32 [16384, 1024], P(('dp', 'shard'))
- grad_bias_qv: float32 [2, 2, 1024], replicated
- grad_bias_out: float32 [2, 1024], replicated
- grad_ln_bias: float32 [2, 2, 1024], replicated
- grad_bias_up: float32 [2, 4096], replicated
- grad_bias_down: float32 [2, 1024], replicated
- rms_values: float32 [2, 3], replicated
The draws below stay inside these ranges and needn't reach their ends.
Inputs may be any that keep to these rules, and one draw needn't show every extreme that they name: `lengths`: each packed row holds two sentences from its first slot on, one of exactly 256 tokens; the remaining slots are padding.
All inputs are finite; a program needn't handle non-finite values.
Results may differ from the reference program's by a relative error of at most 0.022.
Values may be sent and summed in bfloat16 or wider, within the bound.
A program may use at most 256 MiB of HBM per device.

```python
import jax
import jax.numpy as jnp
from jax import lax

D = 1024
HEADS = 16
HEAD_DIM = 64
FF = 4096
LAYERS = 2
ROW = 512
SENT_MOST = 256
NROWS = 32
TOKENS = 16384


def draw_tokens(key, part):
    row_pos = jnp.arange(TOKENS, dtype=jnp.float32) / (TOKENS - 1)
    base = jnp.clip(jax.random.normal(key, (TOKENS, D), jnp.float32), -5.0, 5.0)
    row_scale = 0.6 + 1.2 * row_pos
    return (base * row_scale[:, None]).astype(jnp.bfloat16)


def draw_lengths(key, part):
    row_ids = jnp.arange(NROWS, dtype=jnp.int32)
    other_len = jax.random.randint(key, (NROWS,), 8, SENT_MOST + 1, dtype=jnp.int32)
    longest = jnp.full((NROWS,), SENT_MOST, dtype=jnp.int32)
    flipped = row_ids % 2 == 0
    first_len = jnp.where(flipped, longest, other_len)
    second_len = jnp.where(flipped, other_len, longest)
    return jnp.stack([first_len, second_len], axis=1).astype(jnp.int32)


def levels(own_key, extent, shards, low, top_value):
    level, own = 1.0, jax.random.fold_in(own_key, 6)
    for dim, parts in shards:
        draws = jnp.exp(jax.random.uniform(jax.random.fold_in(own, dim), (parts,), jnp.float32, low / len(shards), top_value / len(shards)))
        level = level * jnp.repeat(draws, extent[dim] // parts).reshape([-1 if axis == dim else 1 for axis in range(len(extent))])
    return level


def normal_values(rng, dims, width, bound, split=(), kind=jnp.bfloat16):
    array = jax.random.normal(rng, dims, jnp.float32) * width
    if len(split) > 0:
        array = levels(rng, dims, split, -0.22, 0.18) * array
    return jnp.clip(array, min=-bound, max=bound).astype(kind)


def setup_inputs(seed: int = 0) -> dict:
    streams_of = jax.random.split(jax.random.key(seed), 14)
    return {
        "tokens": draw_tokens(jax.random.fold_in(streams_of[13], 71), 0),
        "lengths": draw_lengths(jax.random.fold_in(streams_of[13], 71), 0),
        "w_qkv": normal_values(streams_of[2], (LAYERS, D, 3 * D), D ** -0.5, 0.1875, ((1, 32),)),
        "w_out": normal_values(streams_of[3], (LAYERS, D, D), (D // 128) ** -0.5, 2.0, ((1, 32),)),
        "w_up": normal_values(streams_of[4], (LAYERS, D, FF), D ** -0.5, 0.1875, ((1, 32),)),
        "w_down": normal_values(streams_of[5], (LAYERS, FF, D), FF ** -0.5, 0.09375, ((1, 32),)),
        "ln_gain": jnp.clip(1.0 + 0.1 * jax.random.normal(streams_of[6], (LAYERS, 2, D), jnp.float32), 0.5, 1.5),
        "bias_qv": normal_values(streams_of[7], (LAYERS, 2, D), 0.5, 3.0, (), jnp.float32),
        "bias_out": normal_values(streams_of[8], (LAYERS, D), 0.5, 3.0, (), jnp.float32),
        "ln_bias": normal_values(streams_of[9], (LAYERS, 2, D), 0.5, 3.0, (), jnp.float32),
        "bias_up": normal_values(streams_of[10], (LAYERS, FF), 0.5, 3.0, (), jnp.float32),
        "bias_down": normal_values(streams_of[11], (LAYERS, D), 0.5, 3.0, (), jnp.float32),
        "cotangent": normal_values(streams_of[12], (TOKENS, D), 1.0, 6.0, ((0, 32),)),
    }


@jax.custom_vjp
def low(v):
    return lax.optimization_barrier(v.astype(jnp.bfloat16)).astype(jnp.float32)

@jax.custom_vjp
def low_back(v):
    return v

def low_keep(v):
    return (low(v), None)

def low_pass(kept, grad):
    return (grad,)

def back_keep(v):
    return (v, None)

def back_low(kept, grad):
    return (low(grad),)
low.defvjp(low_keep, low_pass)
low_back.defvjp(back_keep, back_low)
highest = lax.Precision.HIGHEST
norm_eps = 1e-06

def matmul(left_side, right_side):
    return jnp.dot(left_side, right_side, precision=highest, preferred_element_type=jnp.float32)

def layer_norm(stream, gain_row, shift_row):
    mean_row = lax.optimization_barrier(jnp.mean(stream, axis=-1, keepdims=True))
    centred = stream - mean_row
    variance = lax.optimization_barrier(jnp.mean(centred * centred, axis=-1, keepdims=True))
    return centred * lax.rsqrt(variance + norm_eps) * gain_row + shift_row

def attention(queries, keys_part, values_part, same_seg):
    q_heads = queries.reshape(ROW, HEADS, HEAD_DIM)
    k_heads = keys_part.reshape(ROW, HEADS, HEAD_DIM)
    v_heads = values_part.reshape(ROW, HEADS, HEAD_DIM)
    scores = jnp.einsum('qhd,khd->hqk', q_heads, k_heads, precision=highest) * HEAD_DIM ** (-0.5)
    scores = low_back(scores)
    scores = jnp.where(same_seg[None], scores, -1e+30)
    row_max = lax.optimization_barrier(jnp.max(scores, axis=-1, keepdims=True))
    exponent = jnp.exp(scores - row_max)
    probs = low(exponent / lax.optimization_barrier(jnp.sum(exponent, axis=-1, keepdims=True)))
    mixed = jnp.einsum('hqk,khd->qhd', probs, v_heads, precision=highest)
    return mixed.reshape(ROW, D)

def row_forward(token_row, seg_row, valid_row, biases, weights, ln_gain):
    bias_qv, bias_out, ln_bias, bias_up, bias_down = biases
    w_qkv, w_out, w_up, w_down = weights
    same_seg = seg_row[:, None] == seg_row[None, :]
    valid_col = valid_row[:, None]
    hidden = token_row
    square_list = []
    for layer_at in range(LAYERS):
        projected = low_back(matmul(low(hidden), w_qkv[layer_at]))
        queries = low(projected[:, 0:D] + bias_qv[layer_at, 0])
        keys_part = low(projected[:, D:2 * D])
        values_part = low(projected[:, 2 * D:3 * D] + bias_qv[layer_at, 1])
        attended = low_back(low(attention(queries, keys_part, values_part, same_seg)))
        branch = low_back(matmul(attended, w_out[layer_at])) + bias_out[layer_at]
        first_out = layer_norm(hidden + branch, ln_gain[layer_at, 0], ln_bias[layer_at, 0])
        pre_act = low_back(matmul(low(first_out), w_up[layer_at])) + bias_up[layer_at]
        activated = low(jax.nn.gelu(pre_act, approximate=False))
        ffn_out = low_back(matmul(activated, w_down[layer_at])) + bias_down[layer_at]
        second = layer_norm(first_out + ffn_out, ln_gain[layer_at, 1], ln_bias[layer_at, 1])
        square_list.append(jnp.stack([jnp.sum(valid_col * hidden * hidden), jnp.sum(valid_col * branch * branch), jnp.sum(valid_col * ffn_out * ffn_out)]))
        hidden = second
    return (hidden, jnp.stack(square_list))

def reference(tokens, lengths, w_qkv, w_out, w_up, w_down, ln_gain, bias_qv, bias_out, ln_bias, bias_up, bias_down, cotangent):
    weights = (w_qkv.astype(jnp.float32), w_out.astype(jnp.float32), w_up.astype(jnp.float32), w_down.astype(jnp.float32))
    token_rows = tokens.astype(jnp.float32).reshape(NROWS, ROW, D)
    cot_rows = cotangent.astype(jnp.float32).reshape(NROWS, ROW, D)
    position = jnp.arange(ROW, dtype=jnp.int32)
    first_end = lengths[:, 0:1].astype(jnp.int32)
    second_end = first_end + lengths[:, 1:2].astype(jnp.int32)
    seg_rows = (position[None] >= first_end).astype(jnp.int32) + (position[None] >= second_end).astype(jnp.int32)
    valid_rows = (position[None] < second_end).astype(jnp.float32)

    def forward(rows_in, biases):

        def one_row(packed):
            return row_forward(packed[0], packed[1], packed[2], biases, weights, ln_gain)
        outputs, squares = lax.map(jax.checkpoint(one_row), (rows_in, seg_rows, valid_rows))
        return (outputs, lax.optimization_barrier(jnp.sum(squares, axis=0)))
    biases = (bias_qv, bias_out, ln_bias, bias_up, bias_down)
    result, pullback, square_sums = jax.vjp(forward, token_rows, biases, has_aux=True)
    grad_rows, grad_biases = pullback(cot_rows * valid_rows[..., None])
    valid_count = jnp.sum(lengths).astype(jnp.float32)
    rms_values = jnp.sqrt(square_sums / (valid_count * D))
    return (result.reshape(TOKENS, D).astype(jnp.bfloat16), grad_rows.reshape(TOKENS, D), grad_biases[0], grad_biases[1], grad_biases[2], grad_biases[3], grad_biases[4], rms_values)
```

```python
import functools
import jax
import jax.numpy as jnp
from jax import lax
from jax.experimental import pallas as pl
from jax.experimental.pallas import tpu as pltpu
from jax.sharding import PartitionSpec as P

BF = jnp.bfloat16
F32 = jnp.float32


def nt(a, b):
    return lax.dot_general(a, b, (((1,), (1,)), ((), ())), preferred_element_type=F32)


def nn(a, b):
    return lax.dot_general(a, b, (((1,), (0,)), ((), ())), preferred_element_type=F32)


def tn(a, b):
    return lax.dot_general(a, b, (((0,), (0,)), ((), ())), preferred_element_type=F32)


def fold8(t):
    return jnp.sum(t.reshape(t.shape[0] // 8, 8, t.shape[1]), axis=0)


class Ring:
    def __init__(self, buf, sem, segments):
        self.buf, self.sem, self.segments = buf, sem, segments
        self.slots, self.rows = buf.shape[0], buf.shape[1]
        self.base = 0

    def fetch(self, at):
        slot = lax.rem(at, self.slots)
        first = 0
        for ref, count in self.segments:
            if isinstance(at, int):
                if first <= at < first + count:
                    row = (at - first) * self.rows
                    pltpu.make_async_copy(ref.at[pl.ds(row, self.rows)], self.buf.at[slot], self.sem.at[slot]).start()
            else:

                @pl.when(jnp.logical_and(at >= first, at < first + count))
                def _(ref=ref, first=first):
                    row = pl.multiple_of((at - first) * self.rows, self.rows)
                    pltpu.make_async_copy(ref.at[pl.ds(row, self.rows)], self.buf.at[slot], self.sem.at[slot]).start()

            first += count

    def prime(self):
        for at in range(self.slots):
            self.fetch(at)

    def run(self, count, body):
        base = self.base

        def step(j, carry):
            at = base + j
            slot = lax.rem(at, self.slots)
            pltpu.make_async_copy(self.segments[0][0].at[pl.ds(0, self.rows)], self.buf.at[slot], self.sem.at[slot]).wait()
            body(j, self.buf[slot])
            self.fetch(at + self.slots)
            return carry

        lax.fori_loop(0, count, step, 0)
        self.base = base + count


def backward_kernel(layers, *refs):
    cot, valid, gain = refs[:3]
    kept = [refs[3 + at * layers : 3 + (at + 1) * layers] for at in range(13)]
    q, k, v, pt, slope, n1, n2, r1, r2, wqkv, wout, wup, wdown = kept
    backward_body(layers, cot, valid, gain, q, k, v, pt, slope, n1, n2, r1, r2, wqkv, wout, wup, wdown, *refs[3 + 13 * layers :])


def backward_body(
    layers, cot, valid, gain, q, k, v, pt, slope, n1, n2, r1, r2, wqkv, wout, wup, wdown,
    dh_out, grads,
    e_buf, x_buf, z_buf, du_buf, dp_buf, do_buf, cot_buf,
    q_buf, k_buf, v_buf, pt_buf, sl_buf, n1_buf, n2_buf,
    ring_a, ring_b, ring_c, sem_a, sem_b, sem_c, sem_in, sem_out,
):
    slots, width = e_buf.shape
    ff = du_buf.shape[1]
    heads = pt[0].shape[0]
    hd = width // heads
    half = slots // 2
    scale = hd ** (-0.5)
    order = list(reversed(range(layers)))

    sources = (n2, slope, n1, q, k, v, pt)
    buffers = (n2_buf, sl_buf, n1_buf, q_buf, k_buf, v_buf, pt_buf)

    def load(which, layer, par):
        return pltpu.make_async_copy(sources[which][layer], buffers[which].at[par], sem_in.at[par, which])

    cot_copy = pltpu.make_async_copy(cot, cot_buf, sem_out.at[0])
    cot_copy.start()
    load(0, order[0], 0).start()
    seg_a = []
    seg_b = []
    seg_c = []
    for l in order:
        seg_a += [(wdown[l], ff // ring_a.shape[1]), (wout[l], width // ring_a.shape[1])]
        seg_b += [(wup[l], width // ring_b.shape[1])]
        seg_c += [(wqkv[l], width // ring_c.shape[1])]
    ra, rb, rc = Ring(ring_a, sem_a, seg_a), Ring(ring_b, sem_b, seg_b), Ring(ring_c, sem_c, seg_c)
    ra.prime()
    load(1, order[0], 0).start()
    rb.prime()
    for which in range(2, 7):
        load(which, order[0], 0).start()
    rc.prime()
    for which in range(7):
        for step, l in enumerate(order[1:], 1):
            if step < 2:
                load(which, l, step).start()

    chunk = 32
    cot_copy.wait()

    def mask_cot(c, carry):
        rows = pl.ds(pl.multiple_of(c * chunk, chunk), chunk)
        e_buf[rows, :] = cot_buf[rows, :].astype(F32) * valid[rows, :]
        return carry

    lax.fori_loop(0, slots // chunk, mask_cot, 0)

    def norm_back(src, dst, gain_row, n_ref, r_ref):
        def step(c, carry):
            s_in, s_out = carry
            rows = pl.ds(pl.multiple_of(c * chunk, chunk), chunk)
            g = src[rows, :]
            n = n_ref[rows, :].astype(F32)
            ge = g * gain_row
            m1 = jnp.mean(ge, axis=1, keepdims=True)
            m2 = jnp.mean(ge * n, axis=1, keepdims=True)
            dz = r_ref[rows, :] * (ge - m1 - n * m2)
            dst[rows, :] = dz
            z_buf[rows, :] = dz.astype(BF)
            return (s_in + fold8(g), s_out + fold8(dz))

        zero = jnp.zeros((8, width), F32)
        s_in, s_out = lax.fori_loop(0, slots // chunk, step, (zero, zero))
        return jnp.sum(s_in, axis=0, keepdims=True), jnp.sum(s_out, axis=0, keepdims=True)

    for step, l in enumerate(order):
        par = step % 2

        load(0, l, par).wait()
        s_in, s_out = norm_back(e_buf, x_buf, gain[l, 1:2, :], n2_buf.at[par], r2[l])
        grads[l, 4:5, :] = s_in
        grads[l, 9:10, :] = s_out

        load(1, l, par).wait()
        wide = ring_a.shape[1]

        def down_body(j, w):
            cols = pl.ds(pl.multiple_of(j * wide, wide), wide)
            du = nt(z_buf[...], w) * sl_buf[par, :, cols].astype(F32)
            du_buf[:, cols] = du.astype(BF)
            part = jnp.sum(fold8(du), axis=0, keepdims=True)
            per = width // wide
            grads[l, pl.ds(5 + j // per, 1), pl.ds(pl.multiple_of(lax.rem(j, per) * wide, wide), wide)] = part

        ra.run(ff // wide, down_body)
        nb = ring_b.shape[1]

        def up_body(j, w):
            cols = pl.ds(pl.multiple_of(j * nb, nb), nb)
            x_buf[:, cols] = x_buf[:, cols] + nt(du_buf[...], w)

        rb.run(width // nb, up_body)

        load(2, l, par).wait()
        s_in, s_out = norm_back(x_buf, x_buf, gain[l, 0:1, :], n1_buf.at[par], r1[l])
        grads[l, 3:4, :] = s_in
        grads[l, 2:3, :] = s_out

        def out_body(j, w):
            cols = pl.ds(pl.multiple_of(j * wide, wide), wide)
            do_buf[:, cols] = nt(z_buf[...], w).astype(BF)

        ra.run(width // wide, out_body)

        for which in range(3, 7):
            load(which, l, par).wait()
        lane = lax.broadcasted_iota(jnp.int32, (1, 2 * hd), 1)
        sides = (lane < hd, lane >= hd)

        def pair(hp, carry):
            cols = pl.ds(pl.multiple_of(hp * 2 * hd, 2 * hd), 2 * hd)
            sum_q = jnp.zeros((8, 2 * hd), F32)
            sum_v = jnp.zeros((8, 2 * hd), F32)
            for b in range(2):
                rows = pl.ds(b * half, half)
                q2, k2, v2, do2 = (r[rows, cols] for r in (q_buf.at[par], k_buf.at[par], v_buf.at[par], do_buf))
                dq = dk = dv = None
                for side in range(2):
                    keep = sides[side]
                    zero = jnp.zeros_like(q2)
                    pb = pt_buf[par, 2 * hp + side, b]
                    dpt = nt(jnp.where(keep, v2, zero), do2)
                    p32 = pb.astype(F32)
                    t = p32 * dpt
                    inner = jnp.sum(fold8(t), axis=0, keepdims=True)
                    ds = (t - p32 * inner).astype(BF)
                    a_v = nn(pb, jnp.where(keep, do2, zero))
                    a_k = nn(ds, jnp.where(keep, q2, zero))
                    a_q = tn(ds, jnp.where(keep, k2, zero))
                    dv = a_v if dv is None else dv + a_v
                    dk = a_k if dk is None else dk + a_k
                    dq = a_q if dq is None else dq + a_q
                dq = dq * scale
                dk = dk * scale
                dp_buf[rows, cols] = dq.astype(BF)
                dp_buf[rows, pl.ds(pl.multiple_of(width + hp * 2 * hd, 2 * hd), 2 * hd)] = dk.astype(BF)
                dp_buf[rows, pl.ds(pl.multiple_of(2 * width + hp * 2 * hd, 2 * hd), 2 * hd)] = dv.astype(BF)
                sum_q = sum_q + fold8(dq)
                sum_v = sum_v + fold8(dv)
            grads[l, 0:1, cols] = jnp.sum(sum_q, axis=0, keepdims=True)
            grads[l, 1:2, cols] = jnp.sum(sum_v, axis=0, keepdims=True)
            return carry

        lax.fori_loop(0, heads // 2, pair, 0)
        nc = ring_c.shape[1]
        last = step == layers - 1

        def qkv_body(j, w):
            cols = pl.ds(pl.multiple_of(j * nc, nc), nc)
            e_buf[:, cols] = x_buf[:, cols] + nt(dp_buf[...], w)
            if last:
                pltpu.make_async_copy(e_buf.at[:, cols], dh_out.at[:, cols], sem_out.at[0]).start()

        rc.run(width // nc, qkv_body)
        for which in range(7):
            if step + 2 < layers:
                load(which, order[step + 2], par).start()
        grads[l, 10:16, :] = jnp.zeros((6, width), F32)

    for j in range(width // nc):
        cols = pl.ds(j * nc, nc)
        pltpu.make_async_copy(e_buf.at[:, cols], dh_out.at[:, cols], sem_out.at[0]).wait()


def backward(cot, valid, gain, kept):
    slots, width = cot.shape
    layers = len(kept[0])
    ff = kept[4][0].shape[1]
    heads = kept[3][0].shape[0]
    half = slots // 2
    hbm = pl.BlockSpec(memory_space=pl.ANY)
    vm = pl.BlockSpec(memory_space=pltpu.VMEM)
    ta, tb, tc = min(512, width), min(256, width), min(256, width)
    return pl.pallas_call(
        functools.partial(backward_kernel, layers),
        out_shape=(
            jax.ShapeDtypeStruct((slots, width), F32),
            jax.ShapeDtypeStruct((layers, 16, width), F32),
        ),
        in_specs=[hbm, vm, vm] + [hbm] * (7 * layers) + [vm] * (2 * layers) + [hbm] * (4 * layers),
        out_specs=(hbm, vm),
        scratch_shapes=[
            pltpu.VMEM((slots, width), F32),
            pltpu.VMEM((slots, width), F32),
            pltpu.VMEM((slots, width), BF),
            pltpu.VMEM((slots, ff), BF),
            pltpu.VMEM((slots, 3 * width), BF),
            pltpu.VMEM((slots, width), BF),
            pltpu.VMEM((slots, width), BF),
        ]
        + [pltpu.VMEM((2, slots, width), BF)] * 3
        + [
            pltpu.VMEM((2, heads, 2, half, half), BF),
            pltpu.VMEM((2, slots, ff), BF),
            pltpu.VMEM((2, slots, width), BF),
            pltpu.VMEM((2, slots, width), BF),
            pltpu.VMEM((3, ta, width), BF),
            pltpu.VMEM((2, tb, ff), BF),
            pltpu.VMEM((2, tc, 3 * width), BF),
            pltpu.SemaphoreType.DMA((3,)),
            pltpu.SemaphoreType.DMA((2,)),
            pltpu.SemaphoreType.DMA((2,)),
            pltpu.SemaphoreType.DMA((2, 7)),
            pltpu.SemaphoreType.DMA((1,)),
        ],
        compiler_params=pltpu.CompilerParams(vmem_limit_bytes=67000000),
        name="backward",
    )(cot, valid, gain, *[a for one in kept for a in one])


HEADS = 16
AXES = ("dp", "shard")


def normalize(stream, gain_row, shift_row):
    mean_row = jnp.mean(stream, axis=-1, keepdims=True)
    centred = stream - mean_row
    variance = jnp.mean(centred * centred, axis=-1, keepdims=True)
    inv_std = lax.rsqrt(variance + 1e-06)
    normed = centred * inv_std
    return normed * gain_row + shift_row, normed, inv_std


def local(
    tokens, lengths, w_qkv, w_out, w_up, w_down, ln_gain, bias_qv, bias_out, ln_bias, bias_up, bias_down, cotangent
):
    slots, width = tokens.shape
    layers = w_qkv.shape[0]
    half = slots // 2
    hd = width // HEADS
    first, second = lengths[0, 0], lengths[0, 1]
    shift = jnp.where(first == half, 0, first)
    place = lax.rem(jnp.arange(slots, dtype=jnp.int32) + shift, slots)
    valid = place < first + second
    same = valid.reshape(2, half)[:, :, None] == valid.reshape(2, half)[:, None, :]
    valid = valid.astype(F32)[:, None]

    def turn(a, by):
        return lax.dynamic_slice_in_dim(jnp.concatenate([a, a], axis=0), by, slots, axis=0)

    stream = turn(tokens, shift).astype(F32)
    cot = turn(cotangent, shift)
    full = [[lax.all_gather(w[l], AXES, axis=0, tiled=True) for w in (w_qkv, w_out, w_up, w_down)] for l in range(layers)]
    kept = []
    squares = []
    for l in range(layers):
        mat_qkv, mat_out, mat_up, mat_down = full[l]
        projected = nn(stream.astype(BF), mat_qkv)
        q = (projected[:, :width] + bias_qv[l, 0]).astype(BF)
        k = projected[:, width : 2 * width].astype(BF)
        v = (projected[:, 2 * width :] + bias_qv[l, 1]).astype(BF)
        q4, k4, v4 = (a.reshape(2, half, HEADS, hd) for a in (q, k, v))
        st = jnp.einsum("bqhd,bkhd->hbkq", q4, k4, preferred_element_type=F32) * hd ** (-0.5)
        st = jnp.where(same[None], st, -1e30)
        ex = jnp.exp(st - jnp.max(st, axis=2, keepdims=True))
        pt = (ex / jnp.sum(ex, axis=2, keepdims=True)).astype(BF)
        mixed = jnp.einsum("hbkq,bkhd->bqhd", pt, v4, preferred_element_type=F32).reshape(slots, width).astype(BF)
        branch = nn(mixed, mat_out) + bias_out[l]
        x1, n1, r1 = normalize(stream + branch, ln_gain[l, 0], ln_bias[l, 0])
        u = nn(x1.astype(BF), mat_up) + bias_up[l]
        phi = 0.5 * (1.0 + lax.erf(u * 0.7071067811865476))
        slope = (phi + u * (jnp.exp(-0.5 * u * u) * 0.3989422804014327)).astype(BF)
        ffn = nn((u * phi).astype(BF), mat_down) + bias_down[l]
        nxt, n2, r2 = normalize(x1 + ffn, ln_gain[l, 1], ln_bias[l, 1])
        squares.append(jnp.stack([jnp.sum(valid * a * a) for a in (stream, branch, ffn)]))
        kept.append((q, k, v, pt, slope, n1.astype(BF), n2.astype(BF), r1, r2))
        stream = nxt
    dh, grads = backward(cot, valid, ln_gain, list(zip(*kept)) + list(zip(*full)))
    count = jnp.sum(lengths).astype(F32)
    grads, squares, count = lax.psum((grads[:, :10], jnp.stack(squares), count), AXES)
    back = lax.rem(slots - shift, slots)
    return (
        turn(stream.astype(BF), back),
        turn(dh, back),
        grads[:, 0:2],
        grads[:, 2],
        grads[:, 3:5],
        grads[:, 5:9].reshape(layers, -1),
        grads[:, 9],
        jnp.sqrt(squares / (count * width)),
    )


def solution(mesh):
    rows = P(AXES, None)
    weight = P(None, AXES, None)
    in_specs = (rows, rows, weight, weight, weight, weight, P(), P(), P(), P(), P(), P(), rows)
    return jax.shard_map(
        local, mesh=mesh, in_specs=in_specs, out_specs=(rows, rows, P(), P(), P(), P(), P(), P()), check_vma=False
    )
```

```python
import functools
import math

import jax
import jax.numpy as jnp
from jax import lax
from jax.experimental import pallas as pl
from jax.experimental.pallas import tpu as pltpu
from jax.sharding import PartitionSpec as P

BF = jnp.bfloat16
F32 = jnp.float32
HEADS = 16
AXES = ("dp", "shard")


def nt(a, b):
    return lax.dot_general(a, b, (((1,), (1,)), ((), ())), preferred_element_type=F32)


def nn(a, b):
    return lax.dot_general(a, b, (((1,), (0,)), ((), ())), preferred_element_type=F32)


def tn(a, b):
    return lax.dot_general(a, b, (((0,), (0,)), ((), ())), preferred_element_type=F32)


def fold8(t):
    return jnp.sum(t.reshape(t.shape[0] // 8, 8, t.shape[1]), axis=0)


class Ring:
    def __init__(self, buf, sem, segments):
        self.buf, self.sem, self.segments = buf, sem, segments
        self.slots, self.rows = buf.shape[0], buf.shape[1]
        self.base = 0

    def fetch(self, at):
        slot = lax.rem(at, self.slots)
        first = 0
        for ref, count in self.segments:
            if isinstance(at, int):
                if first <= at < first + count:
                    row = (at - first) * self.rows
                    pltpu.make_async_copy(ref.at[pl.ds(row, self.rows)], self.buf.at[slot], self.sem.at[slot]).start()
            else:

                @pl.when(jnp.logical_and(at >= first, at < first + count))
                def _(ref=ref, first=first):
                    row = pl.multiple_of((at - first) * self.rows, self.rows)
                    pltpu.make_async_copy(ref.at[pl.ds(row, self.rows)], self.buf.at[slot], self.sem.at[slot]).start()

            first += count

    def prime(self):
        for at in range(self.slots):
            self.fetch(at)

    def run(self, count, body):
        base = self.base

        def step(j, carry):
            at = base + j
            slot = lax.rem(at, self.slots)
            pltpu.make_async_copy(self.segments[0][0].at[pl.ds(0, self.rows)], self.buf.at[slot], self.sem.at[slot]).wait()
            body(j, self.buf[slot])
            self.fetch(at + self.slots)
            return carry

        lax.fori_loop(0, count, step, 0)
        self.base = base + count


def backward_kernel(layers, *refs):
    cot, valid, gain, squares = refs[:4]
    kept = [refs[4 + at * layers : 4 + (at + 1) * layers] for at in range(13)]
    q, k, v, pt, slope, n1, n2, r1, r2, wqkv, wout, wup, wdown = kept
    backward_body(layers, cot, valid, gain, squares, q, k, v, pt, slope, n1, n2, r1, r2, wqkv, wout, wup, wdown, *refs[4 + 13 * layers :])


def backward_body(
    layers, cot, valid, gain, squares, q, k, v, pt, slope, n1, n2, r1, r2, wqkv, wout, wup, wdown,
    dh_out, grads,
    e_buf, x_buf, z_buf, du_buf, dp_buf, do_buf, cot_buf,
    q_buf, k_buf, v_buf, pt_buf, sl_buf, n1_buf, n2_buf,
    ring_a, ring_b, ring_c, sem_a, sem_b, sem_c, sem_in, sem_out,
):
    slots, width = e_buf.shape
    ff = du_buf.shape[1]
    heads = pt[0].shape[0]
    hd = width // heads
    half = slots // 2
    scale = hd ** (-0.5)
    order = list(reversed(range(layers)))

    sources = (n2, slope, n1, q, k, v, pt)
    buffers = (n2_buf, sl_buf, n1_buf, q_buf, k_buf, v_buf, pt_buf)

    def load(which, layer, par):
        return pltpu.make_async_copy(sources[which][layer], buffers[which].at[par], sem_in.at[par, which])

    cot_copy = pltpu.make_async_copy(cot, cot_buf, sem_out.at[0])
    cot_copy.start()
    load(0, order[0], 0).start()
    seg_a = []
    seg_b = []
    seg_c = []
    for l in order:
        seg_a += [(wdown[l], ff // ring_a.shape[1]), (wout[l], width // ring_a.shape[1])]
        seg_b += [(wup[l], width // ring_b.shape[1])]
        seg_c += [(wqkv[l], width // ring_c.shape[1])]
    ra, rb, rc = Ring(ring_a, sem_a, seg_a), Ring(ring_b, sem_b, seg_b), Ring(ring_c, sem_c, seg_c)
    ra.prime()
    load(1, order[0], 0).start()
    rb.prime()
    for which in range(2, 7):
        load(which, order[0], 0).start()
    rc.prime()
    for which in range(7):
        for step, l in enumerate(order[1:], 1):
            if step < 2:
                load(which, l, step).start()

    chunk = 32
    cot_copy.wait()

    def mask_cot(c, carry):
        rows = pl.ds(pl.multiple_of(c * chunk, chunk), chunk)
        e_buf[rows, :] = cot_buf[rows, :].astype(F32) * valid[rows, :]
        return carry

    lax.fori_loop(0, slots // chunk, mask_cot, 0)

    def norm_back(src, dst, gain_row, n_ref, r_ref):
        def step(c, carry):
            s_in, s_out = carry
            rows = pl.ds(pl.multiple_of(c * chunk, chunk), chunk)
            g = src[rows, :]
            n = n_ref[rows, :].astype(F32)
            ge = g * gain_row
            m1 = jnp.mean(ge, axis=1, keepdims=True)
            m2 = jnp.mean(ge * n, axis=1, keepdims=True)
            dz = r_ref[rows, :] * (ge - m1 - n * m2)
            dst[rows, :] = dz
            z_buf[rows, :] = dz.astype(BF)
            return (s_in + fold8(g), s_out + fold8(dz))

        zero = jnp.zeros((8, width), F32)
        s_in, s_out = lax.fori_loop(0, slots // chunk, step, (zero, zero))
        return jnp.sum(s_in, axis=0, keepdims=True), jnp.sum(s_out, axis=0, keepdims=True)

    for step, l in enumerate(order):
        par = step % 2

        load(0, l, par).wait()
        s_in, s_out = norm_back(e_buf, x_buf, gain[l, 1:2, :], n2_buf.at[par], r2[l])
        grads[l, 4:5, :] = s_in
        grads[l, 9:10, :] = s_out

        load(1, l, par).wait()
        wide = ring_a.shape[1]

        def down_body(j, w):
            cols = pl.ds(pl.multiple_of(j * wide, wide), wide)
            du = nt(z_buf[...], w) * sl_buf[par, :, cols].astype(F32)
            du_buf[:, cols] = du.astype(BF)
            part = jnp.sum(fold8(du), axis=0, keepdims=True)
            per = width // wide
            grads[l, pl.ds(5 + j // per, 1), pl.ds(pl.multiple_of(lax.rem(j, per) * wide, wide), wide)] = part

        ra.run(ff // wide, down_body)
        nb = ring_b.shape[1]

        def up_body(j, w):
            cols = pl.ds(pl.multiple_of(j * nb, nb), nb)
            x_buf[:, cols] = x_buf[:, cols] + nt(du_buf[...], w)

        rb.run(width // nb, up_body)

        load(2, l, par).wait()
        s_in, s_out = norm_back(x_buf, x_buf, gain[l, 0:1, :], n1_buf.at[par], r1[l])
        grads[l, 3:4, :] = s_in
        grads[l, 2:3, :] = s_out

        def out_body(j, w):
            cols = pl.ds(pl.multiple_of(j * wide, wide), wide)
            do_buf[:, cols] = nt(z_buf[...], w).astype(BF)

        ra.run(width // wide, out_body)

        for which in range(3, 7):
            load(which, l, par).wait()
        lane = lax.broadcasted_iota(jnp.int32, (1, 2 * hd), 1)
        sides = (lane < hd, lane >= hd)

        def pair(hp, carry):
            cols = pl.ds(pl.multiple_of(hp * 2 * hd, 2 * hd), 2 * hd)
            sum_q = jnp.zeros((8, 2 * hd), F32)
            sum_v = jnp.zeros((8, 2 * hd), F32)
            for b in range(2):
                rows = pl.ds(b * half, half)
                q2, k2, v2, do2 = (r[rows, cols] for r in (q_buf.at[par], k_buf.at[par], v_buf.at[par], do_buf))
                dq = dk = dv = None
                for side in range(2):
                    keep = sides[side]
                    zero = jnp.zeros_like(q2)
                    pb = pt_buf[par, 2 * hp + side, b]
                    dpt = nt(jnp.where(keep, v2, zero), do2)
                    p32 = pb.astype(F32)
                    t = p32 * dpt
                    inner = jnp.sum(fold8(t), axis=0, keepdims=True)
                    ds = (t - p32 * inner).astype(BF)
                    a_v = nn(pb, jnp.where(keep, do2, zero))
                    a_k = nn(ds, jnp.where(keep, q2, zero))
                    a_q = tn(ds, jnp.where(keep, k2, zero))
                    dv = a_v if dv is None else dv + a_v
                    dk = a_k if dk is None else dk + a_k
                    dq = a_q if dq is None else dq + a_q
                dq = dq * scale
                dk = dk * scale
                dp_buf[rows, cols] = dq.astype(BF)
                dp_buf[rows, pl.ds(pl.multiple_of(width + hp * 2 * hd, 2 * hd), 2 * hd)] = dk.astype(BF)
                dp_buf[rows, pl.ds(pl.multiple_of(2 * width + hp * 2 * hd, 2 * hd), 2 * hd)] = dv.astype(BF)
                sum_q = sum_q + fold8(dq)
                sum_v = sum_v + fold8(dv)
            grads[l, 0:1, cols] = jnp.sum(sum_q, axis=0, keepdims=True)
            grads[l, 1:2, cols] = jnp.sum(sum_v, axis=0, keepdims=True)
            return carry

        lax.fori_loop(0, heads // 2, pair, 0)
        nc = ring_c.shape[1]
        last = step == layers - 1

        def qkv_body(j, w):
            cols = pl.ds(pl.multiple_of(j * nc, nc), nc)
            e_buf[:, cols] = x_buf[:, cols] + nt(dp_buf[...], w)
            if last:
                pltpu.make_async_copy(e_buf.at[:, cols], dh_out.at[:, cols], sem_out.at[0]).start()

        rc.run(width // nc, qkv_body)
        for which in range(7):
            if step + 2 < layers:
                load(which, order[step + 2], par).start()
        grads[l, 10:13, :] = squares[3 * l : 3 * l + 3, :]
        grads[l, 13:14, :] = squares[3 * layers : 3 * layers + 1, :]
        grads[l, 14:16, :] = jnp.zeros((2, width), F32)

    for j in range(width // nc):
        cols = pl.ds(j * nc, nc)
        pltpu.make_async_copy(e_buf.at[:, cols], dh_out.at[:, cols], sem_out.at[0]).wait()


def backward(cot, valid, gain, squares, kept):
    slots, width = cot.shape
    layers = len(kept[0])
    ff = kept[4][0].shape[1]
    heads = kept[3][0].shape[0]
    half = slots // 2
    hbm = pl.BlockSpec(memory_space=pl.ANY)
    vm = pl.BlockSpec(memory_space=pltpu.VMEM)
    ta, tb, tc = min(512, width), min(256, width), min(256, width)
    return pl.pallas_call(
        functools.partial(backward_kernel, layers),
        out_shape=(
            jax.ShapeDtypeStruct((slots, width), F32),
            jax.ShapeDtypeStruct((layers, 16, width), F32),
        ),
        in_specs=[hbm, vm, vm, vm] + [hbm] * (7 * layers) + [vm] * (2 * layers) + [hbm] * (4 * layers),
        out_specs=(hbm, vm),
        scratch_shapes=[
            pltpu.VMEM((slots, width), F32),
            pltpu.VMEM((slots, width), F32),
            pltpu.VMEM((slots, width), BF),
            pltpu.VMEM((slots, ff), BF),
            pltpu.VMEM((slots, 3 * width), BF),
            pltpu.VMEM((slots, width), BF),
            pltpu.VMEM((slots, width), BF),
        ]
        + [pltpu.VMEM((2, slots, width), BF)] * 3
        + [
            pltpu.VMEM((2, heads, 2, half, half), BF),
            pltpu.VMEM((2, slots, ff), BF),
            pltpu.VMEM((2, slots, width), BF),
            pltpu.VMEM((2, slots, width), BF),
            pltpu.VMEM((3, ta, width), BF),
            pltpu.VMEM((2, tb, ff), BF),
            pltpu.VMEM((2, tc, 3 * width), BF),
            pltpu.SemaphoreType.DMA((3,)),
            pltpu.SemaphoreType.DMA((2,)),
            pltpu.SemaphoreType.DMA((2,)),
            pltpu.SemaphoreType.DMA((2, 7)),
            pltpu.SemaphoreType.DMA((1,)),
        ],
        compiler_params=pltpu.CompilerParams(vmem_limit_bytes=67000000),
        name="backward",
    )(cot, valid, gain, squares, *[a for one in kept for a in one])


class Fabric:
    def __init__(self, sizes):
        ny, nx, nz = sizes
        dp = lax.axis_index("dp")
        self.size = {"y": ny, "x": nx, "z": nz, "c": 2}
        self.at = {"z": lax.axis_index("shard"), "c": lax.rem(dp, 2), "x": lax.rem(dp // 2, nx), "y": dp // (2 * nx)}

    def device(self, **moved):
        at = {**self.at, **moved}
        return ((at["y"] * self.size["x"] + at["x"]) * 2 + at["c"], at["z"])

    def peers(self, axis):
        n = self.size[axis]
        return [lax.rem(self.at[axis] + step, n) for step in range(1, n)]

    def block(self, **moved):
        at = {**self.at, **moved}
        return ((at["y"] * self.size["x"] + at["x"]) * 2 + at["c"]) * self.size["z"] + at["z"]

    def spans(self, free, **fixed):
        outer = [()]
        for axis in free:
            if axis != "z":
                outer = [old + ((axis, at),) for old in outer for at in range(self.size[axis])]
        runs = []
        for pick in outer:
            where = {**fixed, **dict(pick)}
            if "z" in free:
                runs.append((self.block(**{**where, "z": 0}), self.size["z"]))
            else:
                runs.append((self.block(**where), 1))
        return runs


class Piece:
    def __init__(self, fabric, own, full, cols, order, sems):
        self.fabric, self.own, self.full, self.cols, self.order = fabric, own, full, cols, order
        self.send, self.recv = sems
        self.rows = own.shape[0]
        self.sent = {}

    def view(self, first, blocks):
        start = pl.multiple_of(first * self.rows, self.rows)
        return self.full.at[pl.ds(start, blocks * self.rows), self.cols]

    def push(self, stage, device, spans, own=False):
        for first, blocks in spans:
            dst = self.view(first, blocks)
            src = self.own.at[:, self.cols] if own else dst
            pltpu.make_async_remote_copy(
                src_ref=src,
                dst_ref=dst,
                send_sem=self.send.at[stage],
                recv_sem=self.recv.at[stage],
                device_id=device,
                device_id_type=pl.DeviceIdType.MESH,
            ).start()
            self.sent[stage] = self.sent.get(stage, 0) + blocks

    def await_blocks(self, sem, blocks):
        part = self.full.at[pl.ds(0, blocks * self.rows), self.cols]
        pltpu.make_async_copy(part, part, sem).wait()

    def start(self, stage):
        fab = self.fabric
        partner = fab.device(c=1 - fab.at["c"])
        free = self.order[:stage]
        if stage == 0:
            self.push(3, partner, [(fab.block(), 1)], own=True)
        else:
            self.took(stage - 1)
        if stage < 3:
            axis = self.order[stage]
            spans = [(fab.block(), 1)] if stage == 0 else fab.spans(free)
            for peer in fab.peers(axis):
                self.push(stage, fab.device(**{axis: peer}), spans, own=stage == 0)

    def took(self, stage):
        fab = self.fabric
        partner = fab.device(c=1 - fab.at["c"])
        axis, free = self.order[stage], self.order[:stage]
        held = 1
        for name in free:
            held *= fab.size[name]
        self.await_blocks(self.recv.at[stage], held * (fab.size[axis] - 1))
        for peer in fab.peers(axis):
            self.push(3, partner, fab.spans(free, **{axis: peer}))

    def finish(self):
        fab = self.fabric
        self.await_blocks(self.recv.at[3], fab.size["x"] * fab.size["y"] * fab.size["z"])

    def drain(self):
        for stage, blocks in self.sent.items():
            self.await_blocks(self.send.at[stage], blocks)


ORDERS = ("zxy", "zyx", "xzy", "yzx")


def shares(width):
    unit = 128
    n = width // unit
    if n >= 8:
        side = n // 8
        return [(n // 2 - side) * unit, (n // 2 - side) * unit, side * unit, side * unit]
    if n >= 4:
        return [n // 4 * unit] * 4
    return [width // 2, width // 2, 0, 0]


def forward_kernel(layers, sizes, *refs):
    (tok, vcol, vrow, gain, b_qv, b_out, b_ln, b_up, b_down, s_qkv, s_out, s_up, s_down) = refs[:13]
    act, squares = refs[13:15]
    outs = [refs[15 + at * layers : 15 + (at + 1) * layers] for at in range(13)]
    q_o, k_o, v_o, pt_o, sl_o, n1_o, n2_o, r1_o, r2_o, f_qkv, f_out, f_up, f_down = outs
    (
        h_buf, hb_buf, q_buf, k_buf, v_buf, mix_buf, gu_buf, f_buf, pt_buf, sl_buf, n_buf,
        ring_w, ring_t, own_qkv, own_out, own_up, own_down,
        sem_send, sem_recv, sem_own, sem_ring, sem_save,
    ) = refs[15 + 13 * layers :]
    slots, width = tok.shape
    ff = gu_buf.shape[1]
    heads = pt_buf.shape[0]
    hd = width // heads
    half = slots // 2
    scale = hd ** (-0.5)
    tall = ring_t.shape[2]
    fab = Fabric(sizes)

    shards = ((s_qkv, own_qkv, f_qkv), (s_out, own_out, f_out), (s_up, own_up, f_up), (s_down, own_down, f_down))
    for at, (src, buf, _) in enumerate(shards):
        pltpu.make_async_copy(src, buf, sem_own.at[at]).start()
    barrier = pltpu.get_barrier_semaphore()
    around = [fab.device(**{axis: peer}) for axis in ("z", "x", "y", "c") for peer in fab.peers(axis)]
    for device in around:
        pl.semaphore_signal(barrier, inc=1, device_id=device, device_id_type=pl.DeviceIdType.MESH)
    pl.semaphore_wait(barrier, len(around))

    chunks = []
    pieces_made = 0

    def add(kind, l, at, shard, full, first, count):
        nonlocal pieces_made
        pieces = []
        col = first
        for order, cols in zip(ORDERS, shares(count)):
            if cols:
                sems = (sem_send.at[pieces_made], sem_recv.at[pieces_made])
                pieces.append(Piece(fab, shard.at[l], full, pl.ds(col, cols), order, sems))
                pieces_made += 1
                col += cols
        chunks.append((kind, l, at, full.at[:, pl.ds(first, count)], pieces))

    for l in range(layers):
        for at in range(3):
            add("qkv", l, at, s_qkv, f_qkv[l], at * width, width)
        add("out", l, 0, s_out, f_out[l], 0, width)
        for at in range(ff // width):
            add("up", l, at, s_up, f_up[l], at * width, width)
        for at in range(width // tall):
            add("down", l, at, s_down, f_down[l], at * tall, tall)
    total = len(chunks)

    saves = []
    busy = {}

    def save(src, dst, key):
        at = len(saves)
        copy = pltpu.make_async_copy(src, dst, sem_save.at[at])
        copy.start()
        saves.append(copy)
        busy[key] = at

    waited = set()

    def free(key):
        at = busy.get(key)
        if at is not None and at not in waited:
            saves[at].wait()
            waited.add(at)

    chunk = 32
    steps = slots // chunk
    valid = lambda rows: vcol[rows, :]

    def rows_of(c):
        return pl.ds(pl.multiple_of(c * chunk, chunk), chunk)

    def tiles(w, lhs, count, body, tile=256):
        def step(j, carry):
            cols = pl.ds(pl.multiple_of(j * tile, tile), tile)
            body(cols, nn(lhs[...], w[:, cols]), j * tile)
            return carry

        lax.fori_loop(0, count // tile, step, 0)

    def norm(l, which, bias_row, base, branch, n_dst, r_dst):
        zero = jnp.zeros((8, width), F32)

        def step(c, carry):
            s_h, s_a = carry
            rows = rows_of(c)
            a = branch[rows, :] + bias_row
            h = base[rows, :]
            z = h + a
            mean = jnp.mean(z, axis=1, keepdims=True)
            centred = z - mean
            var = jnp.mean(centred * centred, axis=1, keepdims=True)
            inv = lax.rsqrt(var + 1e-06)
            n = centred * inv
            y = n * gain[l, which : which + 1, :] + b_ln[l, which : which + 1, :]
            base[rows, :] = y
            hb_buf[rows, :] = y.astype(BF)
            n_dst[rows, :] = n.astype(BF)
            r_dst[rows, :] = inv
            ok = valid(rows)
            return s_h + fold8(ok * h * h), s_a + fold8(ok * a * a)

        return lax.fori_loop(0, steps, step, (zero, zero))

    def attention(l):
        lane = lax.broadcasted_iota(jnp.int32, (1, 2 * hd), 1)
        sides = (lane < hd, lane >= hd)

        def pair(hp, carry):
            cols = pl.ds(pl.multiple_of(hp * 2 * hd, 2 * hd), 2 * hd)
            for b in range(2):
                rows = pl.ds(b * half, half)
                q2, k2, v2 = q_buf[rows, cols], k_buf[rows, cols], v_buf[rows, cols]
                mixed = None
                for side in range(2):
                    keep = sides[side]
                    zero = jnp.zeros_like(q2)
                    st = nt(jnp.where(keep, k2, zero), q2) * scale
                    if b == 1:
                        st = jnp.where(vcol[rows, :] == vrow[:, rows], st, -1e30)
                    top = jnp.max(st, axis=0, keepdims=True)
                    ex = jnp.exp(st - top)
                    p = (ex * (1.0 / jnp.sum(ex, axis=0, keepdims=True))).astype(BF)
                    pt_buf[2 * hp + side, b] = p
                    o = tn(p, jnp.where(keep, v2, zero))
                    mixed = o if mixed is None else mixed + o
                mix_buf[rows, cols] = mixed.astype(BF)
            return carry

        lax.fori_loop(0, heads // 2, pair, 0)

    def compute(at):
        kind, l, part, _, _ = chunks[at]
        slot = at % 2
        if kind == "qkv":
            buf, dst = ((q_buf, q_o), (k_buf, k_o), (v_buf, v_o))[part]
            free(("qkv", part))

            def body(cols, t, first):
                if part != 1:
                    t = t + b_qv[l, part // 2 : part // 2 + 1, cols]
                buf[:, cols] = t.astype(BF)

            tiles(ring_w.at[slot], hb_buf, width, body)
            save(buf, dst[l], ("qkv", part))
            if part == 2:
                free("pt")
                attention(l)
                save(pt_buf, pt_o[l], "pt")
        elif kind == "out":

            def body(cols, t, first):
                f_buf[:, cols] = t

            tiles(ring_w.at[slot], mix_buf, width, body)
            free(("n", 0))
            s_h, s_a = norm(l, 0, b_out[l : l + 1, :], h_buf, f_buf, n_buf.at[0], r1_o[l])
            squares[3 * l : 3 * l + 1, :] = jnp.sum(s_h, axis=0, keepdims=True)
            squares[3 * l + 1 : 3 * l + 2, :] = jnp.sum(s_a, axis=0, keepdims=True)
            save(n_buf.at[0], n1_o[l], ("n", 0))
        elif kind == "up":
            par = part % 2
            free(("sl", par))

            def body(cols, t, first):
                wide = pl.ds(pl.multiple_of(part * width + first, 256), 256)
                u = t + b_up[l : l + 1, wide]
                phi = 0.5 * (1.0 + lax.erf(u * 0.7071067811865476))
                sl_buf[par, :, cols] = (phi + u * (jnp.exp(-0.5 * u * u) * 0.3989422804014327)).astype(BF)
                gu_buf[:, wide] = (u * phi).astype(BF)

            tiles(ring_w.at[slot], hb_buf, width, body)
            save(sl_buf.at[par], sl_o[l].at[:, pl.ds(part * width, width)], ("sl", par))
        else:
            f_buf[:, pl.ds(part * tall, tall)] = nn(gu_buf[...], ring_t[slot])
            if part == width // tall - 1:
                free(("n", 1))
                _, s_f = norm(l, 1, b_down[l : l + 1, :], h_buf, f_buf, n_buf.at[1], r2_o[l])
                squares[3 * l + 2 : 3 * l + 3, :] = jnp.sum(s_f, axis=0, keepdims=True)
                save(n_buf.at[1], n2_o[l], ("n", 1))
                if l == layers - 1:
                    save(hb_buf, act, "act")

    def ring(at):
        kind, _, _, src, _ = chunks[at]
        buf = ring_t if kind == "down" else ring_w
        return pltpu.make_async_copy(src, buf.at[at % 2], sem_ring.at[at % 2])

    def relay(stage, at):
        if 0 <= at < total:
            for piece in chunks[at][4]:
                piece.start(stage)

    for at in range(3):
        relay(0, at)
    for at, (src, buf, _) in enumerate(shards):
        pltpu.make_async_copy(src, buf, sem_own.at[at]).wait()
    placed = []
    for at, (_, buf, full) in enumerate(shards):
        rows = buf.shape[1]
        for l in range(layers):
            dst = full[l].at[pl.ds(pl.multiple_of(fab.block() * rows, rows), rows)]
            placed.append(pltpu.make_async_copy(buf.at[l], dst, sem_own.at[4 + at * layers + l]))
            placed[-1].start()

    def widen(c, carry):
        rows = rows_of(c)
        h_buf[rows, :] = tok[rows, :].astype(F32)
        hb_buf[rows, :] = tok[rows, :]
        return carry

    lax.fori_loop(0, steps, widen, 0)
    for copy in placed:
        copy.wait()
    for at in range(-2, total + 1):
        relay(0, at + 3) if at + 3 >= 3 else None
        relay(1, at + 2)
        relay(2, at + 1)
        if 0 <= at < total:
            relay(3, at)
        if at - 1 >= 0:
            ring(at - 1).wait()
        if 0 <= at < total:
            for piece in chunks[at][4]:
                piece.finish()
            ring(at).start()
        if at - 1 >= 0:
            compute(at - 1)

    here = jnp.sum(vcol[...], axis=0, keepdims=True)
    squares[3 * layers :, :] = jnp.broadcast_to(here, (squares.shape[0] - 3 * layers, width))
    for at, copy in enumerate(saves):
        if at not in waited:
            copy.wait()
    for _, _, _, _, pieces in chunks:
        for piece in pieces:
            piece.drain()


def forward(sizes, tokens, vcol, vrow, gain, b_qv, b_out, b_ln, b_up, b_down, s_qkv, s_out, s_up, s_down):
    slots, width = tokens.shape
    layers, own = s_qkv.shape[0], s_qkv.shape[1]
    ff = s_up.shape[2]
    half = slots // 2
    tall = 256
    hbm = pl.BlockSpec(memory_space=pl.ANY)
    vm = pl.BlockSpec(memory_space=pltpu.VMEM)
    chunks = layers * (4 + ff // width + width // tall)
    pieces = layers * (
        (4 + ff // width) * sum(1 for c in shares(width) if c) + width // tall * sum(1 for c in shares(tall) if c)
    )
    saves = layers * (3 + 1 + 1 + ff // width + 1) + 1
    outs = []
    specs = []
    for shape, kind, spec in (
        ((slots, width), BF, hbm),
        ((slots, width), BF, hbm),
        ((slots, width), BF, hbm),
        ((HEADS, 2, half, half), BF, hbm),
        ((slots, ff), BF, hbm),
        ((slots, width), BF, hbm),
        ((slots, width), BF, hbm),
        ((slots, 1), F32, vm),
        ((slots, 1), F32, vm),
        ((width, 3 * width), BF, hbm),
        ((width, width), BF, hbm),
        ((width, ff), BF, hbm),
        ((ff, width), BF, hbm),
    ):
        outs += [jax.ShapeDtypeStruct(shape, kind)] * layers
        specs += [spec] * layers
    result = pl.pallas_call(
        functools.partial(forward_kernel, layers, sizes),
        out_shape=tuple(
            [jax.ShapeDtypeStruct((slots, width), BF), jax.ShapeDtypeStruct((8, width), F32)] + outs
        ),
        in_specs=[vm] * 9 + [hbm] * 4,
        out_specs=tuple([hbm, vm] + specs),
        scratch_shapes=[
            pltpu.VMEM((slots, width), F32),
            pltpu.VMEM((slots, width), BF),
            pltpu.VMEM((slots, width), BF),
            pltpu.VMEM((slots, width), BF),
            pltpu.VMEM((slots, width), BF),
            pltpu.VMEM((slots, width), BF),
            pltpu.VMEM((slots, ff), BF),
            pltpu.VMEM((slots, width), F32),
            pltpu.VMEM((HEADS, 2, half, half), BF),
            pltpu.VMEM((2, slots, width), BF),
            pltpu.VMEM((2, slots, width), BF),
            pltpu.VMEM((2, width, width), BF),
            pltpu.VMEM((2, ff, tall), BF),
            pltpu.VMEM(s_qkv.shape, BF),
            pltpu.VMEM(s_out.shape, BF),
            pltpu.VMEM(s_up.shape, BF),
            pltpu.VMEM(s_down.shape, BF),
            pltpu.SemaphoreType.DMA((pieces, 4)),
            pltpu.SemaphoreType.DMA((pieces, 4)),
            pltpu.SemaphoreType.DMA((4 + 4 * layers,)),
            pltpu.SemaphoreType.DMA((2,)),
            pltpu.SemaphoreType.DMA((saves,)),
        ],
        compiler_params=pltpu.CompilerParams(vmem_limit_bytes=62 << 20, collective_id=0, has_side_effects=True),
        name="forward",
    )(tokens, vcol, vrow, gain, b_qv, b_out, b_ln, b_up, b_down, s_qkv, s_out, s_up, s_down)
    act, squares = result[:2]
    kept = [list(result[2 + at * layers : 2 + (at + 1) * layers]) for at in range(13)]
    return act, squares, kept


def total_kernel(sizes, part, out, z_buf, acc, send, recv):
    fab = Fabric(sizes)
    barrier = pltpu.get_barrier_semaphore()
    around = [fab.device(**{axis: peer}) for axis in ("c", "z", "x", "y") for peer in fab.peers(axis)]
    for device in around:
        pl.semaphore_signal(barrier, inc=1, device_id=device, device_id_type=pl.DeviceIdType.MESH)
    pl.semaphore_wait(barrier, len(around))
    sem = 0
    slot = 0
    acc[...] = part[...]
    for axis in ("c", "z", "x", "y"):
        n = fab.size[axis]
        me = fab.at[axis]
        copies = []
        z_buf[slot + me] = acc[...]
        for peer in fab.peers(axis):
            copies.append(
                pltpu.make_async_remote_copy(
                    src_ref=z_buf.at[slot + me],
                    dst_ref=z_buf.at[slot + me],
                    send_sem=send.at[sem],
                    recv_sem=recv.at[sem],
                    device_id=fab.device(**{axis: peer}),
                    device_id_type=pl.DeviceIdType.MESH,
                )
            )
            copies[-1].start()
            sem += 1
        for copy in copies:
            copy.wait()
        total = z_buf[slot]
        for at in range(1, n):
            total = total + z_buf[slot + at]
        acc[...] = total
        slot += n
    out[...] = acc[...]


def total_of(sizes, part):
    vm = pl.BlockSpec(memory_space=pltpu.VMEM)
    steps = sum(n - 1 for n in sizes) + 1
    slots = sum(sizes) + 2
    return pl.pallas_call(
        functools.partial(total_kernel, sizes),
        out_shape=jax.ShapeDtypeStruct(part.shape, F32),
        in_specs=[vm],
        out_specs=vm,
        scratch_shapes=[
            pltpu.VMEM((slots,) + part.shape, F32),
            pltpu.VMEM(part.shape, F32),
            pltpu.SemaphoreType.DMA((steps,)),
            pltpu.SemaphoreType.DMA((steps,)),
        ],
        compiler_params=pltpu.CompilerParams(vmem_limit_bytes=32 << 20, collective_id=1, has_side_effects=True),
        name="total",
    )(part)


def normalize(stream, gain_row, shift_row):
    mean_row = jnp.mean(stream, axis=-1, keepdims=True)
    centred = stream - mean_row
    variance = jnp.mean(centred * centred, axis=-1, keepdims=True)
    inv_std = lax.rsqrt(variance + 1e-06)
    normed = centred * inv_std
    return normed * gain_row + shift_row, normed, inv_std


def forward_apart(tokens, vcol, vrow, gain, b_qv, b_out, b_ln, b_up, b_down, *shards):
    slots, width = tokens.shape
    layers = b_out.shape[0]
    half = slots // 2
    hd = width // HEADS
    blocks = vcol.reshape(2, half)
    same = blocks[:, :, None] == blocks[:, None, :]
    stream = tokens.astype(F32)
    kept = []
    squares = []
    for l in range(layers):
        mats = [lax.all_gather(w[l], AXES, axis=0, tiled=True) for w in shards]
        projected = nn(stream.astype(BF), mats[0])
        q = (projected[:, :width] + b_qv[l, 0]).astype(BF)
        k = projected[:, width : 2 * width].astype(BF)
        v = (projected[:, 2 * width :] + b_qv[l, 1]).astype(BF)
        q4, k4, v4 = (a.reshape(2, half, HEADS, hd) for a in (q, k, v))
        st = jnp.einsum("bqhd,bkhd->hbkq", q4, k4, preferred_element_type=F32) * hd ** (-0.5)
        st = jnp.where(same[None], st, -1e30)
        ex = jnp.exp(st - jnp.max(st, axis=2, keepdims=True))
        pt = (ex / jnp.sum(ex, axis=2, keepdims=True)).astype(BF)
        mixed = jnp.einsum("hbkq,bkhd->bqhd", pt, v4, preferred_element_type=F32).reshape(slots, width).astype(BF)
        branch = nn(mixed, mats[1]) + b_out[l]
        x1, n1, r1 = normalize(stream + branch, gain[l, 0], b_ln[l, 0])
        u = nn(x1.astype(BF), mats[2]) + b_up[l]
        phi = 0.5 * (1.0 + lax.erf(u * 0.7071067811865476))
        slope = (phi + u * (jnp.exp(-0.5 * u * u) * 0.3989422804014327)).astype(BF)
        ffn = nn((u * phi).astype(BF), mats[3]) + b_down[l]
        nxt, n2, r2 = normalize(x1 + ffn, gain[l, 1], b_ln[l, 1])
        squares += [jnp.sum(vcol * a * a, axis=0) for a in (stream, branch, ffn)]
        kept.append((q, k, v, pt, slope, n1.astype(BF), n2.astype(BF), r1, r2, *mats))
        stream = nxt
    here = jnp.broadcast_to(jnp.sum(vcol), (width,))
    return stream.astype(BF), jnp.stack(squares + [here] * (8 - 3 * layers)), [list(a) for a in zip(*kept)]


def local(
    sizes, tokens, lengths, w_qkv, w_out, w_up, w_down, ln_gain, bias_qv, bias_out, ln_bias, bias_up, bias_down, cotangent
):
    slots, width = tokens.shape
    layers = w_qkv.shape[0]
    half = slots // 2
    first, second = lengths[0, 0], lengths[0, 1]
    shift = jnp.where(first == half, 0, first)
    place = lax.rem(jnp.arange(slots, dtype=jnp.int32) + shift, slots)
    valid = (place < first + second).astype(F32)

    def turn(a, by):
        return lax.dynamic_slice_in_dim(jnp.concatenate([a, a], axis=0), by, slots, axis=0)

    run = functools.partial(forward, sizes) if w_qkv.shape[1] % 8 == 0 else forward_apart
    act, squares, kept = run(
        turn(tokens, shift), valid[:, None], valid[None, :], ln_gain, bias_qv, bias_out, ln_bias, bias_up, bias_down,
        w_qkv, w_out, w_up, w_down,
    )
    dh, part = backward(turn(cotangent, shift), valid[:, None], ln_gain, squares, kept)
    whole = total_of(sizes, part)
    back = lax.rem(slots - shift, slots)
    return (
        turn(act, back),
        turn(dh, back),
        whole[:, 0:2],
        whole[:, 2],
        whole[:, 3:5],
        whole[:, 5:9].reshape(layers, -1),
        whole[:, 9],
        jnp.sqrt(jnp.sum(whole[:, 10:13], axis=2) / (whole[:, 13, 0:1] * width)),
    )


def solution(mesh):
    pairs = mesh.shape["dp"] // 2
    ny = next(n for n in range(math.isqrt(pairs), 0, -1) if pairs % n == 0)
    sizes = (ny, pairs // ny, mesh.shape["shard"])
    rows = P(AXES, None)
    weight = P(None, AXES, None)
    in_specs = (rows, rows, weight, weight, weight, weight, P(), P(), P(), P(), P(), P(), rows)
    out_specs = (rows, rows, P(), P(), P(), P(), P(), P())
    return jax.shard_map(
        functools.partial(local, sizes), mesh=mesh, in_specs=in_specs, out_specs=out_specs, check_vma=False
    )
```

```python
import functools
import math

import jax
import jax.numpy as jnp
from jax import lax
from jax.experimental import pallas as pl
from jax.experimental.pallas import tpu as pltpu
from jax.sharding import PartitionSpec as P

BF = jnp.bfloat16
F32 = jnp.float32
HEADS = 16
AXES = ("dp", "shard")


def nt(a, b):
    return lax.dot_general(a, b, (((1,), (1,)), ((), ())), preferred_element_type=F32)


def nn(a, b):
    return lax.dot_general(a, b, (((1,), (0,)), ((), ())), preferred_element_type=F32)


def tn(a, b):
    return lax.dot_general(a, b, (((0,), (0,)), ((), ())), preferred_element_type=F32)


def fold8(t):
    return jnp.sum(t.reshape(t.shape[0] // 8, 8, t.shape[1]), axis=0)


class Ring:
    def __init__(self, buf, sem, segments):
        self.buf, self.sem, self.segments = buf, sem, segments
        self.slots, self.rows = buf.shape[0], buf.shape[1]
        self.base = 0

    def fetch(self, at):
        slot = lax.rem(at, self.slots)
        first = 0
        for ref, count in self.segments:
            if isinstance(at, int):
                if first <= at < first + count:
                    row = (at - first) * self.rows
                    pltpu.make_async_copy(ref.at[pl.ds(row, self.rows)], self.buf.at[slot], self.sem.at[slot]).start()
            else:

                @pl.when(jnp.logical_and(at >= first, at < first + count))
                def _(ref=ref, first=first):
                    row = pl.multiple_of((at - first) * self.rows, self.rows)
                    pltpu.make_async_copy(ref.at[pl.ds(row, self.rows)], self.buf.at[slot], self.sem.at[slot]).start()

            first += count

    def prime(self):
        for at in range(self.slots):
            self.fetch(at)

    def run(self, count, body):
        base = self.base

        def step(j, carry):
            at = base + j
            slot = lax.rem(at, self.slots)
            pltpu.make_async_copy(self.segments[0][0].at[pl.ds(0, self.rows)], self.buf.at[slot], self.sem.at[slot]).wait()
            body(j, self.buf[slot])
            self.fetch(at + self.slots)
            return carry

        lax.fori_loop(0, count, step, 0)
        self.base = base + count


def backward_kernel(layers, *refs):
    cot, valid, gain, squares = refs[:4]
    qkv, pt, slope, n1, n2, r1, r2, wqkv, wout, wup, wdown = [
        [ref.at[l] for l in range(layers)] for ref in refs[4:15]
    ]
    q, k, v = [[ref.at[part] for ref in qkv] for part in range(3)]
    backward_body(layers, cot, valid, gain, squares, q, k, v, pt, slope, n1, n2, r1, r2, wqkv, wout, wup, wdown, *refs[15:])


def backward_body(
    layers, cot, valid, gain, squares, q, k, v, pt, slope, n1, n2, r1, r2, wqkv, wout, wup, wdown,
    dh_out, grads,
    e_buf, x_buf, z_buf, du_buf, dp_buf, do_buf, cot_buf,
    q_buf, k_buf, v_buf, pt_buf, sl_buf, n1_buf, n2_buf,
    ring_a, ring_b, ring_c, sem_a, sem_b, sem_c, sem_in, sem_out,
):
    slots, width = e_buf.shape
    ff = du_buf.shape[1]
    heads = pt[0].shape[0]
    hd = width // heads
    half = slots // 2
    scale = hd ** (-0.5)
    order = list(reversed(range(layers)))

    sources = (n2, slope, n1, q, k, v, pt)
    buffers = (n2_buf, sl_buf, n1_buf, q_buf, k_buf, v_buf, pt_buf)

    def load(which, layer, par):
        return pltpu.make_async_copy(sources[which][layer], buffers[which].at[par], sem_in.at[par, which])

    cot_copy = pltpu.make_async_copy(cot, cot_buf, sem_out.at[0])
    cot_copy.start()
    load(0, order[0], 0).start()
    seg_a = []
    seg_b = []
    seg_c = []
    for l in order:
        seg_a += [(wdown[l], ff // ring_a.shape[1]), (wout[l], width // ring_a.shape[1])]
        seg_b += [(wup[l], width // ring_b.shape[1])]
        seg_c += [(wqkv[l], width // ring_c.shape[1])]
    ra, rb, rc = Ring(ring_a, sem_a, seg_a), Ring(ring_b, sem_b, seg_b), Ring(ring_c, sem_c, seg_c)
    ra.prime()
    load(1, order[0], 0).start()
    rb.prime()
    for which in range(2, 7):
        load(which, order[0], 0).start()
    rc.prime()
    for which in range(7):
        for step, l in enumerate(order[1:], 1):
            if step < 2:
                load(which, l, step).start()

    chunk = 32
    cot_copy.wait()

    def mask_cot(c, carry):
        rows = pl.ds(pl.multiple_of(c * chunk, chunk), chunk)
        e_buf[rows, :] = cot_buf[rows, :].astype(F32) * valid[rows, :]
        return carry

    lax.fori_loop(0, slots // chunk, mask_cot, 0)

    def norm_back(src, dst, gain_row, n_ref, r_ref):
        def step(c, carry):
            s_in, s_out = carry
            rows = pl.ds(pl.multiple_of(c * chunk, chunk), chunk)
            g = src[rows, :]
            n = n_ref[rows, :].astype(F32)
            ge = g * gain_row
            m1 = jnp.mean(ge, axis=1, keepdims=True)
            m2 = jnp.mean(ge * n, axis=1, keepdims=True)
            dz = r_ref[rows, :] * (ge - m1 - n * m2)
            dst[rows, :] = dz
            z_buf[rows, :] = dz.astype(BF)
            return (s_in + fold8(g), s_out + fold8(dz))

        zero = jnp.zeros((8, width), F32)
        s_in, s_out = lax.fori_loop(0, slots // chunk, step, (zero, zero))
        return jnp.sum(s_in, axis=0, keepdims=True), jnp.sum(s_out, axis=0, keepdims=True)

    for step, l in enumerate(order):
        par = step % 2

        load(0, l, par).wait()
        s_in, s_out = norm_back(e_buf, x_buf, gain[l, 1:2, :], n2_buf.at[par], r2[l])
        grads[l, 4:5, :] = s_in
        grads[l, 9:10, :] = s_out

        load(1, l, par).wait()
        wide = ring_a.shape[1]

        def down_body(j, w):
            cols = pl.ds(pl.multiple_of(j * wide, wide), wide)
            du = nt(z_buf[...], w) * sl_buf[par, :, cols].astype(F32)
            du_buf[:, cols] = du.astype(BF)
            part = jnp.sum(fold8(du), axis=0, keepdims=True)
            per = width // wide
            grads[l, pl.ds(5 + j // per, 1), pl.ds(pl.multiple_of(lax.rem(j, per) * wide, wide), wide)] = part

        ra.run(ff // wide, down_body)
        nb = ring_b.shape[1]

        def up_body(j, w):
            cols = pl.ds(pl.multiple_of(j * nb, nb), nb)
            x_buf[:, cols] = x_buf[:, cols] + nt(du_buf[...], w)

        rb.run(width // nb, up_body)

        load(2, l, par).wait()
        s_in, s_out = norm_back(x_buf, x_buf, gain[l, 0:1, :], n1_buf.at[par], r1[l])
        grads[l, 3:4, :] = s_in
        grads[l, 2:3, :] = s_out

        def out_body(j, w):
            cols = pl.ds(pl.multiple_of(j * wide, wide), wide)
            do_buf[:, cols] = nt(z_buf[...], w).astype(BF)

        ra.run(width // wide, out_body)

        for which in range(3, 7):
            load(which, l, par).wait()
        lane = lax.broadcasted_iota(jnp.int32, (1, 2 * hd), 1)
        sides = (lane < hd, lane >= hd)

        def pair(hp, carry):
            cols = pl.ds(pl.multiple_of(hp * 2 * hd, 2 * hd), 2 * hd)
            sum_q = jnp.zeros((8, 2 * hd), F32)
            sum_v = jnp.zeros((8, 2 * hd), F32)
            for b in range(2):
                rows = pl.ds(b * half, half)
                q2, k2, v2, do2 = (r[rows, cols] for r in (q_buf.at[par], k_buf.at[par], v_buf.at[par], do_buf))
                dq = dk = dv = None
                for side in range(2):
                    keep = sides[side]
                    zero = jnp.zeros_like(q2)
                    pb = pt_buf[par, 2 * hp + side, b]
                    dpt = nt(jnp.where(keep, v2, zero), do2)
                    p32 = pb.astype(F32)
                    t = p32 * dpt
                    inner = jnp.sum(fold8(t), axis=0, keepdims=True)
                    ds = (t - p32 * inner).astype(BF)
                    a_v = nn(pb, jnp.where(keep, do2, zero))
                    a_k = nn(ds, jnp.where(keep, q2, zero))
                    a_q = tn(ds, jnp.where(keep, k2, zero))
                    dv = a_v if dv is None else dv + a_v
                    dk = a_k if dk is None else dk + a_k
                    dq = a_q if dq is None else dq + a_q
                dq = dq * scale
                dk = dk * scale
                dp_buf[rows, cols] = dq.astype(BF)
                dp_buf[rows, pl.ds(pl.multiple_of(width + hp * 2 * hd, 2 * hd), 2 * hd)] = dk.astype(BF)
                dp_buf[rows, pl.ds(pl.multiple_of(2 * width + hp * 2 * hd, 2 * hd), 2 * hd)] = dv.astype(BF)
                sum_q = sum_q + fold8(dq)
                sum_v = sum_v + fold8(dv)
            grads[l, 0:1, cols] = jnp.sum(sum_q, axis=0, keepdims=True)
            grads[l, 1:2, cols] = jnp.sum(sum_v, axis=0, keepdims=True)
            return carry

        lax.fori_loop(0, heads // 2, pair, 0)
        nc = ring_c.shape[1]
        last = step == layers - 1

        def qkv_body(j, w):
            cols = pl.ds(pl.multiple_of(j * nc, nc), nc)
            e_buf[:, cols] = x_buf[:, cols] + nt(dp_buf[...], w)
            if last:
                pltpu.make_async_copy(e_buf.at[:, cols], dh_out.at[:, cols], sem_out.at[0]).start()

        rc.run(width // nc, qkv_body)
        for which in range(7):
            if step + 2 < layers:
                load(which, order[step + 2], par).start()
        grads[l, 10:13, :] = squares[3 * l : 3 * l + 3, :]
        grads[l, 13:14, :] = squares[3 * layers : 3 * layers + 1, :]
        grads[l, 14:16, :] = jnp.zeros((2, width), F32)

    for j in range(width // nc):
        cols = pl.ds(j * nc, nc)
        pltpu.make_async_copy(e_buf.at[:, cols], dh_out.at[:, cols], sem_out.at[0]).wait()


def backward(cot, valid, gain, squares, kept):
    slots, width = cot.shape
    layers, heads = kept[1].shape[:2]
    ff = kept[2].shape[2]
    half = slots // 2
    hbm = pl.BlockSpec(memory_space=pl.ANY)
    vm = pl.BlockSpec(memory_space=pltpu.VMEM)
    ta, tb, tc = min(512, width), min(256, width), min(256, width)
    return pl.pallas_call(
        functools.partial(backward_kernel, layers),
        out_shape=(
            jax.ShapeDtypeStruct((slots, width), F32),
            jax.ShapeDtypeStruct((layers, 16, width), F32),
        ),
        in_specs=[hbm, vm, vm, vm] + [hbm] * 5 + [vm] * 2 + [hbm] * 4,
        out_specs=(hbm, vm),
        scratch_shapes=[
            pltpu.VMEM((slots, width), F32),
            pltpu.VMEM((slots, width), F32),
            pltpu.VMEM((slots, width), BF),
            pltpu.VMEM((slots, ff), BF),
            pltpu.VMEM((slots, 3 * width), BF),
            pltpu.VMEM((slots, width), BF),
            pltpu.VMEM((slots, width), BF),
        ]
        + [pltpu.VMEM((2, slots, width), BF)] * 3
        + [
            pltpu.VMEM((2, heads, 2, half, half), BF),
            pltpu.VMEM((2, slots, ff), BF),
            pltpu.VMEM((2, slots, width), BF),
            pltpu.VMEM((2, slots, width), BF),
            pltpu.VMEM((3, ta, width), BF),
            pltpu.VMEM((2, tb, ff), BF),
            pltpu.VMEM((2, tc, 3 * width), BF),
            pltpu.SemaphoreType.DMA((3,)),
            pltpu.SemaphoreType.DMA((2,)),
            pltpu.SemaphoreType.DMA((2,)),
            pltpu.SemaphoreType.DMA((2, 7)),
            pltpu.SemaphoreType.DMA((1,)),
        ],
        compiler_params=pltpu.CompilerParams(vmem_limit_bytes=67000000),
        name="backward",
    )(cot, valid, gain, squares, *kept)


class Fabric:
    def __init__(self, sizes):
        ny, nx, nz = sizes
        dp = lax.axis_index("dp")
        self.size = {"y": ny, "x": nx, "z": nz, "c": 2}
        self.at = {"z": lax.axis_index("shard"), "c": lax.rem(dp, 2), "x": lax.rem(dp // 2, nx), "y": dp // (2 * nx)}

    def device(self, **moved):
        at = {**self.at, **moved}
        return ((at["y"] * self.size["x"] + at["x"]) * 2 + at["c"], at["z"])

    def peers(self, axis):
        n = self.size[axis]
        return [lax.rem(self.at[axis] + step, n) for step in range(1, n)]

    def block(self, **moved):
        at = {**self.at, **moved}
        return ((at["y"] * self.size["x"] + at["x"]) * 2 + at["c"]) * self.size["z"] + at["z"]


class Relay:
    def __init__(self, fabric, kinds, per, count, sems):
        self.fab, self.kinds, self.per, self.count = fabric, kinds, per, count
        self.send, self.recv = sems
        at = fabric.at
        self.pair = lax.div(at["z"], 2) * 2
        self.other = 2 - self.pair
        self.mate = self.pair + 1 - lax.rem(at["z"], 2)
        self.inner = jnp.logical_or(at["z"] == 1, at["z"] == 2)

    def wait(self, sem, blocks):
        _, _, _, full, rows, cols = self.kinds[0]
        part = full.at[0, pl.ds(0, blocks * rows), pl.ds(0, cols // 2)]
        pltpu.make_async_copy(part, part, sem).wait()

    def each(self, t, act):
        l = lax.div(t, self.per)
        j = t - l * self.per
        for first, number, own, full, rows, cols in self.kinds:

            @pl.when(jnp.logical_and(j >= first, j < first + number))
            def _(first=first, own=own, full=full, rows=rows, cols=cols):
                for piece in range(2):
                    col = pl.multiple_of((j - first) * cols + piece * (cols // 2), cols // 2)
                    act(l, own, full, rows, pl.ds(col, cols // 2), piece)

    def push(self, t, piece, sem, device, src, dst):
        pltpu.make_async_remote_copy(
            src_ref=src,
            dst_ref=dst,
            send_sem=self.send.at[2 * t + piece, sem],
            recv_sem=self.recv.at[2 * t + piece, sem],
            device_id=device,
            device_id_type=pl.DeviceIdType.MESH,
        ).start()

    def stage(self, s, t):
        fab = self.fab
        at = fab.at
        partner = fab.device(c=1 - at["c"])

        @pl.when(jnp.logical_and(t >= 0, t < self.count))
        def _():
            for piece in range(2):
                if s == 1:
                    self.wait(self.recv.at[2 * t + piece, 0], 1)
                elif s == 2:
                    self.wait(self.recv.at[2 * t + piece, 1], 2)
                elif s == 3:
                    pl.when(self.inner)(lambda piece=piece: self.wait(self.recv.at[2 * t + piece, 2], 4))
                elif s == 4:
                    pl.when(jnp.logical_not(self.inner))(
                        lambda piece=piece: self.wait(self.recv.at[2 * t + piece, 2], 4)
                    )
                elif s == 5:
                    self.wait(self.recv.at[2 * t + piece, 3], 8)

            def act(l, own, full, rows, cols, piece):
                u, v = (("x", "y"), ("y", "x"))[piece]

                def view(first, blocks):
                    return full.at[l, pl.ds(pl.multiple_of(first * rows, rows), blocks * rows), cols]

                def out(sem, device, runs):
                    for first, blocks in runs:
                        self.push(t, piece, sem, device, view(first, blocks), view(first, blocks))

                far = [(fab.block(**{u: each, "z": self.other}), 2) for each in range(2)]
                if s == 0:
                    mine = view(fab.block(), 1)
                    self.push(t, piece, 0, fab.device(z=self.mate), own.at[l, :, cols], mine)
                    self.push(t, piece, 4, partner, own.at[l, :, cols], mine)
                elif s == 1:
                    out(1, fab.device(**{u: 1 - at[u]}), [(fab.block(z=self.pair), 2)])
                    out(4, partner, [(fab.block(z=self.mate), 1)])
                elif s == 2:
                    near = [(fab.block(**{u: each, "z": self.pair}), 2) for each in range(2)]
                    pl.when(self.inner)(lambda: out(2, fab.device(z=3 - at["z"]), near))
                    out(4, partner, [(fab.block(**{u: 1 - at[u], "z": self.pair}), 2)])
                elif s == 3:

                    @pl.when(self.inner)
                    def _():
                        out(2, fab.device(z=self.mate), far)
                        out(4, partner, far)

                elif s == 4:
                    out(3, fab.device(**{v: 1 - at[v]}), [(fab.block(**{u: each, "z": 0}), 4) for each in range(2)])
                    pl.when(jnp.logical_not(self.inner))(lambda: out(4, partner, far))
                else:
                    out(4, partner, [(fab.block(**{v: 1 - at[v], u: each, "z": 0}), 4) for each in range(2)])

            self.each(t, act)

    def finish(self, t):
        for piece in range(2):
            self.wait(self.recv.at[2 * t + piece, 4], 16)

    def drain(self, t):
        for piece in range(2):
            for sem, blocks in ((0, 1), (1, 2), (3, 8), (4, 16)):
                self.wait(self.send.at[2 * t + piece, sem], blocks)
            pl.when(self.inner)(lambda piece=piece: self.wait(self.send.at[2 * t + piece, 2], 8))


LEADS = (9, 7, 5, 4, 2, 1)


def forward_kernel(layers, sizes, *refs):
    (tok, vcol, vrow, gain, b_qv, b_out, b_ln, b_up, b_down, s_qkv, s_out, s_up, s_down) = refs[:13]
    (act, squares, qkv_o, pt_o, sl_o, n1_o, n2_o, r1_o, r2_o, f_qkv, f_out, f_up, f_down) = refs[13:26]
    (
        h_buf, hb_buf, qkv_buf, mix_buf, gu_buf, f_buf, pt_buf, sl_buf, n_buf,
        ring_w, ring_t, own_qkv, own_out, own_up, own_down,
        sem_send, sem_recv, sem_own, sem_ring, sem_save,
    ) = refs[26:]
    slots, width = tok.shape
    ff = gu_buf.shape[1]
    heads = pt_buf.shape[0]
    hd = width // heads
    half = slots // 2
    scale = hd ** (-0.5)
    tall = ring_t.shape[2]
    fab = Fabric(sizes)

    shards = ((s_qkv, own_qkv, f_qkv), (s_out, own_out, f_out), (s_up, own_up, f_up), (s_down, own_down, f_down))
    for at, (src, buf, _) in enumerate(shards):
        pltpu.make_async_copy(src, buf, sem_own.at[at]).start()
    barrier = pltpu.get_barrier_semaphore()
    around = [fab.device(**{axis: peer}) for axis in ("z", "x", "y", "c") for peer in fab.peers(axis)]
    for device in around:
        pl.semaphore_signal(barrier, inc=1, device_id=device, device_id_type=pl.DeviceIdType.MESH)
    pl.semaphore_wait(barrier, len(around))

    ups, downs = ff // width, width // tall
    kinds = (
        (0, 3, s_qkv, f_qkv, s_qkv.shape[1], width),
        (3, 1, s_out, f_out, s_out.shape[1], width),
        (4, ups, s_up, f_up, s_up.shape[1], width),
        (4 + ups, downs, s_down, f_down, s_down.shape[1], tall),
    )
    per = 4 + ups + downs
    total = layers * per
    relay = Relay(fab, kinds, per, total, (sem_send, sem_recv))

    def save(src, dst, key):
        pltpu.make_async_copy(src, dst, sem_save.at[key]).start()

    def free(src, dst, key, when):
        pl.when(when)(lambda: pltpu.make_async_copy(src, dst, sem_save.at[key]).wait())

    chunk = 32
    steps = slots // chunk

    def rows_of(c):
        return pl.ds(pl.multiple_of(c * chunk, chunk), chunk)

    def tiles(w, lhs, count, body, tile=256):
        def step(j, carry):
            cols = pl.ds(pl.multiple_of(j * tile, tile), tile)
            body(cols, nn(lhs[...], w[:, cols]), j * tile)
            return carry

        lax.fori_loop(0, count // tile, step, 0)

    def norm(l, which, bias_row, base, branch, n_dst, r_dst):
        zero = jnp.zeros((8, width), F32)
        gain_row = gain[l, which : which + 1, :]
        shift_row = b_ln[l, which : which + 1, :]

        def step(c, carry):
            s_h, s_a = carry
            rows = rows_of(c)
            a = branch[rows, :] + bias_row
            h = base[rows, :]
            z = h + a
            mean = jnp.mean(z, axis=1, keepdims=True)
            centred = z - mean
            var = jnp.mean(centred * centred, axis=1, keepdims=True)
            inv = lax.rsqrt(var + 1e-06)
            n = centred * inv
            y = n * gain_row + shift_row
            base[rows, :] = y
            hb_buf[rows, :] = y.astype(BF)
            n_dst[rows, :] = n.astype(BF)
            r_dst[rows, :] = inv
            ok = vcol[rows, :]
            return s_h + fold8(ok * h * h), s_a + fold8(ok * a * a)

        return lax.fori_loop(0, steps, step, (zero, zero))

    def attention():
        lane = lax.broadcasted_iota(jnp.int32, (1, 2 * hd), 1)
        sides = (lane < hd, lane >= hd)

        def pair(hp, carry):
            cols = pl.ds(pl.multiple_of(hp * 2 * hd, 2 * hd), 2 * hd)
            for b in range(2):
                rows = pl.ds(b * half, half)
                q2, k2, v2 = qkv_buf[0, rows, cols], qkv_buf[1, rows, cols], qkv_buf[2, rows, cols]
                mixed = None
                for side in range(2):
                    keep = sides[side]
                    zero = jnp.zeros_like(q2)
                    st = nt(jnp.where(keep, k2, zero), q2) * scale
                    if b == 1:
                        st = jnp.where(vcol[rows, :] == vrow[:, rows], st, -1e30)
                    top = jnp.max(st, axis=0, keepdims=True)
                    ex = jnp.exp(st - top)
                    p = (ex * (1.0 / jnp.sum(ex, axis=0, keepdims=True))).astype(BF)
                    pt_buf[2 * hp + side, b] = p
                    o = tn(p, jnp.where(keep, v2, zero))
                    mixed = o if mixed is None else mixed + o
                mix_buf[rows, cols] = mixed.astype(BF)
            return carry

        lax.fori_loop(0, heads // 2, pair, 0)

    def compute(t):
        l = lax.div(t, per)
        j = t - l * per
        slot = lax.rem(t, 2)
        later = l > 0

        @pl.when(j < 3)
        def _():
            free(qkv_buf.at[j], qkv_o.at[0, j], j, later)
            keep = (j != 1).astype(F32)

            def body(cols, t, first):
                bias = b_qv[l, pl.ds(lax.div(j, 2), 1), cols] * keep
                qkv_buf[j, :, cols] = (t + bias).astype(BF)

            tiles(ring_w.at[slot], hb_buf, width, body)
            save(qkv_buf.at[j], qkv_o.at[l, j], j)

            @pl.when(j == 2)
            def _():
                free(pt_buf, pt_o.at[0], 3, later)
                attention()
                save(pt_buf, pt_o.at[l], 3)

        @pl.when(j == 3)
        def _():
            def body(cols, t, first):
                f_buf[:, cols] = t

            tiles(ring_w.at[slot], mix_buf, width, body)
            free(n_buf.at[0], n1_o.at[0], 4, later)
            s_h, s_a = norm(l, 0, b_out[pl.ds(l, 1), :], h_buf, f_buf, n_buf.at[0], r1_o.at[l])
            squares[pl.ds(3 * l, 1), :] = jnp.sum(s_h, axis=0, keepdims=True)
            squares[pl.ds(3 * l + 1, 1), :] = jnp.sum(s_a, axis=0, keepdims=True)
            save(n_buf.at[0], n1_o.at[l], 4)

        @pl.when(jnp.logical_and(j >= 4, j < 4 + ups))
        def _():
            part = j - 4
            par = lax.rem(part, 2)
            start = pl.multiple_of(part * width, width)
            free(sl_buf.at[par], sl_o.at[0, :, pl.ds(0, width)], 6 + par, jnp.logical_or(later, part >= 2))

            def body(cols, t, first):
                wide = pl.ds(pl.multiple_of(part * width + first, 256), 256)
                u = t + b_up[pl.ds(l, 1), wide]
                phi = 0.5 * (1.0 + lax.erf(u * 0.7071067811865476))
                sl_buf[par, :, cols] = (phi + u * (jnp.exp(-0.5 * u * u) * 0.3989422804014327)).astype(BF)
                gu_buf[:, wide] = (u * phi).astype(BF)

            tiles(ring_w.at[slot], hb_buf, width, body)
            save(sl_buf.at[par], sl_o.at[l, :, pl.ds(start, width)], 6 + par)

        @pl.when(j >= 4 + ups)
        def _():
            part = j - 4 - ups
            f_buf[:, pl.ds(pl.multiple_of(part * tall, tall), tall)] = nn(gu_buf[...], ring_t[slot])

            @pl.when(part == downs - 1)
            def _():
                free(n_buf.at[1], n2_o.at[0], 5, later)
                _, s_f = norm(l, 1, b_down[pl.ds(l, 1), :], h_buf, f_buf, n_buf.at[1], r2_o.at[l])
                squares[pl.ds(3 * l + 2, 1), :] = jnp.sum(s_f, axis=0, keepdims=True)
                save(n_buf.at[1], n2_o.at[l], 5)

    def ring_start(t):
        l = lax.div(t, per)
        j = t - l * per
        slot = lax.rem(t, 2)
        for first, number, _, full, _, cols in kinds:
            buf = ring_t if cols == tall else ring_w

            @pl.when(jnp.logical_and(j >= first, j < first + number))
            def _(first=first, full=full, cols=cols, buf=buf):
                src = full.at[l, :, pl.ds(pl.multiple_of((j - first) * cols, cols), cols)]
                pltpu.make_async_copy(src, buf.at[slot], sem_ring.at[slot]).start()

    def ring_wait(t):
        slot = lax.rem(t, 2)
        pltpu.make_async_copy(f_out.at[0], ring_w.at[slot], sem_ring.at[slot]).wait()

    early = LEADS[0] - LEADS[1]
    for t in range(early):
        relay.stage(0, jnp.int32(t))
    for at, (src, buf, _) in enumerate(shards):
        pltpu.make_async_copy(src, buf, sem_own.at[at]).wait()
    placed = []
    for at, (_, buf, full) in enumerate(shards):
        rows = buf.shape[1]
        for l in range(layers):
            dst = full.at[l, pl.ds(pl.multiple_of(fab.block() * rows, rows), rows)]
            placed.append(pltpu.make_async_copy(buf.at[l], dst, sem_own.at[4 + at * layers + l]))
            placed[-1].start()

    def widen(c, carry):
        rows = rows_of(c)
        h_buf[rows, :] = tok[rows, :].astype(F32)
        hb_buf[rows, :] = tok[rows, :]
        return carry

    lax.fori_loop(0, steps, widen, 0)
    for copy in placed:
        copy.wait()

    def step(i, carry):
        at = i - LEADS[1]
        for s, lead in enumerate(LEADS):
            relay.stage(s, at + lead)
        pl.when(jnp.logical_and(at >= 1, at <= total))(lambda: ring_wait(at - 1))

        @pl.when(jnp.logical_and(at >= 0, at < total))
        def _():
            relay.finish(at)
            ring_start(at)

        pl.when(at >= 1)(lambda: relay.drain(at - 1))
        pl.when(at >= 1)(lambda: compute(at - 1))
        return carry

    lax.fori_loop(0, total + 1 + LEADS[1], step, 0)
    pltpu.make_async_copy(hb_buf, act, sem_own.at[0]).start()
    here = jnp.sum(vcol[...], axis=0, keepdims=True)
    squares[3 * layers :, :] = jnp.broadcast_to(here, (squares.shape[0] - 3 * layers, width))
    for part in range(3):
        free(qkv_buf.at[part], qkv_o.at[0, part], part, True)
    free(pt_buf, pt_o.at[0], 3, True)
    free(n_buf.at[0], n1_o.at[0], 4, True)
    free(n_buf.at[1], n2_o.at[0], 5, True)
    for par in range(2):
        free(sl_buf.at[par], sl_o.at[0, :, pl.ds(0, width)], 6 + par, True)
    pltpu.make_async_copy(hb_buf, act, sem_own.at[0]).wait()


def forward(sizes, tokens, vcol, vrow, gain, b_qv, b_out, b_ln, b_up, b_down, s_qkv, s_out, s_up, s_down):
    slots, width = tokens.shape
    layers = s_qkv.shape[0]
    ff = s_up.shape[2]
    half = slots // 2
    tall = width * width // ff
    hbm = pl.BlockSpec(memory_space=pl.ANY)
    vm = pl.BlockSpec(memory_space=pltpu.VMEM)
    chunks = layers * (4 + ff // width + width // tall)
    outs = [
        ((slots, width), BF, hbm),
        ((8, width), F32, vm),
        ((layers, 3, slots, width), BF, hbm),
        ((layers, HEADS, 2, half, half), BF, hbm),
        ((layers, slots, ff), BF, hbm),
        ((layers, slots, width), BF, hbm),
        ((layers, slots, width), BF, hbm),
        ((layers, slots, 1), F32, vm),
        ((layers, slots, 1), F32, vm),
        ((layers, width, 3 * width), BF, hbm),
        ((layers, width, width), BF, hbm),
        ((layers, width, ff), BF, hbm),
        ((layers, ff, width), BF, hbm),
    ]
    result = pl.pallas_call(
        functools.partial(forward_kernel, layers, sizes),
        out_shape=tuple(jax.ShapeDtypeStruct(shape, kind) for shape, kind, _ in outs),
        in_specs=[vm] * 9 + [hbm] * 4,
        out_specs=tuple(spec for _, _, spec in outs),
        scratch_shapes=[
            pltpu.VMEM((slots, width), F32),
            pltpu.VMEM((slots, width), BF),
            pltpu.VMEM((3, slots, width), BF),
            pltpu.VMEM((slots, width), BF),
            pltpu.VMEM((slots, ff), BF),
            pltpu.VMEM((slots, width), F32),
            pltpu.VMEM((HEADS, 2, half, half), BF),
            pltpu.VMEM((2, slots, width), BF),
            pltpu.VMEM((2, slots, width), BF),
            pltpu.VMEM((2, width, width), BF),
            pltpu.VMEM((2, ff, tall), BF),
            pltpu.VMEM(s_qkv.shape, BF),
            pltpu.VMEM(s_out.shape, BF),
            pltpu.VMEM(s_up.shape, BF),
            pltpu.VMEM(s_down.shape, BF),
            pltpu.SemaphoreType.DMA((2 * chunks, 5)),
            pltpu.SemaphoreType.DMA((2 * chunks, 5)),
            pltpu.SemaphoreType.DMA((4 + 4 * layers,)),
            pltpu.SemaphoreType.DMA((2,)),
            pltpu.SemaphoreType.DMA((8,)),
        ],
        compiler_params=pltpu.CompilerParams(vmem_limit_bytes=62 << 20, collective_id=0, has_side_effects=True),
        name="forward",
    )(tokens, vcol, vrow, gain, b_qv, b_out, b_ln, b_up, b_down, s_qkv, s_out, s_up, s_down)
    return result[0], result[1], list(result[2:])


def total_kernel(sizes, part, out, z_buf, acc, send, recv):
    fab = Fabric(sizes)
    barrier = pltpu.get_barrier_semaphore()
    around = [fab.device(**{axis: peer}) for axis in ("c", "z", "x", "y") for peer in fab.peers(axis)]
    for device in around:
        pl.semaphore_signal(barrier, inc=1, device_id=device, device_id_type=pl.DeviceIdType.MESH)
    pl.semaphore_wait(barrier, len(around))
    sem = 0
    slot = 0
    acc[...] = part[...]
    for axis in ("c", "z", "x", "y"):
        n = fab.size[axis]
        me = fab.at[axis]
        copies = []
        z_buf[slot + me] = acc[...]
        for peer in fab.peers(axis):
            copies.append(
                pltpu.make_async_remote_copy(
                    src_ref=z_buf.at[slot + me],
                    dst_ref=z_buf.at[slot + me],
                    send_sem=send.at[sem],
                    recv_sem=recv.at[sem],
                    device_id=fab.device(**{axis: peer}),
                    device_id_type=pl.DeviceIdType.MESH,
                )
            )
            copies[-1].start()
            sem += 1
        for copy in copies:
            copy.wait()
        total = z_buf[slot]
        for at in range(1, n):
            total = total + z_buf[slot + at]
        acc[...] = total
        slot += n
    out[...] = acc[...]


def total_of(sizes, part):
    vm = pl.BlockSpec(memory_space=pltpu.VMEM)
    steps = sum(n - 1 for n in sizes) + 1
    slots = sum(sizes) + 2
    return pl.pallas_call(
        functools.partial(total_kernel, sizes),
        out_shape=jax.ShapeDtypeStruct(part.shape, F32),
        in_specs=[vm],
        out_specs=vm,
        scratch_shapes=[
            pltpu.VMEM((slots,) + part.shape, F32),
            pltpu.VMEM(part.shape, F32),
            pltpu.SemaphoreType.DMA((steps,)),
            pltpu.SemaphoreType.DMA((steps,)),
        ],
        compiler_params=pltpu.CompilerParams(vmem_limit_bytes=32 << 20, collective_id=1, has_side_effects=True),
        name="total",
    )(part)


def normalize(stream, gain_row, shift_row):
    mean_row = jnp.mean(stream, axis=-1, keepdims=True)
    centred = stream - mean_row
    variance = jnp.mean(centred * centred, axis=-1, keepdims=True)
    inv_std = lax.rsqrt(variance + 1e-06)
    normed = centred * inv_std
    return normed * gain_row + shift_row, normed, inv_std


def forward_apart(tokens, vcol, vrow, gain, b_qv, b_out, b_ln, b_up, b_down, *shards):
    slots, width = tokens.shape
    layers = b_out.shape[0]
    half = slots // 2
    hd = width // HEADS
    blocks = vcol.reshape(2, half)
    same = blocks[:, :, None] == blocks[:, None, :]
    stream = tokens.astype(F32)
    kept = []
    squares = []
    for l in range(layers):
        mats = [lax.all_gather(w[l], AXES, axis=0, tiled=True) for w in shards]
        projected = nn(stream.astype(BF), mats[0])
        q = (projected[:, :width] + b_qv[l, 0]).astype(BF)
        k = projected[:, width : 2 * width].astype(BF)
        v = (projected[:, 2 * width :] + b_qv[l, 1]).astype(BF)
        q4, k4, v4 = (a.reshape(2, half, HEADS, hd) for a in (q, k, v))
        st = jnp.einsum("bqhd,bkhd->hbkq", q4, k4, preferred_element_type=F32) * hd ** (-0.5)
        st = jnp.where(same[None], st, -1e30)
        ex = jnp.exp(st - jnp.max(st, axis=2, keepdims=True))
        pt = (ex / jnp.sum(ex, axis=2, keepdims=True)).astype(BF)
        mixed = jnp.einsum("hbkq,bkhd->bqhd", pt, v4, preferred_element_type=F32).reshape(slots, width).astype(BF)
        branch = nn(mixed, mats[1]) + b_out[l]
        x1, n1, r1 = normalize(stream + branch, gain[l, 0], b_ln[l, 0])
        u = nn(x1.astype(BF), mats[2]) + b_up[l]
        phi = 0.5 * (1.0 + lax.erf(u * 0.7071067811865476))
        slope = (phi + u * (jnp.exp(-0.5 * u * u) * 0.3989422804014327)).astype(BF)
        ffn = nn((u * phi).astype(BF), mats[3]) + b_down[l]
        nxt, n2, r2 = normalize(x1 + ffn, gain[l, 1], b_ln[l, 1])
        squares += [jnp.sum(vcol * a * a, axis=0) for a in (stream, branch, ffn)]
        kept.append((jnp.stack([q, k, v]), pt, slope, n1.astype(BF), n2.astype(BF), r1, r2, *mats))
        stream = nxt
    here = jnp.broadcast_to(jnp.sum(vcol), (width,))
    return stream.astype(BF), jnp.stack(squares + [here] * (8 - 3 * layers)), [jnp.stack(a) for a in zip(*kept)]


def local(
    sizes, tokens, lengths, w_qkv, w_out, w_up, w_down, ln_gain, bias_qv, bias_out, ln_bias, bias_up, bias_down, cotangent
):
    slots, width = tokens.shape
    layers = w_qkv.shape[0]
    half = slots // 2
    first, second = lengths[0, 0], lengths[0, 1]
    shift = jnp.where(first == half, 0, first)
    place = lax.rem(jnp.arange(slots, dtype=jnp.int32) + shift, slots)
    valid = (place < first + second).astype(F32)

    def turn(a, by):
        return lax.dynamic_slice_in_dim(jnp.concatenate([a, a], axis=0), by, slots, axis=0)

    run = functools.partial(forward, sizes) if sizes == (2, 2, 4) else forward_apart
    act, squares, kept = run(
        turn(tokens, shift), valid[:, None], valid[None, :], ln_gain, bias_qv, bias_out, ln_bias, bias_up, bias_down,
        w_qkv, w_out, w_up, w_down,
    )
    dh, part = backward(turn(cotangent, shift), valid[:, None], ln_gain, squares, kept)
    whole = total_of(sizes, part)
    back = lax.rem(slots - shift, slots)
    return (
        turn(act, back),
        turn(dh, back),
        whole[:, 0:2],
        whole[:, 2],
        whole[:, 3:5],
        whole[:, 5:9].reshape(layers, -1),
        whole[:, 9],
        jnp.sqrt(jnp.sum(whole[:, 10:13], axis=2) / (whole[:, 13, 0:1] * width)),
    )


def solution(mesh):
    pairs = mesh.shape["dp"] // 2
    ny = next(n for n in range(math.isqrt(pairs), 0, -1) if pairs % n == 0)
    sizes = (ny, pairs // ny, mesh.shape["shard"])
    rows = P(AXES, None)
    weight = P(None, AXES, None)
    in_specs = (rows, rows, weight, weight, weight, weight, P(), P(), P(), P(), P(), P(), rows)
    out_specs = (rows, rows, P(), P(), P(), P(), P(), P())
    return jax.shard_map(
        functools.partial(local, sizes), mesh=mesh, in_specs=in_specs, out_specs=out_specs, check_vma=False
    )
```

```python
import functools
import math

import jax
import jax.numpy as jnp
from jax import lax
from jax.experimental import pallas as pl
from jax.experimental.pallas import tpu as pltpu
from jax.sharding import PartitionSpec as P

BF = jnp.bfloat16
F32 = jnp.float32
HEADS = 16
AXES = ("dp", "shard")
KERNEL_MESH = (2, 2, 4)


def nt(a, b):
    return lax.dot_general(a, b, (((1,), (1,)), ((), ())), preferred_element_type=F32)


def nn(a, b):
    return lax.dot_general(a, b, (((1,), (0,)), ((), ())), preferred_element_type=F32)


def tn(a, b):
    return lax.dot_general(a, b, (((0,), (0,)), ((), ())), preferred_element_type=F32)


def fold8(t):
    return jnp.sum(t.reshape(t.shape[0] // 8, 8, t.shape[1]), axis=0)


class Ring:
    def __init__(self, buf, sem, segments):
        self.buf, self.sem, self.segments = buf, sem, segments
        self.slots, self.rows = buf.shape[0], buf.shape[1]
        self.base = 0

    def fetch(self, at):
        slot = lax.rem(at, self.slots)
        first = 0
        for ref, count in self.segments:
            if isinstance(at, int):
                if first <= at < first + count:
                    row = (at - first) * self.rows
                    pltpu.make_async_copy(ref.at[pl.ds(row, self.rows)], self.buf.at[slot], self.sem.at[slot]).start()
            else:

                @pl.when(jnp.logical_and(at >= first, at < first + count))
                def _(ref=ref, first=first):
                    row = pl.multiple_of((at - first) * self.rows, self.rows)
                    pltpu.make_async_copy(ref.at[pl.ds(row, self.rows)], self.buf.at[slot], self.sem.at[slot]).start()

            first += count

    def prime(self):
        for at in range(self.slots):
            self.fetch(at)

    def run(self, count, body, first=0):
        base = self.base

        def step(j, carry):
            at = base + j
            slot = lax.rem(at, self.slots)
            pltpu.make_async_copy(self.segments[0][0].at[pl.ds(0, self.rows)], self.buf.at[slot], self.sem.at[slot]).wait()
            body(first + j, self.buf[slot])
            self.fetch(at + self.slots)
            return carry

        lax.fori_loop(0, count, step, 0)
        self.base = base + count


class Fabric:
    def __init__(self, sizes):
        ny, nx, nz = sizes
        dp = lax.axis_index("dp")
        self.size = {"y": ny, "x": nx, "z": nz, "c": 2}
        self.at = {"z": lax.axis_index("shard"), "c": lax.rem(dp, 2), "x": lax.rem(dp // 2, nx), "y": dp // (2 * nx)}

    def device(self, **moved):
        at = {**self.at, **moved}
        return ((at["y"] * self.size["x"] + at["x"]) * 2 + at["c"], at["z"])

    def peers(self, axis):
        n = self.size[axis]
        return [lax.rem(self.at[axis] + step, n) for step in range(1, n)]

    def block(self, **moved):
        at = {**self.at, **moved}
        return ((at["y"] * self.size["x"] + at["x"]) * 2 + at["c"]) * self.size["z"] + at["z"]


class Total:
    def __init__(self, fabric, rest):
        (self.plane, self.line, self.mine, self.late, self.late_plane, self.late_line, self.send, self.recv) = rest
        self.fab = fabric
        self.me = lax.axis_index("dp")
        self.z = fabric.at["z"]
        self.n, self.nz = self.plane.shape[0], fabric.size["z"]
        self.mates = [(lax.rem(self.me + step, self.n), self.z) for step in range(1, self.n)]
        self.others = [(self.me, lax.rem(self.z + step, self.nz)) for step in range(1, self.nz)]

    def greet(self):
        barrier = pltpu.get_barrier_semaphore()
        for device in self.mates + self.others:
            pl.semaphore_signal(barrier, inc=1, device_id=device, device_id_type=pl.DeviceIdType.MESH)

    def met(self):
        pl.semaphore_wait(pltpu.get_barrier_semaphore(), len(self.mates) + len(self.others))

    def push(self, src, dst, sem, device):
        pltpu.make_async_remote_copy(
            src_ref=src,
            dst_ref=dst,
            send_sem=self.send.at[sem],
            recv_sem=self.recv.at[sem],
            device_id=device,
            device_id_type=pl.DeviceIdType.MESH,
        ).start()

    def wait(self, part, sems):
        for sem in sems:
            pltpu.make_async_copy(part, part, sem).wait()

    def share(self, ref, at):
        cols = ref.shape[2] // self.n
        return ref.at[:, :, pl.ds(pl.multiple_of(at * cols, cols), cols)]

    def spread(self, part):
        self.plane[self.me] = self.share(part, self.me)[...]
        for device in self.mates:
            self.push(self.share(part, device[0]), self.plane.at[self.me], 0, device)

    def along(self):
        self.wait(self.plane.at[pl.ds(0, self.n - 1)], (self.send.at[0], self.recv.at[0]))
        self.line[self.z] = self.added(self.plane)
        for device in self.others:
            self.push(self.line.at[self.z], self.line.at[self.z], 1, device)

    def back(self, out):
        self.wait(self.line.at[pl.ds(0, self.nz - 1)], (self.send.at[1], self.recv.at[1]))
        total = self.added(self.line)
        self.mine[...] = total
        self.share(out, self.me)[...] = total
        for device in self.mates:
            self.push(self.mine, self.share(out, self.me), 2, device)

    def late_spread(self):
        self.late_plane[self.me] = self.late[...]
        for device in self.mates:
            self.push(self.late, self.late_plane.at[self.me], 3, device)

    def late_along(self):
        self.wait(self.late_plane.at[pl.ds(0, self.n - 1)], (self.send.at[3], self.recv.at[3]))
        self.late_line[self.z] = self.added(self.late_plane)
        for device in self.others:
            self.push(self.late_line.at[self.z], self.late_line.at[self.z], 4, device)

    def close(self):
        self.wait(self.late_line.at[pl.ds(0, self.nz - 1)], (self.send.at[4], self.recv.at[4]))
        self.wait(self.plane.at[pl.ds(0, self.n - 1)], (self.send.at[2], self.recv.at[2]))
        return self.added(self.late_line)

    def added(self, ref):
        total = ref[0]
        for at in range(1, ref.shape[0]):
            total = total + ref[at]
        return total


def backward_kernel(layers, sizes, *refs):
    cot, valid, gain, squares = refs[:4]
    qkv, pt, slope, n1, n2, r1, r2, wqkv, wout, wup, wdown = [
        [ref.at[l] for l in range(layers)] for ref in refs[4:15]
    ]
    q, k, v = [[ref.at[part] for ref in qkv] for part in range(3)]
    backward_body(
        layers, sizes, cot, valid, gain, squares, q, k, v, pt, slope, n1, n2, r1, r2, wqkv, wout, wup, wdown, *refs[15:]
    )


def backward_body(
    layers, sizes, cot, valid, gain, squares, q, k, v, pt, slope, n1, n2, r1, r2, wqkv, wout, wup, wdown,
    dh_out, summed,
    e_buf, x_buf, z_buf, du_buf, dp_buf, do_buf, cot_buf,
    q_buf, k_buf, v_buf, pt_buf, sl_buf, n1_buf, n2_buf,
    ring_a, ring_b, ring_c, sem_a, sem_b, sem_c, sem_in, sem_out, *rest,
):
    slots, width = e_buf.shape
    ff = du_buf.shape[1]
    heads = pt[0].shape[0]
    hd = width // heads
    half = slots // 2
    scale = hd ** (-0.5)
    order = list(reversed(range(layers)))
    fused = len(rest) > 0
    grads = rest[0] if fused else summed
    team = None
    if fused:
        team = Total(Fabric(sizes), rest[1:])
        team.greet()

    sources = (n2, slope, n1, q, k, v, pt)
    buffers = (n2_buf, sl_buf, n1_buf, q_buf, k_buf, v_buf, pt_buf)

    def load(which, layer, par):
        return pltpu.make_async_copy(sources[which][layer], buffers[which].at[par], sem_in.at[par, which])

    cot_copy = pltpu.make_async_copy(cot, cot_buf, sem_out.at[0])
    cot_copy.start()
    load(0, order[0], 0).start()
    seg_a = []
    seg_b = []
    seg_c = []
    for l in order:
        seg_a += [(wdown[l], ff // ring_a.shape[1]), (wout[l], width // ring_a.shape[1])]
        seg_b += [(wup[l], width // ring_b.shape[1])]
        seg_c += [(wqkv[l], width // ring_c.shape[1])]
    ra, rb, rc = Ring(ring_a, sem_a, seg_a), Ring(ring_b, sem_b, seg_b), Ring(ring_c, sem_c, seg_c)
    ra.prime()
    load(1, order[0], 0).start()
    rb.prime()
    for which in range(2, 7):
        load(which, order[0], 0).start()
    rc.prime()
    for which in range(7):
        for step, l in enumerate(order[1:], 1):
            if step < 2:
                load(which, l, step).start()

    chunk = 32
    cot_copy.wait()

    def mask_cot(c, carry):
        rows = pl.ds(pl.multiple_of(c * chunk, chunk), chunk)
        e_buf[rows, :] = cot_buf[rows, :].astype(F32) * valid[rows, :]
        return carry

    lax.fori_loop(0, slots // chunk, mask_cot, 0)

    def norm_back(src, dst, gain_row, n_ref, r_ref):
        def step(c, carry):
            s_in, s_out = carry
            rows = pl.ds(pl.multiple_of(c * chunk, chunk), chunk)
            g = src[rows, :]
            n = n_ref[rows, :].astype(F32)
            ge = g * gain_row
            m1 = jnp.mean(ge, axis=1, keepdims=True)
            m2 = jnp.mean(ge * n, axis=1, keepdims=True)
            dz = r_ref[rows, :] * (ge - m1 - n * m2)
            dst[rows, :] = dz
            z_buf[rows, :] = dz.astype(BF)
            return (s_in + fold8(g), s_out + fold8(dz))

        zero = jnp.zeros((8, width), F32)
        s_in, s_out = lax.fori_loop(0, slots // chunk, step, (zero, zero))
        return jnp.sum(s_in, axis=0, keepdims=True), jnp.sum(s_out, axis=0, keepdims=True)

    for l in range(layers):
        grads[l, 10:13, :] = squares[3 * l : 3 * l + 3, :]
        grads[l, 13:14, :] = squares[3 * layers : 3 * layers + 1, :]
        grads[l, 14:16, :] = jnp.zeros((2, width), F32)
    if fused:
        grads[order[-1], 0:2, :] = jnp.zeros((2, width), F32)

    for step, l in enumerate(order):
        par = step % 2
        last = step == layers - 1
        early = fused and last

        load(0, l, par).wait()
        s_in, s_out = norm_back(e_buf, x_buf, gain[l, 1:2, :], n2_buf.at[par], r2[l])
        grads[l, 4:5, :] = s_in
        grads[l, 9:10, :] = s_out

        load(1, l, par).wait()
        wide = ring_a.shape[1]

        def down_body(j, w):
            cols = pl.ds(pl.multiple_of(j * wide, wide), wide)
            du = nt(z_buf[...], w) * sl_buf[par, :, cols].astype(F32)
            du_buf[:, cols] = du.astype(BF)
            part = jnp.sum(fold8(du), axis=0, keepdims=True)
            per = width // wide
            grads[l, pl.ds(5 + j // per, 1), pl.ds(pl.multiple_of(lax.rem(j, per) * wide, wide), wide)] = part

        ra.run(ff // wide, down_body)
        nb = ring_b.shape[1]

        def up_body(j, w):
            cols = pl.ds(pl.multiple_of(j * nb, nb), nb)
            x_buf[:, cols] = x_buf[:, cols] + nt(du_buf[...], w)

        rb.run(width // nb, up_body)

        load(2, l, par).wait()
        s_in, s_out = norm_back(x_buf, x_buf, gain[l, 0:1, :], n1_buf.at[par], r1[l])
        grads[l, 3:4, :] = s_in
        grads[l, 2:3, :] = s_out

        def out_body(j, w):
            cols = pl.ds(pl.multiple_of(j * wide, wide), wide)
            do_buf[:, cols] = nt(z_buf[...], w).astype(BF)

        ra.run(width // wide, out_body)

        for which in range(3, 7):
            load(which, l, par).wait()
        lane = lax.broadcasted_iota(jnp.int32, (1, 2 * hd), 1)
        sides = (lane < hd, lane >= hd)

        def pair(hp, carry):
            cols = pl.ds(pl.multiple_of(hp * 2 * hd, 2 * hd), 2 * hd)
            sum_q = jnp.zeros((8, 2 * hd), F32)
            sum_v = jnp.zeros((8, 2 * hd), F32)
            for b in range(2):
                rows = pl.ds(b * half, half)
                q2, k2, v2, do2 = (r[rows, cols] for r in (q_buf.at[par], k_buf.at[par], v_buf.at[par], do_buf))
                dq = dk = dv = None
                for side in range(2):
                    keep = sides[side]
                    zero = jnp.zeros_like(q2)
                    pb = pt_buf[par, 2 * hp + side, b]
                    dpt = nt(jnp.where(keep, v2, zero), do2)
                    p32 = pb.astype(F32)
                    t = p32 * dpt
                    inner = jnp.sum(fold8(t), axis=0, keepdims=True)
                    ds = (t - p32 * inner).astype(BF)
                    a_v = nn(pb, jnp.where(keep, do2, zero))
                    a_k = nn(ds, jnp.where(keep, q2, zero))
                    a_q = tn(ds, jnp.where(keep, k2, zero))
                    dv = a_v if dv is None else dv + a_v
                    dk = a_k if dk is None else dk + a_k
                    dq = a_q if dq is None else dq + a_q
                dq = dq * scale
                dk = dk * scale
                dp_buf[rows, cols] = dq.astype(BF)
                dp_buf[rows, pl.ds(pl.multiple_of(width + hp * 2 * hd, 2 * hd), 2 * hd)] = dk.astype(BF)
                dp_buf[rows, pl.ds(pl.multiple_of(2 * width + hp * 2 * hd, 2 * hd), 2 * hd)] = dv.astype(BF)
                sum_q = sum_q + fold8(dq)
                sum_v = sum_v + fold8(dv)
            terms = team.late if early else grads.at[l]
            terms[0:1, cols] = jnp.sum(sum_q, axis=0, keepdims=True)
            terms[1:2, cols] = jnp.sum(sum_v, axis=0, keepdims=True)
            return carry

        if early:
            team.met()
            team.spread(grads)
            lax.fori_loop(0, 3, pair, 0)
            team.along()
            lax.fori_loop(3, 6, pair, 0)
            team.back(summed)
            lax.fori_loop(6, heads // 2, pair, 0)
            team.late_spread()
        else:
            lax.fori_loop(0, heads // 2, pair, 0)
        nc = ring_c.shape[1]

        def qkv_body(j, w):
            cols = pl.ds(pl.multiple_of(j * nc, nc), nc)
            e_buf[:, cols] = x_buf[:, cols] + nt(dp_buf[...], w)
            if last:
                pltpu.make_async_copy(e_buf.at[:, cols], dh_out.at[:, cols], sem_out.at[0]).start()

        rc.run(width // nc // 2, qkv_body)
        if early:
            team.late_along()
        rc.run(width // nc // 2, qkv_body, width // nc // 2)
        for which in range(7):
            if step + 2 < layers:
                load(which, order[step + 2], par).start()

    if fused:
        summed[order[-1], 0:2, :] = team.close()
    for j in range(width // nc):
        cols = pl.ds(j * nc, nc)
        pltpu.make_async_copy(e_buf.at[:, cols], dh_out.at[:, cols], sem_out.at[0]).wait()


def backward(sizes, cot, valid, gain, squares, kept):
    slots, width = cot.shape
    layers, heads = kept[1].shape[:2]
    ff = kept[2].shape[2]
    half = slots // 2
    hbm = pl.BlockSpec(memory_space=pl.ANY)
    vm = pl.BlockSpec(memory_space=pltpu.VMEM)
    ta, tb, tc = min(512, width), min(256, width), min(256, width)
    team = []
    params = {}
    if sizes == KERNEL_MESH:
        plane, line = 2 * sizes[0] * sizes[1], sizes[2]
        team = [
            pltpu.VMEM((layers, 16, width), F32),
            pltpu.VMEM((plane, layers, 16, width // plane), F32),
            pltpu.VMEM((line, layers, 16, width // plane), F32),
            pltpu.VMEM((layers, 16, width // plane), F32),
            pltpu.VMEM((2, width), F32),
            pltpu.VMEM((plane, 2, width), F32),
            pltpu.VMEM((line, 2, width), F32),
            pltpu.SemaphoreType.DMA((5,)),
            pltpu.SemaphoreType.DMA((5,)),
        ]
        params = dict(collective_id=1, has_side_effects=True)
    return pl.pallas_call(
        functools.partial(backward_kernel, layers, sizes),
        out_shape=(
            jax.ShapeDtypeStruct((slots, width), F32),
            jax.ShapeDtypeStruct((layers, 16, width), F32),
        ),
        in_specs=[hbm, vm, vm, vm] + [hbm] * 5 + [vm] * 2 + [hbm] * 4,
        out_specs=(hbm, vm),
        scratch_shapes=[
            pltpu.VMEM((slots, width), F32),
            pltpu.VMEM((slots, width), F32),
            pltpu.VMEM((slots, width), BF),
            pltpu.VMEM((slots, ff), BF),
            pltpu.VMEM((slots, 3 * width), BF),
            pltpu.VMEM((slots, width), BF),
            pltpu.VMEM((slots, width), BF),
        ]
        + [pltpu.VMEM((2, slots, width), BF)] * 3
        + [
            pltpu.VMEM((2, heads, 2, half, half), BF),
            pltpu.VMEM((2, slots, ff), BF),
            pltpu.VMEM((2, slots, width), BF),
            pltpu.VMEM((2, slots, width), BF),
            pltpu.VMEM((3, ta, width), BF),
            pltpu.VMEM((2, tb, ff), BF),
            pltpu.VMEM((2, tc, 3 * width), BF),
            pltpu.SemaphoreType.DMA((3,)),
            pltpu.SemaphoreType.DMA((2,)),
            pltpu.SemaphoreType.DMA((2,)),
            pltpu.SemaphoreType.DMA((2, 7)),
            pltpu.SemaphoreType.DMA((1,)),
        ]
        + team,
        compiler_params=pltpu.CompilerParams(vmem_limit_bytes=67000000, **params),
        name="backward",
    )(cot, valid, gain, squares, *kept)


class Relay:
    def __init__(self, fabric, kinds, per, count, sems):
        self.fab, self.kinds, self.per, self.count = fabric, kinds, per, count
        self.send, self.recv = sems
        at = fabric.at
        self.pair = lax.div(at["z"], 2) * 2
        self.other = 2 - self.pair
        self.mate = self.pair + 1 - lax.rem(at["z"], 2)
        self.inner = jnp.logical_or(at["z"] == 1, at["z"] == 2)

    def wait(self, sem, blocks):
        _, _, _, full, rows, cols = self.kinds[0]
        part = full.at[0, pl.ds(0, blocks * rows), pl.ds(0, cols // 2)]
        pltpu.make_async_copy(part, part, sem).wait()

    def each(self, t, act):
        l = lax.div(t, self.per)
        j = t - l * self.per
        for first, number, own, full, rows, cols in self.kinds:

            @pl.when(jnp.logical_and(j >= first, j < first + number))
            def _(first=first, own=own, full=full, rows=rows, cols=cols):
                for piece in range(2):
                    col = pl.multiple_of((j - first) * cols + piece * (cols // 2), cols // 2)
                    act(l, own, full, rows, pl.ds(col, cols // 2), piece)

    def push(self, t, piece, sem, device, src, dst):
        pltpu.make_async_remote_copy(
            src_ref=src,
            dst_ref=dst,
            send_sem=self.send.at[2 * t + piece, sem],
            recv_sem=self.recv.at[2 * t + piece, sem],
            device_id=device,
            device_id_type=pl.DeviceIdType.MESH,
        ).start()

    def stage(self, s, t):
        fab = self.fab
        at = fab.at
        partner = fab.device(c=1 - at["c"])

        @pl.when(jnp.logical_and(t >= 0, t < self.count))
        def _():
            for piece in range(2):
                if s == 1:
                    self.wait(self.recv.at[2 * t + piece, 0], 1)
                elif s == 2:
                    self.wait(self.recv.at[2 * t + piece, 1], 2)
                elif s == 3:
                    pl.when(self.inner)(lambda piece=piece: self.wait(self.recv.at[2 * t + piece, 2], 4))
                elif s == 4:
                    pl.when(jnp.logical_not(self.inner))(
                        lambda piece=piece: self.wait(self.recv.at[2 * t + piece, 2], 4)
                    )
                elif s == 5:
                    self.wait(self.recv.at[2 * t + piece, 3], 8)

            def act(l, own, full, rows, cols, piece):
                u, v = (("x", "y"), ("y", "x"))[piece]

                def view(first, blocks):
                    return full.at[l, pl.ds(pl.multiple_of(first * rows, rows), blocks * rows), cols]

                def out(sem, device, runs):
                    for first, blocks in runs:
                        self.push(t, piece, sem, device, view(first, blocks), view(first, blocks))

                far = [(fab.block(**{u: each, "z": self.other}), 2) for each in range(2)]
                if s == 0:
                    mine = view(fab.block(), 1)
                    self.push(t, piece, 0, fab.device(z=self.mate), own.at[l, :, cols], mine)
                    self.push(t, piece, 4, partner, own.at[l, :, cols], mine)
                elif s == 1:
                    out(1, fab.device(**{u: 1 - at[u]}), [(fab.block(z=self.pair), 2)])
                    out(4, partner, [(fab.block(z=self.mate), 1)])
                elif s == 2:
                    near = [(fab.block(**{u: each, "z": self.pair}), 2) for each in range(2)]
                    pl.when(self.inner)(lambda: out(2, fab.device(z=3 - at["z"]), near))
                    out(4, partner, [(fab.block(**{u: 1 - at[u], "z": self.pair}), 2)])
                elif s == 3:

                    @pl.when(self.inner)
                    def _():
                        out(2, fab.device(z=self.mate), far)
                        out(4, partner, far)

                elif s == 4:
                    out(3, fab.device(**{v: 1 - at[v]}), [(fab.block(**{u: each, "z": 0}), 4) for each in range(2)])
                    pl.when(jnp.logical_not(self.inner))(lambda: out(4, partner, far))
                else:
                    out(4, partner, [(fab.block(**{v: 1 - at[v], u: each, "z": 0}), 4) for each in range(2)])

            self.each(t, act)

    def finish(self, t):
        for piece in range(2):
            self.wait(self.recv.at[2 * t + piece, 4], 16)

    def drain(self, t):
        for piece in range(2):
            for sem, blocks in ((0, 1), (1, 2), (3, 8), (4, 16)):
                self.wait(self.send.at[2 * t + piece, sem], blocks)
            pl.when(self.inner)(lambda piece=piece: self.wait(self.send.at[2 * t + piece, 2], 8))


LEADS = (12, 10, 8, 6, 4, 2)


def forward_kernel(layers, sizes, *refs):
    (tok, vcol, vrow, gain, b_qv, b_out, b_ln, b_up, b_down, s_qkv, s_out, s_up, s_down) = refs[:13]
    (act, squares, qkv_o, pt_o, sl_o, n1_o, n2_o, r1_o, r2_o, f_qkv, f_out, f_up, f_down) = refs[13:26]
    (
        h_buf, hb_buf, qkv_buf, mix_buf, gu_buf, f_buf, pt_buf, sl_buf, n_buf,
        ring_w, ring_t, own_qkv, own_out, own_up, own_down,
        sem_send, sem_recv, sem_own, sem_ring, sem_save,
    ) = refs[26:]
    slots, width = tok.shape
    ff = gu_buf.shape[1]
    heads = pt_buf.shape[0]
    hd = width // heads
    half = slots // 2
    scale = hd ** (-0.5)
    tall = ring_t.shape[2]
    fab = Fabric(sizes)

    shards = ((s_qkv, own_qkv, f_qkv), (s_out, own_out, f_out), (s_up, own_up, f_up), (s_down, own_down, f_down))
    for at, (src, buf, _) in enumerate(shards):
        pltpu.make_async_copy(src, buf, sem_own.at[at]).start()
    barrier = pltpu.get_barrier_semaphore()
    around = [fab.device(**{axis: peer}) for axis in ("z", "x", "y", "c") for peer in fab.peers(axis)]
    for device in around:
        pl.semaphore_signal(barrier, inc=1, device_id=device, device_id_type=pl.DeviceIdType.MESH)
    pl.semaphore_wait(barrier, len(around))

    ups, downs = ff // width, width // tall
    kinds = (
        (0, 3, s_qkv, f_qkv, s_qkv.shape[1], width),
        (3, 1, s_out, f_out, s_out.shape[1], width),
        (4, ups, s_up, f_up, s_up.shape[1], width),
        (4 + ups, downs, s_down, f_down, s_down.shape[1], tall),
    )
    per = 4 + ups + downs
    total = layers * per
    relay = Relay(fab, kinds, per, total, (sem_send, sem_recv))

    def save(src, dst, key):
        pltpu.make_async_copy(src, dst, sem_save.at[key]).start()

    def free(src, dst, key, when):
        pl.when(when)(lambda: pltpu.make_async_copy(src, dst, sem_save.at[key]).wait())

    chunk = 32
    steps = slots // chunk

    def rows_of(c):
        return pl.ds(pl.multiple_of(c * chunk, chunk), chunk)

    def tiles(w, lhs, count, body, tile=256):
        def step(j, carry):
            cols = pl.ds(pl.multiple_of(j * tile, tile), tile)
            body(cols, nn(lhs[...], w[:, cols]), j * tile)
            return carry

        lax.fori_loop(0, count // tile, step, 0)

    def norm(l, which, bias_row, base, branch, n_dst, r_dst):
        zero = jnp.zeros((8, width), F32)
        gain_row = gain[l, which : which + 1, :]
        shift_row = b_ln[l, which : which + 1, :]

        def step(c, carry):
            s_h, s_a = carry
            rows = rows_of(c)
            a = branch[rows, :] + bias_row
            h = base[rows, :]
            z = h + a
            mean = jnp.mean(z, axis=1, keepdims=True)
            centred = z - mean
            var = jnp.mean(centred * centred, axis=1, keepdims=True)
            inv = lax.rsqrt(var + 1e-06)
            n = centred * inv
            y = n * gain_row + shift_row
            base[rows, :] = y
            hb_buf[rows, :] = y.astype(BF)
            n_dst[rows, :] = n.astype(BF)
            r_dst[rows, :] = inv
            ok = vcol[rows, :]
            return s_h + fold8(ok * h * h), s_a + fold8(ok * a * a)

        return lax.fori_loop(0, steps, step, (zero, zero))

    def attention():
        lane = lax.broadcasted_iota(jnp.int32, (1, 2 * hd), 1)
        sides = (lane < hd, lane >= hd)

        def pair(hp, carry):
            cols = pl.ds(pl.multiple_of(hp * 2 * hd, 2 * hd), 2 * hd)
            for b in range(2):
                rows = pl.ds(b * half, half)
                q2, k2, v2 = qkv_buf[0, rows, cols], qkv_buf[1, rows, cols], qkv_buf[2, rows, cols]
                mixed = None
                for side in range(2):
                    keep = sides[side]
                    zero = jnp.zeros_like(q2)
                    st = nt(jnp.where(keep, k2, zero), q2) * scale
                    if b == 1:
                        st = jnp.where(vcol[rows, :] == vrow[:, rows], st, -1e30)
                    top = jnp.max(st, axis=0, keepdims=True)
                    ex = jnp.exp(st - top)
                    p = (ex * (1.0 / jnp.sum(ex, axis=0, keepdims=True))).astype(BF)
                    pt_buf[2 * hp + side, b] = p
                    o = tn(p, jnp.where(keep, v2, zero))
                    mixed = o if mixed is None else mixed + o
                mix_buf[rows, cols] = mixed.astype(BF)
            return carry

        lax.fori_loop(0, heads // 2, pair, 0)

    def compute(t):
        l = lax.div(t, per)
        j = t - l * per
        slot = lax.rem(t, 2)
        later = l > 0

        @pl.when(j < 3)
        def _():
            free(qkv_buf.at[j], qkv_o.at[0, j], j, later)
            keep = (j != 1).astype(F32)

            def body(cols, t, first):
                bias = b_qv[l, pl.ds(lax.div(j, 2), 1), cols] * keep
                qkv_buf[j, :, cols] = (t + bias).astype(BF)

            tiles(ring_w.at[slot], hb_buf, width, body)
            save(qkv_buf.at[j], qkv_o.at[l, j], j)

            @pl.when(j == 2)
            def _():
                free(pt_buf, pt_o.at[0], 3, later)
                attention()
                save(pt_buf, pt_o.at[l], 3)

        @pl.when(j == 3)
        def _():
            def body(cols, t, first):
                f_buf[:, cols] = t

            tiles(ring_w.at[slot], mix_buf, width, body)
            free(n_buf.at[0], n1_o.at[0], 4, later)
            s_h, s_a = norm(l, 0, b_out[pl.ds(l, 1), :], h_buf, f_buf, n_buf.at[0], r1_o.at[l])
            squares[pl.ds(3 * l, 1), :] = jnp.sum(s_h, axis=0, keepdims=True)
            squares[pl.ds(3 * l + 1, 1), :] = jnp.sum(s_a, axis=0, keepdims=True)
            save(n_buf.at[0], n1_o.at[l], 4)

        @pl.when(jnp.logical_and(j >= 4, j < 4 + ups))
        def _():
            part = j - 4
            par = lax.rem(part, 2)
            start = pl.multiple_of(part * width, width)
            free(sl_buf.at[par], sl_o.at[0, :, pl.ds(0, width)], 6 + par, jnp.logical_or(later, part >= 2))

            def body(cols, t, first):
                wide = pl.ds(pl.multiple_of(part * width + first, 256), 256)
                u = t + b_up[pl.ds(l, 1), wide]
                phi = 0.5 * (1.0 + lax.erf(u * 0.7071067811865476))
                sl_buf[par, :, cols] = (phi + u * (jnp.exp(-0.5 * u * u) * 0.3989422804014327)).astype(BF)
                gu_buf[:, wide] = (u * phi).astype(BF)

            tiles(ring_w.at[slot], hb_buf, width, body)
            save(sl_buf.at[par], sl_o.at[l, :, pl.ds(start, width)], 6 + par)

        @pl.when(j >= 4 + ups)
        def _():
            part = j - 4 - ups
            f_buf[:, pl.ds(pl.multiple_of(part * tall, tall), tall)] = nn(gu_buf[...], ring_t[slot])

            @pl.when(part == downs - 1)
            def _():
                free(n_buf.at[1], n2_o.at[0], 5, later)
                _, s_f = norm(l, 1, b_down[pl.ds(l, 1), :], h_buf, f_buf, n_buf.at[1], r2_o.at[l])
                squares[pl.ds(3 * l + 2, 1), :] = jnp.sum(s_f, axis=0, keepdims=True)
                save(n_buf.at[1], n2_o.at[l], 5)

    def ring_start(t):
        l = lax.div(t, per)
        j = t - l * per
        slot = lax.rem(t, 2)
        for first, number, _, full, _, cols in kinds:
            buf = ring_t if cols == tall else ring_w

            @pl.when(jnp.logical_and(j >= first, j < first + number))
            def _(first=first, full=full, cols=cols, buf=buf):
                src = full.at[l, :, pl.ds(pl.multiple_of((j - first) * cols, cols), cols)]
                pltpu.make_async_copy(src, buf.at[slot], sem_ring.at[slot]).start()

    def ring_wait(t):
        slot = lax.rem(t, 2)
        pltpu.make_async_copy(f_out.at[0], ring_w.at[slot], sem_ring.at[slot]).wait()

    early = LEADS[0] - LEADS[1]
    for t in range(early):
        relay.stage(0, jnp.int32(t))
    for at, (src, buf, _) in enumerate(shards):
        pltpu.make_async_copy(src, buf, sem_own.at[at]).wait()
    placed = []
    for at, (_, buf, full) in enumerate(shards):
        rows = buf.shape[1]
        for l in range(layers):
            dst = full.at[l, pl.ds(pl.multiple_of(fab.block() * rows, rows), rows)]
            placed.append(pltpu.make_async_copy(buf.at[l], dst, sem_own.at[4 + at * layers + l]))
            placed[-1].start()

    def widen(c, carry):
        rows = rows_of(c)
        h_buf[rows, :] = tok[rows, :].astype(F32)
        hb_buf[rows, :] = tok[rows, :]
        return carry

    lax.fori_loop(0, steps, widen, 0)
    for copy in placed:
        copy.wait()

    def step(i, carry):
        at = i - LEADS[1]
        for s, lead in enumerate(LEADS):
            relay.stage(s, at + lead)
        pl.when(jnp.logical_and(at >= 1, at <= total))(lambda: ring_wait(at - 1))

        @pl.when(jnp.logical_and(at >= 0, at < total))
        def _():
            relay.finish(at)
            ring_start(at)

        pl.when(at >= 1)(lambda: relay.drain(at - 1))
        pl.when(at >= 1)(lambda: compute(at - 1))
        return carry

    lax.fori_loop(0, total + 1 + LEADS[1], step, 0)
    pltpu.make_async_copy(hb_buf, act, sem_own.at[0]).start()
    here = jnp.sum(vcol[...], axis=0, keepdims=True)
    squares[3 * layers :, :] = jnp.broadcast_to(here, (squares.shape[0] - 3 * layers, width))
    for part in range(3):
        free(qkv_buf.at[part], qkv_o.at[0, part], part, True)
    free(pt_buf, pt_o.at[0], 3, True)
    free(n_buf.at[0], n1_o.at[0], 4, True)
    free(n_buf.at[1], n2_o.at[0], 5, True)
    for par in range(2):
        free(sl_buf.at[par], sl_o.at[0, :, pl.ds(0, width)], 6 + par, True)
    pltpu.make_async_copy(hb_buf, act, sem_own.at[0]).wait()


def forward(sizes, tokens, vcol, vrow, gain, b_qv, b_out, b_ln, b_up, b_down, s_qkv, s_out, s_up, s_down):
    slots, width = tokens.shape
    layers = s_qkv.shape[0]
    ff = s_up.shape[2]
    half = slots // 2
    tall = width * width // ff
    hbm = pl.BlockSpec(memory_space=pl.ANY)
    vm = pl.BlockSpec(memory_space=pltpu.VMEM)
    chunks = layers * (4 + ff // width + width // tall)
    outs = [
        ((slots, width), BF, hbm),
        ((8, width), F32, vm),
        ((layers, 3, slots, width), BF, hbm),
        ((layers, HEADS, 2, half, half), BF, hbm),
        ((layers, slots, ff), BF, hbm),
        ((layers, slots, width), BF, hbm),
        ((layers, slots, width), BF, hbm),
        ((layers, slots, 1), F32, vm),
        ((layers, slots, 1), F32, vm),
        ((layers, width, 3 * width), BF, hbm),
        ((layers, width, width), BF, hbm),
        ((layers, width, ff), BF, hbm),
        ((layers, ff, width), BF, hbm),
    ]
    result = pl.pallas_call(
        functools.partial(forward_kernel, layers, sizes),
        out_shape=tuple(jax.ShapeDtypeStruct(shape, kind) for shape, kind, _ in outs),
        in_specs=[vm] * 9 + [hbm] * 4,
        out_specs=tuple(spec for _, _, spec in outs),
        scratch_shapes=[
            pltpu.VMEM((slots, width), F32),
            pltpu.VMEM((slots, width), BF),
            pltpu.VMEM((3, slots, width), BF),
            pltpu.VMEM((slots, width), BF),
            pltpu.VMEM((slots, ff), BF),
            pltpu.VMEM((slots, width), F32),
            pltpu.VMEM((HEADS, 2, half, half), BF),
            pltpu.VMEM((2, slots, width), BF),
            pltpu.VMEM((2, slots, width), BF),
            pltpu.VMEM((2, width, width), BF),
            pltpu.VMEM((2, ff, tall), BF),
            pltpu.VMEM(s_qkv.shape, BF),
            pltpu.VMEM(s_out.shape, BF),
            pltpu.VMEM(s_up.shape, BF),
            pltpu.VMEM(s_down.shape, BF),
            pltpu.SemaphoreType.DMA((2 * chunks, 5)),
            pltpu.SemaphoreType.DMA((2 * chunks, 5)),
            pltpu.SemaphoreType.DMA((4 + 4 * layers,)),
            pltpu.SemaphoreType.DMA((2,)),
            pltpu.SemaphoreType.DMA((8,)),
        ],
        compiler_params=pltpu.CompilerParams(vmem_limit_bytes=62 << 20, collective_id=0, has_side_effects=True),
        name="forward",
    )(tokens, vcol, vrow, gain, b_qv, b_out, b_ln, b_up, b_down, s_qkv, s_out, s_up, s_down)
    return result[0], result[1], list(result[2:])


def normalize(stream, gain_row, shift_row):
    mean_row = jnp.mean(stream, axis=-1, keepdims=True)
    centred = stream - mean_row
    variance = jnp.mean(centred * centred, axis=-1, keepdims=True)
    inv_std = lax.rsqrt(variance + 1e-06)
    normed = centred * inv_std
    return normed * gain_row + shift_row, normed, inv_std


def forward_apart(tokens, vcol, vrow, gain, b_qv, b_out, b_ln, b_up, b_down, *shards):
    slots, width = tokens.shape
    layers = b_out.shape[0]
    half = slots // 2
    hd = width // HEADS
    blocks = vcol.reshape(2, half)
    same = blocks[:, :, None] == blocks[:, None, :]
    stream = tokens.astype(F32)
    kept = []
    squares = []
    for l in range(layers):
        mats = [lax.all_gather(w[l], AXES, axis=0, tiled=True) for w in shards]
        projected = nn(stream.astype(BF), mats[0])
        q = (projected[:, :width] + b_qv[l, 0]).astype(BF)
        k = projected[:, width : 2 * width].astype(BF)
        v = (projected[:, 2 * width :] + b_qv[l, 1]).astype(BF)
        q4, k4, v4 = (a.reshape(2, half, HEADS, hd) for a in (q, k, v))
        st = jnp.einsum("bqhd,bkhd->hbkq", q4, k4, preferred_element_type=F32) * hd ** (-0.5)
        st = jnp.where(same[None], st, -1e30)
        ex = jnp.exp(st - jnp.max(st, axis=2, keepdims=True))
        pt = (ex / jnp.sum(ex, axis=2, keepdims=True)).astype(BF)
        mixed = jnp.einsum("hbkq,bkhd->bqhd", pt, v4, preferred_element_type=F32).reshape(slots, width).astype(BF)
        branch = nn(mixed, mats[1]) + b_out[l]
        x1, n1, r1 = normalize(stream + branch, gain[l, 0], b_ln[l, 0])
        u = nn(x1.astype(BF), mats[2]) + b_up[l]
        phi = 0.5 * (1.0 + lax.erf(u * 0.7071067811865476))
        slope = (phi + u * (jnp.exp(-0.5 * u * u) * 0.3989422804014327)).astype(BF)
        ffn = nn((u * phi).astype(BF), mats[3]) + b_down[l]
        nxt, n2, r2 = normalize(x1 + ffn, gain[l, 1], b_ln[l, 1])
        squares += [jnp.sum(vcol * a * a, axis=0) for a in (stream, branch, ffn)]
        kept.append((jnp.stack([q, k, v]), pt, slope, n1.astype(BF), n2.astype(BF), r1, r2, *mats))
        stream = nxt
    here = jnp.broadcast_to(jnp.sum(vcol), (width,))
    return stream.astype(BF), jnp.stack(squares + [here] * (8 - 3 * layers)), [jnp.stack(a) for a in zip(*kept)]


def local(
    sizes, tokens, lengths, w_qkv, w_out, w_up, w_down, ln_gain, bias_qv, bias_out, ln_bias, bias_up, bias_down, cotangent
):
    slots, width = tokens.shape
    layers = w_qkv.shape[0]
    half = slots // 2
    first, second = lengths[0, 0], lengths[0, 1]
    shift = jnp.where(first == half, 0, first)
    place = lax.rem(jnp.arange(slots, dtype=jnp.int32) + shift, slots)
    valid = (place < first + second).astype(F32)

    def turn(a, by):
        return lax.dynamic_slice_in_dim(jnp.concatenate([a, a], axis=0), by, slots, axis=0)

    run = functools.partial(forward, sizes) if sizes == KERNEL_MESH else forward_apart
    act, squares, kept = run(
        turn(tokens, shift), valid[:, None], valid[None, :], ln_gain, bias_qv, bias_out, ln_bias, bias_up, bias_down,
        w_qkv, w_out, w_up, w_down,
    )
    dh, whole = backward(sizes, turn(cotangent, shift), valid[:, None], ln_gain, squares, kept)
    if sizes != KERNEL_MESH:
        whole = lax.psum(whole, AXES)
    back = lax.rem(slots - shift, slots)
    return (
        turn(act, back),
        turn(dh, back),
        whole[:, 0:2],
        whole[:, 2],
        whole[:, 3:5],
        whole[:, 5:9].reshape(layers, -1),
        whole[:, 9],
        jnp.sqrt(jnp.sum(whole[:, 10:13], axis=2) / (whole[:, 13, 0:1] * width)),
    )


def solution(mesh):
    pairs = mesh.shape["dp"] // 2
    ny = next(n for n in range(math.isqrt(pairs), 0, -1) if pairs % n == 0)
    sizes = (ny, pairs // ny, mesh.shape["shard"])
    rows = P(AXES, None)
    weight = P(None, AXES, None)
    in_specs = (rows, rows, weight, weight, weight, weight, P(), P(), P(), P(), P(), P(), rows)
    out_specs = (rows, rows, P(), P(), P(), P(), P(), P())
    return jax.shard_map(
        functools.partial(local, sizes), mesh=mesh, in_specs=in_specs, out_specs=out_specs, check_vma=False
    )
```

```python
import functools
import math

import jax
import jax.numpy as jnp
from jax import lax
from jax.experimental import pallas as pl
from jax.experimental.pallas import tpu as pltpu
from jax.sharding import PartitionSpec as P

BF = jnp.bfloat16
F32 = jnp.float32
HEADS = 16
AXES = ("dp", "shard")
KERNEL_MESH = (2, 2, 4)


def nt(a, b):
    return lax.dot_general(a, b, (((1,), (1,)), ((), ())), preferred_element_type=F32)


def nn(a, b):
    return lax.dot_general(a, b, (((1,), (0,)), ((), ())), preferred_element_type=F32)


def tn(a, b):
    return lax.dot_general(a, b, (((0,), (0,)), ((), ())), preferred_element_type=F32)


def fold8(t):
    return jnp.sum(t.reshape(t.shape[0] // 8, 8, t.shape[1]), axis=0)


class Ring:
    def __init__(self, buf, sem, segments):
        self.buf, self.sem, self.segments = buf, sem, segments
        self.slots, self.rows = buf.shape[0], buf.shape[1]
        self.base = 0

    def fetch(self, at):
        slot = lax.rem(at, self.slots)
        first = 0
        for ref, count in self.segments:
            if isinstance(at, int):
                if first <= at < first + count:
                    row = (at - first) * self.rows
                    pltpu.make_async_copy(ref.at[pl.ds(row, self.rows)], self.buf.at[slot], self.sem.at[slot]).start()
            else:

                @pl.when(jnp.logical_and(at >= first, at < first + count))
                def _(ref=ref, first=first):
                    row = pl.multiple_of((at - first) * self.rows, self.rows)
                    pltpu.make_async_copy(ref.at[pl.ds(row, self.rows)], self.buf.at[slot], self.sem.at[slot]).start()

            first += count

    def prime(self):
        for at in range(self.slots):
            self.fetch(at)

    def run(self, count, body, first=0):
        base = self.base

        def step(j, carry):
            at = base + j
            slot = lax.rem(at, self.slots)
            pltpu.make_async_copy(self.segments[0][0].at[pl.ds(0, self.rows)], self.buf.at[slot], self.sem.at[slot]).wait()
            body(first + j, self.buf[slot])
            self.fetch(at + self.slots)
            return carry

        lax.fori_loop(0, count, step, 0)
        self.base = base + count


class Fabric:
    def __init__(self, sizes):
        ny, nx, nz = sizes
        dp = lax.axis_index("dp")
        self.size = {"y": ny, "x": nx, "z": nz, "c": 2}
        self.at = {"z": lax.axis_index("shard"), "c": lax.rem(dp, 2), "x": lax.rem(dp // 2, nx), "y": dp // (2 * nx)}

    def device(self, **moved):
        at = {**self.at, **moved}
        return ((at["y"] * self.size["x"] + at["x"]) * 2 + at["c"], at["z"])

    def peers(self, axis):
        n = self.size[axis]
        return [lax.rem(self.at[axis] + step, n) for step in range(1, n)]

    def block(self, **moved):
        at = {**self.at, **moved}
        return ((at["y"] * self.size["x"] + at["x"]) * 2 + at["c"]) * self.size["z"] + at["z"]


class Total:
    def __init__(self, fabric, rest):
        (self.plane, self.line, self.mine, self.late, self.late_plane, self.late_line, self.send, self.recv) = rest
        self.fab = fabric
        self.me = lax.axis_index("dp")
        self.z = fabric.at["z"]
        self.n, self.nz = self.plane.shape[0], fabric.size["z"]
        self.mates = [(lax.rem(self.me + step, self.n), self.z) for step in range(1, self.n)]
        self.others = [(self.me, lax.rem(self.z + step, self.nz)) for step in range(1, self.nz)]

    def greet(self):
        barrier = pltpu.get_barrier_semaphore()
        for device in self.mates + self.others:
            pl.semaphore_signal(barrier, inc=1, device_id=device, device_id_type=pl.DeviceIdType.MESH)

    def met(self):
        pl.semaphore_wait(pltpu.get_barrier_semaphore(), len(self.mates) + len(self.others))

    def push(self, src, dst, sem, device):
        pltpu.make_async_remote_copy(
            src_ref=src,
            dst_ref=dst,
            send_sem=self.send.at[sem],
            recv_sem=self.recv.at[sem],
            device_id=device,
            device_id_type=pl.DeviceIdType.MESH,
        ).start()

    def wait(self, part, sems):
        for sem in sems:
            pltpu.make_async_copy(part, part, sem).wait()

    def share(self, ref, at):
        cols = ref.shape[2] // self.n
        return ref.at[:, :, pl.ds(pl.multiple_of(at * cols, cols), cols)]

    def spread(self, part):
        self.plane[self.me] = self.share(part, self.me)[...]
        for device in self.mates:
            self.push(self.share(part, device[0]), self.plane.at[self.me], 0, device)

    def along(self):
        self.wait(self.plane.at[pl.ds(0, self.n - 1)], (self.send.at[0], self.recv.at[0]))
        self.line[self.z] = self.added(self.plane)
        for device in self.others:
            self.push(self.line.at[self.z], self.line.at[self.z], 1, device)

    def back(self, out):
        self.wait(self.line.at[pl.ds(0, self.nz - 1)], (self.send.at[1], self.recv.at[1]))
        total = self.added(self.line)
        self.mine[...] = total
        self.share(out, self.me)[...] = total
        for device in self.mates:
            self.push(self.mine, self.share(out, self.me), 2, device)

    def late_spread(self):
        self.late_plane[self.me] = self.late[...]
        for device in self.mates:
            self.push(self.late, self.late_plane.at[self.me], 3, device)

    def late_along(self):
        self.wait(self.late_plane.at[pl.ds(0, self.n - 1)], (self.send.at[3], self.recv.at[3]))
        self.late_line[self.z] = self.added(self.late_plane)
        for device in self.others:
            self.push(self.late_line.at[self.z], self.late_line.at[self.z], 4, device)

    def close(self):
        self.wait(self.late_line.at[pl.ds(0, self.nz - 1)], (self.send.at[4], self.recv.at[4]))
        self.wait(self.plane.at[pl.ds(0, self.n - 1)], (self.send.at[2], self.recv.at[2]))
        return self.added(self.late_line)

    def added(self, ref):
        total = ref[0]
        for at in range(1, ref.shape[0]):
            total = total + ref[at]
        return total


def backward_kernel(layers, sizes, *refs):
    cot, gain, squares = refs[:3]
    qkv, pt, slope, n1, n2, r1, r2, wqkv, wout, wup, wdown = [
        [ref.at[l] for l in range(layers)] for ref in refs[3:14]
    ]
    q, k, v = [[ref.at[part] for ref in qkv] for part in range(3)]
    backward_body(
        layers, sizes, cot, gain, squares, q, k, v, pt, slope, n1, n2, r1, r2, wqkv, wout, wup, wdown, *refs[14:]
    )


def backward_body(
    layers, sizes, cot, gain, squares, q, k, v, pt, slope, n1, n2, r1, r2, wqkv, wout, wup, wdown,
    dh_out, summed,
    e_buf, x_buf, z_buf, du_buf, dp_buf, do_buf, cot_buf,
    q_buf, k_buf, v_buf, pt_buf, sl_buf, n1_buf, n2_buf,
    ring_a, ring_b, ring_c, sem_a, sem_b, sem_c, sem_in, sem_out, *rest,
):
    slots, width = e_buf.shape
    ff = du_buf.shape[1]
    heads = pt[0].shape[0]
    hd = width // heads
    half = slots // 2
    scale = hd ** (-0.5)
    order = list(reversed(range(layers)))
    fused = len(rest) > 0
    grads = rest[0] if fused else summed
    team = None
    if fused:
        team = Total(Fabric(sizes), rest[1:])
        team.greet()

    sources = (n2, slope, n1, q, k, v, pt)
    buffers = (n2_buf, sl_buf, n1_buf, q_buf, k_buf, v_buf, pt_buf)

    def load(which, layer, par):
        return pltpu.make_async_copy(sources[which][layer], buffers[which].at[par], sem_in.at[par, which])

    cot_copy = pltpu.make_async_copy(cot, cot_buf, sem_out.at[0])
    cot_copy.start()
    load(0, order[0], 0).start()
    seg_a = []
    seg_b = []
    seg_c = []
    for l in order:
        seg_a += [(wdown[l], ff // ring_a.shape[1]), (wout[l], width // ring_a.shape[1])]
        seg_b += [(wup[l], width // ring_b.shape[1])]
        seg_c += [(wqkv[l], width // ring_c.shape[1])]
    ra, rb, rc = Ring(ring_a, sem_a, seg_a), Ring(ring_b, sem_b, seg_b), Ring(ring_c, sem_c, seg_c)
    ra.prime()
    load(1, order[0], 0).start()
    rb.prime()
    for which in range(2, 7):
        load(which, order[0], 0).start()
    rc.prime()
    for which in range(7):
        for step, l in enumerate(order[1:], 1):
            if step < 2:
                load(which, l, step).start()

    chunk = 32
    cot_copy.wait()

    def widen(c, carry):
        rows = pl.ds(pl.multiple_of(c * chunk, chunk), chunk)
        e_buf[rows, :] = cot_buf[rows, :].astype(F32)
        return carry

    lax.fori_loop(0, slots // chunk, widen, 0)

    def norm_back(src, dst, gain_row, n_ref, r_ref):
        def step(c, carry):
            s_in, s_out = carry
            rows = pl.ds(pl.multiple_of(c * chunk, chunk), chunk)
            g = src[rows, :]
            n = n_ref[rows, :].astype(F32)
            ge = g * gain_row
            m1 = jnp.mean(ge, axis=1, keepdims=True)
            m2 = jnp.mean(ge * n, axis=1, keepdims=True)
            dz = r_ref[rows, :] * (ge - m1 - n * m2)
            dst[rows, :] = dz
            z_buf[rows, :] = dz.astype(BF)
            return (s_in + fold8(g), s_out + fold8(dz))

        zero = jnp.zeros((8, width), F32)
        s_in, s_out = lax.fori_loop(0, slots // chunk, step, (zero, zero))
        return jnp.sum(s_in, axis=0, keepdims=True), jnp.sum(s_out, axis=0, keepdims=True)

    for l in range(layers):
        grads[l, 10:13, :] = squares[3 * l : 3 * l + 3, :]
        grads[l, 13:14, :] = squares[3 * layers : 3 * layers + 1, :]
        grads[l, 14:16, :] = jnp.zeros((2, width), F32)
    if fused:
        grads[order[-1], 0:2, :] = jnp.zeros((2, width), F32)

    for step, l in enumerate(order):
        par = step % 2
        last = step == layers - 1
        early = fused and last

        load(0, l, par).wait()
        s_in, s_out = norm_back(e_buf, x_buf, gain[l, 1:2, :], n2_buf.at[par], r2[l])
        grads[l, 4:5, :] = s_in
        grads[l, 9:10, :] = s_out

        load(1, l, par).wait()
        wide = ring_a.shape[1]

        def down_body(j, w):
            cols = pl.ds(pl.multiple_of(j * wide, wide), wide)
            du = nt(z_buf[...], w) * sl_buf[par, :, cols].astype(F32)
            du_buf[:, cols] = du.astype(BF)
            part = jnp.sum(fold8(du), axis=0, keepdims=True)
            per = width // wide
            grads[l, pl.ds(5 + j // per, 1), pl.ds(pl.multiple_of(lax.rem(j, per) * wide, wide), wide)] = part

        ra.run(ff // wide, down_body)
        nb = ring_b.shape[1]

        def up_body(j, w):
            cols = pl.ds(pl.multiple_of(j * nb, nb), nb)
            x_buf[:, cols] = x_buf[:, cols] + nt(du_buf[...], w)

        rb.run(width // nb, up_body)

        load(2, l, par).wait()
        s_in, s_out = norm_back(x_buf, x_buf, gain[l, 0:1, :], n1_buf.at[par], r1[l])
        grads[l, 3:4, :] = s_in
        grads[l, 2:3, :] = s_out

        def out_body(j, w):
            cols = pl.ds(pl.multiple_of(j * wide, wide), wide)
            do_buf[:, cols] = nt(z_buf[...], w).astype(BF)

        ra.run(width // wide, out_body)

        for which in range(3, 7):
            load(which, l, par).wait()
        lane = lax.broadcasted_iota(jnp.int32, (1, 2 * hd), 1)
        sides = (lane < hd, lane >= hd)

        def pair(hp, carry):
            cols = pl.ds(pl.multiple_of(hp * 2 * hd, 2 * hd), 2 * hd)
            sum_q = jnp.zeros((8, 2 * hd), F32)
            sum_v = jnp.zeros((8, 2 * hd), F32)
            for b in range(2):
                rows = pl.ds(b * half, half)
                q2, k2, v2, do2 = (r[rows, cols] for r in (q_buf.at[par], k_buf.at[par], v_buf.at[par], do_buf))
                dq = dk = dv = None
                for side in range(2):
                    keep = sides[side]
                    zero = jnp.zeros_like(q2)
                    pb = pt_buf[par, 2 * hp + side, b]
                    dpt = nt(jnp.where(keep, v2, zero), do2)
                    p32 = pb.astype(F32)
                    t = p32 * dpt
                    inner = jnp.sum(fold8(t), axis=0, keepdims=True)
                    ds = (t - p32 * inner).astype(BF)
                    a_v = nn(pb, jnp.where(keep, do2, zero))
                    a_k = nn(ds, jnp.where(keep, q2, zero))
                    a_q = tn(ds, jnp.where(keep, k2, zero))
                    dv = a_v if dv is None else dv + a_v
                    dk = a_k if dk is None else dk + a_k
                    dq = a_q if dq is None else dq + a_q
                dq = dq * scale
                dk = dk * scale
                dp_buf[rows, cols] = dq.astype(BF)
                dp_buf[rows, pl.ds(pl.multiple_of(width + hp * 2 * hd, 2 * hd), 2 * hd)] = dk.astype(BF)
                dp_buf[rows, pl.ds(pl.multiple_of(2 * width + hp * 2 * hd, 2 * hd), 2 * hd)] = dv.astype(BF)
                sum_q = sum_q + fold8(dq)
                sum_v = sum_v + fold8(dv)
            terms = team.late if early else grads.at[l]
            terms[0:1, cols] = jnp.sum(sum_q, axis=0, keepdims=True)
            terms[1:2, cols] = jnp.sum(sum_v, axis=0, keepdims=True)
            return carry

        if early:
            team.met()
            team.spread(grads)
            lax.fori_loop(0, 3, pair, 0)
            team.along()
            lax.fori_loop(3, 6, pair, 0)
            team.back(summed)
            lax.fori_loop(6, heads // 2, pair, 0)
            team.late_spread()
        else:
            lax.fori_loop(0, heads // 2, pair, 0)
        nc = ring_c.shape[1]

        def qkv_body(j, w):
            cols = pl.ds(pl.multiple_of(j * nc, nc), nc)
            e_buf[:, cols] = x_buf[:, cols] + nt(dp_buf[...], w)
            if last:
                pltpu.make_async_copy(e_buf.at[:, cols], dh_out.at[:, cols], sem_out.at[0]).start()

        rc.run(width // nc // 2, qkv_body)
        if early:
            team.late_along()
        rc.run(width // nc // 2, qkv_body, width // nc // 2)
        for which in range(7):
            if step + 2 < layers:
                load(which, order[step + 2], par).start()

    if fused:
        summed[order[-1], 0:2, :] = team.close()
    for j in range(width // nc):
        cols = pl.ds(j * nc, nc)
        pltpu.make_async_copy(e_buf.at[:, cols], dh_out.at[:, cols], sem_out.at[0]).wait()


def backward(sizes, cot, gain, squares, kept):
    slots, width = cot.shape
    layers, heads = kept[1].shape[:2]
    ff = kept[2].shape[2]
    half = slots // 2
    hbm = pl.BlockSpec(memory_space=pl.ANY)
    vm = pl.BlockSpec(memory_space=pltpu.VMEM)
    ta, tb, tc = min(512, width), min(256, width), min(256, width)
    team = []
    params = {}
    if sizes == KERNEL_MESH:
        plane, line = 2 * sizes[0] * sizes[1], sizes[2]
        team = [
            pltpu.VMEM((layers, 16, width), F32),
            pltpu.VMEM((plane, layers, 16, width // plane), F32),
            pltpu.VMEM((line, layers, 16, width // plane), F32),
            pltpu.VMEM((layers, 16, width // plane), F32),
            pltpu.VMEM((2, width), F32),
            pltpu.VMEM((plane, 2, width), F32),
            pltpu.VMEM((line, 2, width), F32),
            pltpu.SemaphoreType.DMA((5,)),
            pltpu.SemaphoreType.DMA((5,)),
        ]
        params = dict(collective_id=1, has_side_effects=True)
    return pl.pallas_call(
        functools.partial(backward_kernel, layers, sizes),
        out_shape=(
            jax.ShapeDtypeStruct((slots, width), F32),
            jax.ShapeDtypeStruct((layers, 16, width), F32),
        ),
        in_specs=[hbm, vm, vm] + [hbm] * 5 + [vm] * 2 + [hbm] * 4,
        out_specs=(hbm, vm),
        scratch_shapes=[
            pltpu.VMEM((slots, width), F32),
            pltpu.VMEM((slots, width), F32),
            pltpu.VMEM((slots, width), BF),
            pltpu.VMEM((slots, ff), BF),
            pltpu.VMEM((slots, 3 * width), BF),
            pltpu.VMEM((slots, width), BF),
            pltpu.VMEM((slots, width), BF),
        ]
        + [pltpu.VMEM((2, slots, width), BF)] * 3
        + [
            pltpu.VMEM((2, heads, 2, half, half), BF),
            pltpu.VMEM((2, slots, ff), BF),
            pltpu.VMEM((2, slots, width), BF),
            pltpu.VMEM((2, slots, width), BF),
            pltpu.VMEM((3, ta, width), BF),
            pltpu.VMEM((2, tb, ff), BF),
            pltpu.VMEM((2, tc, 3 * width), BF),
            pltpu.SemaphoreType.DMA((3,)),
            pltpu.SemaphoreType.DMA((2,)),
            pltpu.SemaphoreType.DMA((2,)),
            pltpu.SemaphoreType.DMA((2, 7)),
            pltpu.SemaphoreType.DMA((1,)),
        ]
        + team,
        compiler_params=pltpu.CompilerParams(vmem_limit_bytes=67000000, **params),
        name="backward",
    )(cot, gain, squares, *kept)


class Relay:
    def __init__(self, fabric, kinds, per, count, sems):
        self.fab, self.kinds, self.per, self.count = fabric, kinds, per, count
        self.send, self.recv = sems
        at = fabric.at
        self.pair = lax.div(at["z"], 2) * 2
        self.other = 2 - self.pair
        self.mate = self.pair + 1 - lax.rem(at["z"], 2)
        self.inner = jnp.logical_or(at["z"] == 1, at["z"] == 2)

    def wait(self, sem, blocks):
        _, _, _, full, rows, cols = self.kinds[0]
        part = full.at[0, pl.ds(0, blocks * rows), pl.ds(0, cols // 2)]
        pltpu.make_async_copy(part, part, sem).wait()

    def each(self, t, act):
        l = lax.div(t, self.per)
        j = t - l * self.per
        for first, number, own, full, rows, cols in self.kinds:

            @pl.when(jnp.logical_and(j >= first, j < first + number))
            def _(first=first, own=own, full=full, rows=rows, cols=cols):
                for piece in range(2):
                    col = pl.multiple_of((j - first) * cols + piece * (cols // 2), cols // 2)
                    act(l, own, full, rows, pl.ds(col, cols // 2), piece)

    def push(self, t, piece, sem, device, src, dst):
        pltpu.make_async_remote_copy(
            src_ref=src,
            dst_ref=dst,
            send_sem=self.send.at[2 * t + piece, sem],
            recv_sem=self.recv.at[2 * t + piece, sem],
            device_id=device,
            device_id_type=pl.DeviceIdType.MESH,
        ).start()

    def stage(self, s, t):
        fab = self.fab
        at = fab.at
        partner = fab.device(c=1 - at["c"])

        @pl.when(jnp.logical_and(t >= 0, t < self.count))
        def _():
            for piece in range(2):
                if s == 1:
                    self.wait(self.recv.at[2 * t + piece, 0], 1)
                elif s == 2:
                    self.wait(self.recv.at[2 * t + piece, 1], 2)
                elif s == 3:
                    pl.when(self.inner)(lambda piece=piece: self.wait(self.recv.at[2 * t + piece, 2], 4))
                elif s == 4:
                    pl.when(jnp.logical_not(self.inner))(
                        lambda piece=piece: self.wait(self.recv.at[2 * t + piece, 2], 4)
                    )
                elif s == 5:
                    self.wait(self.recv.at[2 * t + piece, 3], 8)

            def act(l, own, full, rows, cols, piece):
                u, v = (("x", "y"), ("y", "x"))[piece]

                def view(first, blocks):
                    return full.at[l, pl.ds(pl.multiple_of(first * rows, rows), blocks * rows), cols]

                def out(sem, device, runs):
                    for first, blocks in runs:
                        self.push(t, piece, sem, device, view(first, blocks), view(first, blocks))

                far = [(fab.block(**{u: each, "z": self.other}), 2) for each in range(2)]
                if s == 0:
                    mine = view(fab.block(), 1)
                    self.push(t, piece, 0, fab.device(z=self.mate), own.at[l, :, cols], mine)
                    self.push(t, piece, 4, partner, own.at[l, :, cols], mine)
                elif s == 1:
                    out(1, fab.device(**{u: 1 - at[u]}), [(fab.block(z=self.pair), 2)])
                    out(4, partner, [(fab.block(z=self.mate), 1)])
                elif s == 2:
                    near = [(fab.block(**{u: each, "z": self.pair}), 2) for each in range(2)]
                    pl.when(self.inner)(lambda: out(2, fab.device(z=3 - at["z"]), near))
                    out(4, partner, [(fab.block(**{u: 1 - at[u], "z": self.pair}), 2)])
                elif s == 3:

                    @pl.when(self.inner)
                    def _():
                        out(2, fab.device(z=self.mate), far)
                        out(4, partner, far)

                elif s == 4:
                    out(3, fab.device(**{v: 1 - at[v]}), [(fab.block(**{u: each, "z": 0}), 4) for each in range(2)])
                    pl.when(jnp.logical_not(self.inner))(lambda: out(4, partner, far))
                else:
                    out(4, partner, [(fab.block(**{v: 1 - at[v], u: each, "z": 0}), 4) for each in range(2)])

            self.each(t, act)

    def finish(self, t):
        for piece in range(2):
            self.wait(self.recv.at[2 * t + piece, 4], 16)

    def drain(self, t):
        for piece in range(2):
            for sem, blocks in ((0, 1), (1, 2), (3, 8), (4, 16)):
                self.wait(self.send.at[2 * t + piece, sem], blocks)
            pl.when(self.inner)(lambda piece=piece: self.wait(self.send.at[2 * t + piece, 2], 8))


LEADS = (12, 10, 8, 6, 4, 2)


def forward_kernel(layers, sizes, *refs):
    (lens, tok, cot, gain, b_qv, b_out, b_ln, b_up, b_down, s_qkv, s_out, s_up, s_down) = refs[:13]
    (act, squares, back, cot_o, qkv_o, pt_o, sl_o, n1_o, n2_o, r1_o, r2_o, f_qkv, f_out, f_up, f_down) = refs[13:28]
    (
        h_buf, hb_buf, qkv_buf, mix_buf, gu_buf, f_buf, pt_buf, sl_buf, n_buf,
        ring_w, ring_t, own_qkv, own_out, own_up, own_down, turn, vcol, vrow,
        sem_send, sem_recv, sem_own, sem_ring, sem_save,
    ) = refs[28:]
    slots, width = tok.shape
    ff = gu_buf.shape[1]
    heads = pt_buf.shape[0]
    hd = width // heads
    half = slots // 2
    scale = hd ** (-0.5)
    tall = ring_t.shape[2]
    fab = Fabric(sizes)

    shards = ((s_qkv, own_qkv, f_qkv), (s_out, own_out, f_out), (s_up, own_up, f_up), (s_down, own_down, f_down))
    for at, (src, buf, _) in enumerate(shards):
        pltpu.make_async_copy(src, buf, sem_own.at[at]).start()
    pltpu.make_async_copy(cot, mix_buf, sem_save.at[3]).start()
    barrier = pltpu.get_barrier_semaphore()
    around = [fab.device(**{axis: peer}) for axis in ("z", "x", "y", "c") for peer in fab.peers(axis)]
    for device in around:
        pl.semaphore_signal(barrier, inc=1, device_id=device, device_id_type=pl.DeviceIdType.MESH)
    pl.semaphore_wait(barrier, len(around))

    ups, downs = ff // width, width // tall
    kinds = (
        (0, 3, s_qkv, f_qkv, s_qkv.shape[1], width),
        (3, 1, s_out, f_out, s_out.shape[1], width),
        (4, ups, s_up, f_up, s_up.shape[1], width),
        (4 + ups, downs, s_down, f_down, s_down.shape[1], tall),
    )
    per = 4 + ups + downs
    total = layers * per
    relay = Relay(fab, kinds, per, total, (sem_send, sem_recv))

    def save(src, dst, key):
        pltpu.make_async_copy(src, dst, sem_save.at[key]).start()

    def free(src, dst, key, when):
        pl.when(when)(lambda: pltpu.make_async_copy(src, dst, sem_save.at[key]).wait())

    chunk = 32
    steps = slots // chunk

    def rows_of(c):
        return pl.ds(pl.multiple_of(c * chunk, chunk), chunk)

    def tiles(w, lhs, count, body, tile=256):
        def step(j, carry):
            cols = pl.ds(pl.multiple_of(j * tile, tile), tile)
            body(cols, nn(lhs[...], w[:, cols]), j * tile)
            return carry

        lax.fori_loop(0, count // tile, step, 0)

    def norm(l, which, bias_row, base, branch, n_dst, r_dst):
        zero = jnp.zeros((8, width), F32)
        gain_row = gain[l, which : which + 1, :]
        shift_row = b_ln[l, which : which + 1, :]

        def step(c, carry):
            s_h, s_a = carry
            rows = rows_of(c)
            a = branch[rows, :] + bias_row
            h = base[rows, :]
            z = h + a
            mean = jnp.mean(z, axis=1, keepdims=True)
            centred = z - mean
            var = jnp.mean(centred * centred, axis=1, keepdims=True)
            inv = lax.rsqrt(var + 1e-06)
            n = centred * inv
            y = n * gain_row + shift_row
            base[rows, :] = y
            hb_buf[rows, :] = y.astype(BF)
            n_dst[rows, :] = n.astype(BF)
            r_dst[rows, :] = inv
            ok = vcol[rows, :]
            return s_h + fold8(ok * h * h), s_a + fold8(ok * a * a)

        return lax.fori_loop(0, steps, step, (zero, zero))

    def attention():
        lane = lax.broadcasted_iota(jnp.int32, (1, 2 * hd), 1)
        sides = (lane < hd, lane >= hd)

        def pair(hp, carry):
            cols = pl.ds(pl.multiple_of(hp * 2 * hd, 2 * hd), 2 * hd)
            for b in range(2):
                rows = pl.ds(b * half, half)
                q2, k2, v2 = qkv_buf[0, rows, cols], qkv_buf[1, rows, cols], qkv_buf[2, rows, cols]
                mixed = None
                for side in range(2):
                    keep = sides[side]
                    zero = jnp.zeros_like(q2)
                    st = nt(jnp.where(keep, k2, zero), q2) * scale
                    if b == 1:
                        st = jnp.where(vcol[rows, :] == vrow[:, rows], st, -1e30)
                    top = jnp.max(st, axis=0, keepdims=True)
                    ex = jnp.exp(st - top)
                    p = (ex * (1.0 / jnp.sum(ex, axis=0, keepdims=True))).astype(BF)
                    pt_buf[2 * hp + side, b] = p
                    o = tn(p, jnp.where(keep, v2, zero))
                    mixed = o if mixed is None else mixed + o
                mix_buf[rows, cols] = mixed.astype(BF)
            return carry

        lax.fori_loop(0, heads // 2, pair, 0)

    def compute(t):
        l = lax.div(t, per)
        j = t - l * per
        slot = lax.rem(t, 2)
        later = l > 0

        @pl.when(j < 3)
        def _():
            free(qkv_buf.at[j], qkv_o.at[0, j], j, later)
            keep = (j != 1).astype(F32)

            def body(cols, t, first):
                bias = b_qv[l, pl.ds(lax.div(j, 2), 1), cols] * keep
                qkv_buf[j, :, cols] = (t + bias).astype(BF)

            tiles(ring_w.at[slot], hb_buf, width, body)
            save(qkv_buf.at[j], qkv_o.at[l, j], j)

            @pl.when(j == 2)
            def _():
                free(pt_buf, pt_o.at[0], 3, later)
                attention()
                save(pt_buf, pt_o.at[l], 3)

        @pl.when(j == 3)
        def _():
            def body(cols, t, first):
                f_buf[:, cols] = t

            tiles(ring_w.at[slot], mix_buf, width, body)
            free(n_buf.at[0], n1_o.at[0], 4, later)
            s_h, s_a = norm(l, 0, b_out[pl.ds(l, 1), :], h_buf, f_buf, n_buf.at[0], r1_o.at[l])
            squares[pl.ds(3 * l, 1), :] = jnp.sum(s_h, axis=0, keepdims=True)
            squares[pl.ds(3 * l + 1, 1), :] = jnp.sum(s_a, axis=0, keepdims=True)
            save(n_buf.at[0], n1_o.at[l], 4)

        @pl.when(jnp.logical_and(j >= 4, j < 4 + ups))
        def _():
            part = j - 4
            par = lax.rem(part, 2)
            start = pl.multiple_of(part * width, width)
            free(sl_buf.at[par], sl_o.at[0, :, pl.ds(0, width)], 6 + par, jnp.logical_or(later, part >= 2))

            def body(cols, t, first):
                wide = pl.ds(pl.multiple_of(part * width + first, 256), 256)
                u = t + b_up[pl.ds(l, 1), wide]
                phi = 0.5 * (1.0 + lax.erf(u * 0.7071067811865476))
                sl_buf[par, :, cols] = (phi + u * (jnp.exp(-0.5 * u * u) * 0.3989422804014327)).astype(BF)
                gu_buf[:, wide] = (u * phi).astype(BF)

            tiles(ring_w.at[slot], hb_buf, width, body)
            save(sl_buf.at[par], sl_o.at[l, :, pl.ds(start, width)], 6 + par)

        @pl.when(j >= 4 + ups)
        def _():
            part = j - 4 - ups
            f_buf[:, pl.ds(pl.multiple_of(part * tall, tall), tall)] = nn(gu_buf[...], ring_t[slot])

            @pl.when(part == downs - 1)
            def _():
                free(n_buf.at[1], n2_o.at[0], 5, True)
                _, s_f = norm(l, 1, b_down[pl.ds(l, 1), :], h_buf, f_buf, n_buf.at[1], r2_o.at[l])
                squares[pl.ds(3 * l + 2, 1), :] = jnp.sum(s_f, axis=0, keepdims=True)
                save(n_buf.at[1], n2_o.at[l], 5)

    def ring_start(t):
        l = lax.div(t, per)
        j = t - l * per
        slot = lax.rem(t, 2)
        for first, number, _, full, _, cols in kinds:
            buf = ring_t if cols == tall else ring_w

            @pl.when(jnp.logical_and(j >= first, j < first + number))
            def _(first=first, full=full, cols=cols, buf=buf):
                src = full.at[l, :, pl.ds(pl.multiple_of((j - first) * cols, cols), cols)]
                pltpu.make_async_copy(src, buf.at[slot], sem_ring.at[slot]).start()

    def ring_wait(t):
        slot = lax.rem(t, 2)
        pltpu.make_async_copy(f_out.at[0], ring_w.at[slot], sem_ring.at[slot]).wait()

    for t in range(LEADS[0] - LEADS[1]):
        relay.stage(0, jnp.int32(t))
    for at, (src, buf, _) in enumerate(shards):
        pltpu.make_async_copy(src, buf, sem_own.at[at]).wait()
    placed = []
    for at, (_, buf, full) in enumerate(shards):
        rows = buf.shape[1]
        for l in range(layers):
            dst = full.at[l, pl.ds(pl.multiple_of(fab.block() * rows, rows), rows)]
            placed.append(pltpu.make_async_copy(buf.at[l], dst, sem_own.at[4 + at * layers + l]))
            placed[-1].start()

    first, second = lens[0, 0], lens[0, 1]
    shift = jnp.where(first == half, 0, first)
    back[0] = slots - shift

    def source(slot):
        return jnp.where(slot + shift >= slots, slot + shift - slots, slot + shift)

    vcol[...] = (source(lax.broadcasted_iota(jnp.int32, (slots, 1), 0)) < first + second).astype(F32)
    vrow[...] = (source(lax.broadcasted_iota(jnp.int32, (1, slots), 1)) < first + second).astype(F32)

    def turning(c, carry):
        rows = rows_of(c)
        slot = lax.broadcasted_iota(jnp.int32, (chunk, slots), 0) + c * chunk
        turn[rows, :] = (source(slot) == lax.broadcasted_iota(jnp.int32, (chunk, slots), 1)).astype(F32).astype(BF)
        return carry

    lax.fori_loop(0, steps, turning, 0)

    def turned(dst, src):
        def body(j, carry):
            cols = pl.ds(pl.multiple_of(j * 256, 256), 256)
            dst(cols, nn(turn[...], src[:, cols]))
            return carry

        lax.fori_loop(0, width // 256, body, 0)

    def put_tokens(cols, t):
        h_buf[:, cols] = t
        hb_buf[:, cols] = t.astype(BF)

    def put_cotangent(cols, t):
        n_buf[1, :, cols] = (t * vcol[...]).astype(BF)

    turned(put_tokens, tok)
    for copy in placed:
        copy.wait()

    def step(i, carry):
        at = i - LEADS[1]
        for s, lead in enumerate(LEADS):
            relay.stage(s, at + lead)

        @pl.when(i == 4)
        def _():
            pltpu.make_async_copy(cot, mix_buf, sem_save.at[3]).wait()
            turned(put_cotangent, mix_buf)
            save(n_buf.at[1], cot_o, 5)

        pl.when(jnp.logical_and(at >= 1, at <= total))(lambda: ring_wait(at - 1))

        @pl.when(jnp.logical_and(at >= 0, at < total))
        def _():
            relay.finish(at)
            ring_start(at)

        pl.when(at >= 1)(lambda: relay.drain(at - 1))
        pl.when(at >= 1)(lambda: compute(at - 1))
        return carry

    lax.fori_loop(0, total + 1 + LEADS[1], step, 0)
    pltpu.make_async_copy(hb_buf, act, sem_own.at[0]).start()
    here = jnp.sum(vcol[...], axis=0, keepdims=True)
    squares[3 * layers :, :] = jnp.broadcast_to(here, (squares.shape[0] - 3 * layers, width))
    for part in range(3):
        free(qkv_buf.at[part], qkv_o.at[0, part], part, True)
    free(pt_buf, pt_o.at[0], 3, True)
    free(n_buf.at[0], n1_o.at[0], 4, True)
    free(n_buf.at[1], n2_o.at[0], 5, True)
    for par in range(2):
        free(sl_buf.at[par], sl_o.at[0, :, pl.ds(0, width)], 6 + par, True)
    pltpu.make_async_copy(hb_buf, act, sem_own.at[0]).wait()


def forward(sizes, lengths, tokens, cotangent, gain, b_qv, b_out, b_ln, b_up, b_down, s_qkv, s_out, s_up, s_down):
    slots, width = tokens.shape
    layers = s_qkv.shape[0]
    ff = s_up.shape[2]
    half = slots // 2
    tall = width * width // ff
    hbm = pl.BlockSpec(memory_space=pl.ANY)
    vm = pl.BlockSpec(memory_space=pltpu.VMEM)
    chunks = layers * (4 + ff // width + width // tall)
    outs = [
        ((slots, width), BF, hbm),
        ((8, width), F32, vm),
        ((1,), jnp.int32, pl.BlockSpec(memory_space=pltpu.SMEM)),
        ((slots, width), BF, hbm),
        ((layers, 3, slots, width), BF, hbm),
        ((layers, HEADS, 2, half, half), BF, hbm),
        ((layers, slots, ff), BF, hbm),
        ((layers, slots, width), BF, hbm),
        ((layers, slots, width), BF, hbm),
        ((layers, slots, 1), F32, vm),
        ((layers, slots, 1), F32, vm),
        ((layers, width, 3 * width), BF, hbm),
        ((layers, width, width), BF, hbm),
        ((layers, width, ff), BF, hbm),
        ((layers, ff, width), BF, hbm),
    ]
    result = pl.pallas_call(
        functools.partial(forward_kernel, layers, sizes),
        out_shape=tuple(jax.ShapeDtypeStruct(shape, kind) for shape, kind, _ in outs),
        in_specs=[pl.BlockSpec(memory_space=pltpu.SMEM), vm, hbm] + [vm] * 6 + [hbm] * 4,
        out_specs=tuple(spec for _, _, spec in outs),
        scratch_shapes=[
            pltpu.VMEM((slots, width), F32),
            pltpu.VMEM((slots, width), BF),
            pltpu.VMEM((3, slots, width), BF),
            pltpu.VMEM((slots, width), BF),
            pltpu.VMEM((slots, ff), BF),
            pltpu.VMEM((slots, width), F32),
            pltpu.VMEM((HEADS, 2, half, half), BF),
            pltpu.VMEM((2, slots, width), BF),
            pltpu.VMEM((2, slots, width), BF),
            pltpu.VMEM((2, width, width), BF),
            pltpu.VMEM((2, ff, tall), BF),
            pltpu.VMEM(s_qkv.shape, BF),
            pltpu.VMEM(s_out.shape, BF),
            pltpu.VMEM(s_up.shape, BF),
            pltpu.VMEM(s_down.shape, BF),
            pltpu.VMEM((slots, slots), BF),
            pltpu.VMEM((slots, 1), F32),
            pltpu.VMEM((1, slots), F32),
            pltpu.SemaphoreType.DMA((2 * chunks, 5)),
            pltpu.SemaphoreType.DMA((2 * chunks, 5)),
            pltpu.SemaphoreType.DMA((4 + 4 * layers,)),
            pltpu.SemaphoreType.DMA((2,)),
            pltpu.SemaphoreType.DMA((8,)),
        ],
        compiler_params=pltpu.CompilerParams(vmem_limit_bytes=62 << 20, collective_id=0, has_side_effects=True),
        name="forward",
    )(lengths, tokens, cotangent, gain, b_qv, b_out, b_ln, b_up, b_down, s_qkv, s_out, s_up, s_down)
    return result[0], result[1], result[2], result[3], list(result[4:])


def normalize(stream, gain_row, shift_row):
    mean_row = jnp.mean(stream, axis=-1, keepdims=True)
    centred = stream - mean_row
    variance = jnp.mean(centred * centred, axis=-1, keepdims=True)
    inv_std = lax.rsqrt(variance + 1e-06)
    normed = centred * inv_std
    return normed * gain_row + shift_row, normed, inv_std


def turned_by(a, by):
    return lax.dynamic_slice_in_dim(jnp.concatenate([a, a], axis=0), by, a.shape[0], axis=0)


def forward_apart(lengths, tokens, cotangent, gain, b_qv, b_out, b_ln, b_up, b_down, *shards):
    slots, width = tokens.shape
    shift = jnp.where(lengths[0, 0] == slots // 2, 0, lengths[0, 0])
    place = lax.rem(jnp.arange(slots, dtype=jnp.int32) + shift, slots)
    vcol = (place < lengths[0, 0] + lengths[0, 1]).astype(F32)[:, None]
    tokens = turned_by(tokens, shift)
    masked = turned_by(cotangent, shift) * vcol.astype(BF)
    layers = b_out.shape[0]
    half = slots // 2
    hd = width // HEADS
    blocks = vcol.reshape(2, half)
    same = blocks[:, :, None] == blocks[:, None, :]
    stream = tokens.astype(F32)
    kept = []
    squares = []
    for l in range(layers):
        mats = [lax.all_gather(w[l], AXES, axis=0, tiled=True) for w in shards]
        projected = nn(stream.astype(BF), mats[0])
        q = (projected[:, :width] + b_qv[l, 0]).astype(BF)
        k = projected[:, width : 2 * width].astype(BF)
        v = (projected[:, 2 * width :] + b_qv[l, 1]).astype(BF)
        q4, k4, v4 = (a.reshape(2, half, HEADS, hd) for a in (q, k, v))
        st = jnp.einsum("bqhd,bkhd->hbkq", q4, k4, preferred_element_type=F32) * hd ** (-0.5)
        st = jnp.where(same[None], st, -1e30)
        ex = jnp.exp(st - jnp.max(st, axis=2, keepdims=True))
        pt = (ex / jnp.sum(ex, axis=2, keepdims=True)).astype(BF)
        mixed = jnp.einsum("hbkq,bkhd->bqhd", pt, v4, preferred_element_type=F32).reshape(slots, width).astype(BF)
        branch = nn(mixed, mats[1]) + b_out[l]
        x1, n1, r1 = normalize(stream + branch, gain[l, 0], b_ln[l, 0])
        u = nn(x1.astype(BF), mats[2]) + b_up[l]
        phi = 0.5 * (1.0 + lax.erf(u * 0.7071067811865476))
        slope = (phi + u * (jnp.exp(-0.5 * u * u) * 0.3989422804014327)).astype(BF)
        ffn = nn((u * phi).astype(BF), mats[3]) + b_down[l]
        nxt, n2, r2 = normalize(x1 + ffn, gain[l, 1], b_ln[l, 1])
        squares += [jnp.sum(vcol * a * a, axis=0) for a in (stream, branch, ffn)]
        kept.append((jnp.stack([q, k, v]), pt, slope, n1.astype(BF), n2.astype(BF), r1, r2, *mats))
        stream = nxt
    here = jnp.broadcast_to(jnp.sum(vcol), (width,))
    return stream.astype(BF), jnp.stack(squares + [here] * (8 - 3 * layers)), (slots - shift)[None], masked, [jnp.stack(a) for a in zip(*kept)]


def local(
    sizes, tokens, lengths, w_qkv, w_out, w_up, w_down, ln_gain, bias_qv, bias_out, ln_bias, bias_up, bias_down, cotangent
):
    slots, width = tokens.shape
    layers = w_qkv.shape[0]
    run = functools.partial(forward, sizes) if sizes == KERNEL_MESH else forward_apart
    act, squares, back, cot, kept = run(
        lengths, tokens, cotangent, ln_gain, bias_qv, bias_out, ln_bias, bias_up, bias_down, w_qkv, w_out, w_up, w_down
    )
    dh, whole = backward(sizes, cot, ln_gain, squares, kept)
    if sizes != KERNEL_MESH:
        whole = lax.psum(whole, AXES)
    back = back[0].astype(jnp.uint32)
    return (
        turned_by(act, back),
        turned_by(dh, back),
        whole[:, 0:2],
        whole[:, 2],
        whole[:, 3:5],
        whole[:, 5:9].reshape(layers, -1),
        whole[:, 9],
        jnp.sqrt(jnp.sum(whole[:, 10:13], axis=2) / (whole[:, 13, 0:1] * width)),
    )


def solution(mesh):
    pairs = mesh.shape["dp"] // 2
    ny = next(n for n in range(math.isqrt(pairs), 0, -1) if pairs % n == 0)
    sizes = (ny, pairs // ny, mesh.shape["shard"])
    rows = P(AXES, None)
    weight = P(None, AXES, None)
    in_specs = (rows, rows, weight, weight, weight, weight, P(), P(), P(), P(), P(), P(), rows)
    out_specs = (rows, rows, P(), P(), P(), P(), P(), P())
    return jax.shard_map(
        functools.partial(local, sizes), mesh=mesh, in_specs=in_specs, out_specs=out_specs, check_vma=False
    )
```

```python
import functools
import math

import jax
import jax.numpy as jnp
from jax import lax
from jax.experimental import pallas as pl
from jax.experimental.pallas import tpu as pltpu
from jax.sharding import PartitionSpec as P

BF = jnp.bfloat16
F32 = jnp.float32
HEADS = 16
AXES = ("dp", "shard")
KERNEL_MESH = (2, 2, 4)


def nt(a, b):
    return lax.dot_general(a, b, (((1,), (1,)), ((), ())), preferred_element_type=F32)


def nn(a, b):
    return lax.dot_general(a, b, (((1,), (0,)), ((), ())), preferred_element_type=F32)


def tn(a, b):
    return lax.dot_general(a, b, (((0,), (0,)), ((), ())), preferred_element_type=F32)


def fold8(t):
    return jnp.sum(t.reshape(t.shape[0] // 8, 8, t.shape[1]), axis=0)


class Ring:
    def __init__(self, buf, sem, segments):
        self.buf, self.sem, self.segments = buf, sem, segments
        self.slots, self.rows = buf.shape[0], buf.shape[1]
        self.base = 0

    def fetch(self, at):
        slot = lax.rem(at, self.slots)
        first = 0
        for ref, count in self.segments:
            if isinstance(at, int):
                if first <= at < first + count:
                    row = (at - first) * self.rows
                    pltpu.make_async_copy(ref.at[pl.ds(row, self.rows)], self.buf.at[slot], self.sem.at[slot]).start()
            else:

                @pl.when(jnp.logical_and(at >= first, at < first + count))
                def _(ref=ref, first=first):
                    row = pl.multiple_of((at - first) * self.rows, self.rows)
                    pltpu.make_async_copy(ref.at[pl.ds(row, self.rows)], self.buf.at[slot], self.sem.at[slot]).start()

            first += count

    def prime(self):
        for at in range(self.slots):
            self.fetch(at)

    def run(self, count, body, first=0):
        base = self.base

        def step(j, carry):
            at = base + j
            slot = lax.rem(at, self.slots)
            pltpu.make_async_copy(self.segments[0][0].at[pl.ds(0, self.rows)], self.buf.at[slot], self.sem.at[slot]).wait()
            body(first + j, self.buf[slot])
            self.fetch(at + self.slots)
            return carry

        lax.fori_loop(0, count, step, 0)
        self.base = base + count


class Fabric:
    def __init__(self, sizes):
        ny, nx, nz = sizes
        dp = lax.axis_index("dp")
        self.size = {"y": ny, "x": nx, "z": nz, "c": 2}
        self.at = {"z": lax.axis_index("shard"), "c": lax.rem(dp, 2), "x": lax.rem(dp // 2, nx), "y": dp // (2 * nx)}

    def device(self, **moved):
        at = {**self.at, **moved}
        return ((at["y"] * self.size["x"] + at["x"]) * 2 + at["c"], at["z"])

    def peers(self, axis):
        n = self.size[axis]
        return [lax.rem(self.at[axis] + step, n) for step in range(1, n)]

    def block(self, **moved):
        at = {**self.at, **moved}
        return ((at["y"] * self.size["x"] + at["x"]) * 2 + at["c"]) * self.size["z"] + at["z"]


class Total:
    def __init__(self, fabric, rest):
        (self.plane, self.line, self.mine, self.late, self.late_plane, self.late_line, self.send, self.recv) = rest
        self.fab = fabric
        self.me = lax.axis_index("dp")
        self.z = fabric.at["z"]
        self.n, self.nz = self.plane.shape[0], fabric.size["z"]
        self.mates = [(lax.rem(self.me + step, self.n), self.z) for step in range(1, self.n)]
        self.others = [(self.me, lax.rem(self.z + step, self.nz)) for step in range(1, self.nz)]

    def greet(self):
        barrier = pltpu.get_barrier_semaphore()
        for device in self.mates + self.others:
            pl.semaphore_signal(barrier, inc=1, device_id=device, device_id_type=pl.DeviceIdType.MESH)

    def met(self):
        pl.semaphore_wait(pltpu.get_barrier_semaphore(), len(self.mates) + len(self.others))

    def push(self, src, dst, sem, device):
        pltpu.make_async_remote_copy(
            src_ref=src,
            dst_ref=dst,
            send_sem=self.send.at[sem],
            recv_sem=self.recv.at[sem],
            device_id=device,
            device_id_type=pl.DeviceIdType.MESH,
        ).start()

    def wait(self, part, sems):
        for sem in sems:
            pltpu.make_async_copy(part, part, sem).wait()

    def share(self, ref, at):
        cols = ref.shape[2] // self.n
        return ref.at[:, :, pl.ds(pl.multiple_of(at * cols, cols), cols)]

    def spread(self, part):
        self.plane[self.me] = self.share(part, self.me)[...]
        for device in self.mates:
            self.push(self.share(part, device[0]), self.plane.at[self.me], 0, device)

    def along(self):
        self.wait(self.plane.at[pl.ds(0, self.n - 1)], (self.send.at[0], self.recv.at[0]))
        self.line[self.z] = self.added(self.plane)
        for device in self.others:
            self.push(self.line.at[self.z], self.line.at[self.z], 1, device)

    def back(self, out):
        self.wait(self.line.at[pl.ds(0, self.nz - 1)], (self.send.at[1], self.recv.at[1]))
        total = self.added(self.line)
        self.mine[...] = total
        self.share(out, self.me)[...] = total
        for device in self.mates:
            self.push(self.mine, self.share(out, self.me), 2, device)

    def late_spread(self):
        self.late_plane[self.me] = self.late[...]
        for device in self.mates:
            self.push(self.late, self.late_plane.at[self.me], 3, device)

    def late_along(self):
        self.wait(self.late_plane.at[pl.ds(0, self.n - 1)], (self.send.at[3], self.recv.at[3]))
        self.late_line[self.z] = self.added(self.late_plane)
        for device in self.others:
            self.push(self.late_line.at[self.z], self.late_line.at[self.z], 4, device)

    def close(self):
        self.wait(self.late_line.at[pl.ds(0, self.nz - 1)], (self.send.at[4], self.recv.at[4]))
        self.wait(self.plane.at[pl.ds(0, self.n - 1)], (self.send.at[2], self.recv.at[2]))
        return self.added(self.late_line)

    def added(self, ref):
        total = ref[0]
        for at in range(1, ref.shape[0]):
            total = total + ref[at]
        return total


def backward_kernel(layers, sizes, *refs):
    cot, gain, squares = refs[:3]
    qkv, pt, slope, n1, n2, r1, r2, wqkv, wout, wup, wdown = [
        [ref.at[l] for l in range(layers)] for ref in refs[3:14]
    ]
    q, k, v = [[ref.at[part] for ref in qkv] for part in range(3)]
    backward_body(
        layers, sizes, cot, gain, squares, q, k, v, pt, slope, n1, n2, r1, r2, wqkv, wout, wup, wdown, *refs[14:]
    )


def backward_body(
    layers, sizes, cot, gain, squares, q, k, v, pt, slope, n1, n2, r1, r2, wqkv, wout, wup, wdown,
    dh_out, summed,
    e_buf, x_buf, z_buf, du_buf, dp_buf, do_buf, cot_buf,
    q_buf, k_buf, v_buf, pt_buf, sl_buf, n1_buf, n2_buf,
    ring_a, ring_b, ring_c, sem_a, sem_b, sem_c, sem_in, sem_out, *rest,
):
    slots, width = e_buf.shape
    ff = du_buf.shape[1]
    heads = pt[0].shape[0]
    hd = width // heads
    half = slots // 2
    scale = hd ** (-0.5)
    order = list(reversed(range(layers)))
    fused = len(rest) > 0
    grads = rest[0] if fused else summed
    team = None
    if fused:
        team = Total(Fabric(sizes), rest[1:])
        team.greet()

    sources = (n2, slope, n1, q, k, v, pt)
    buffers = (n2_buf, sl_buf, n1_buf, q_buf, k_buf, v_buf, pt_buf)

    def load(which, layer, par):
        return pltpu.make_async_copy(sources[which][layer], buffers[which].at[par], sem_in.at[par, which])

    cot_copy = pltpu.make_async_copy(cot, cot_buf, sem_out.at[0])
    cot_copy.start()
    load(0, order[0], 0).start()
    seg_a = []
    seg_b = []
    seg_c = []
    for l in order:
        seg_a += [(wdown[l], ff // ring_a.shape[1]), (wout[l], width // ring_a.shape[1])]
        seg_b += [(wup[l], width // ring_b.shape[1])]
        seg_c += [(wqkv[l], width // ring_c.shape[1])]
    ra, rb, rc = Ring(ring_a, sem_a, seg_a), Ring(ring_b, sem_b, seg_b), Ring(ring_c, sem_c, seg_c)
    ra.prime()
    load(1, order[0], 0).start()
    rb.prime()
    for which in range(2, 7):
        load(which, order[0], 0).start()
    rc.prime()
    for which in range(7):
        for step, l in enumerate(order[1:], 1):
            if step < 2:
                load(which, l, step).start()

    chunk = 32
    cot_copy.wait()

    def widen(c, carry):
        rows = pl.ds(pl.multiple_of(c * chunk, chunk), chunk)
        e_buf[rows, :] = cot_buf[rows, :].astype(F32)
        return carry

    lax.fori_loop(0, slots // chunk, widen, 0)

    def norm_back(src, dst, gain_row, n_ref, r_ref):
        def step(c, carry):
            s_in, s_out = carry
            rows = pl.ds(pl.multiple_of(c * chunk, chunk), chunk)
            g = src[rows, :]
            n = n_ref[rows, :].astype(F32)
            ge = g * gain_row
            m1 = jnp.mean(ge, axis=1, keepdims=True)
            m2 = jnp.mean(ge * n, axis=1, keepdims=True)
            dz = r_ref[rows, :] * (ge - m1 - n * m2)
            dst[rows, :] = dz
            z_buf[rows, :] = dz.astype(BF)
            return (s_in + fold8(g), s_out + fold8(dz))

        zero = jnp.zeros((8, width), F32)
        s_in, s_out = lax.fori_loop(0, slots // chunk, step, (zero, zero))
        return jnp.sum(s_in, axis=0, keepdims=True), jnp.sum(s_out, axis=0, keepdims=True)

    for l in range(layers):
        grads[l, 10:13, :] = squares[3 * l : 3 * l + 3, :]
        grads[l, 13:14, :] = squares[3 * layers : 3 * layers + 1, :]
        grads[l, 14:16, :] = jnp.zeros((2, width), F32)
    if fused:
        grads[order[-1], 0:2, :] = jnp.zeros((2, width), F32)

    for step, l in enumerate(order):
        par = step % 2
        last = step == layers - 1
        early = fused and last

        load(0, l, par).wait()
        s_in, s_out = norm_back(e_buf, x_buf, gain[l, 1:2, :], n2_buf.at[par], r2[l])
        grads[l, 4:5, :] = s_in
        grads[l, 9:10, :] = s_out

        load(1, l, par).wait()
        wide = ring_a.shape[1]

        def down_body(j, w):
            cols = pl.ds(pl.multiple_of(j * wide, wide), wide)
            du = nt(z_buf[...], w) * sl_buf[par, :, cols].astype(F32)
            du_buf[:, cols] = du.astype(BF)
            part = jnp.sum(fold8(du), axis=0, keepdims=True)
            per = width // wide
            grads[l, pl.ds(5 + j // per, 1), pl.ds(pl.multiple_of(lax.rem(j, per) * wide, wide), wide)] = part

        ra.run(ff // wide, down_body)
        nb = ring_b.shape[1]

        def up_body(j, w):
            cols = pl.ds(pl.multiple_of(j * nb, nb), nb)
            x_buf[:, cols] = x_buf[:, cols] + nt(du_buf[...], w)

        rb.run(width // nb, up_body)

        load(2, l, par).wait()
        s_in, s_out = norm_back(x_buf, x_buf, gain[l, 0:1, :], n1_buf.at[par], r1[l])
        grads[l, 3:4, :] = s_in
        grads[l, 2:3, :] = s_out

        def out_body(j, w):
            cols = pl.ds(pl.multiple_of(j * wide, wide), wide)
            do_buf[:, cols] = nt(z_buf[...], w).astype(BF)

        ra.run(width // wide, out_body)

        for which in range(3, 7):
            load(which, l, par).wait()
        lane = lax.broadcasted_iota(jnp.int32, (1, 2 * hd), 1)
        sides = (lane < hd, lane >= hd)

        def pair(hp, carry):
            cols = pl.ds(pl.multiple_of(hp * 2 * hd, 2 * hd), 2 * hd)
            sum_q = jnp.zeros((8, 2 * hd), F32)
            sum_v = jnp.zeros((8, 2 * hd), F32)
            for b in range(2):
                rows = pl.ds(b * half, half)
                q2, k2, v2, do2 = (r[rows, cols] for r in (q_buf.at[par], k_buf.at[par], v_buf.at[par], do_buf))
                dq = dk = dv = None
                for side in range(2):
                    keep = sides[side]
                    zero = jnp.zeros_like(q2)
                    pb = pt_buf[par, 2 * hp + side, b]
                    dpt = nt(jnp.where(keep, v2, zero), do2)
                    p32 = pb.astype(F32)
                    t = p32 * dpt
                    inner = jnp.sum(fold8(t), axis=0, keepdims=True)
                    ds = (t - p32 * inner).astype(BF)
                    a_v = nn(pb, jnp.where(keep, do2, zero))
                    a_k = nn(ds, jnp.where(keep, q2, zero))
                    a_q = tn(ds, jnp.where(keep, k2, zero))
                    dv = a_v if dv is None else dv + a_v
                    dk = a_k if dk is None else dk + a_k
                    dq = a_q if dq is None else dq + a_q
                dq = dq * scale
                dk = dk * scale
                dp_buf[rows, cols] = dq.astype(BF)
                dp_buf[rows, pl.ds(pl.multiple_of(width + hp * 2 * hd, 2 * hd), 2 * hd)] = dk.astype(BF)
                dp_buf[rows, pl.ds(pl.multiple_of(2 * width + hp * 2 * hd, 2 * hd), 2 * hd)] = dv.astype(BF)
                sum_q = sum_q + fold8(dq)
                sum_v = sum_v + fold8(dv)
            terms = team.late if early else grads.at[l]
            terms[0:1, cols] = jnp.sum(sum_q, axis=0, keepdims=True)
            terms[1:2, cols] = jnp.sum(sum_v, axis=0, keepdims=True)
            return carry

        if early:
            team.met()
            team.spread(grads)
            lax.fori_loop(0, 3, pair, 0)
            team.along()
            lax.fori_loop(3, 6, pair, 0)
            team.back(summed)
            lax.fori_loop(6, heads // 2, pair, 0)
            team.late_spread()
        else:
            lax.fori_loop(0, heads // 2, pair, 0)
        nc = ring_c.shape[1]

        def qkv_body(j, w):
            cols = pl.ds(pl.multiple_of(j * nc, nc), nc)
            e_buf[:, cols] = x_buf[:, cols] + nt(dp_buf[...], w)
            if last:
                pltpu.make_async_copy(e_buf.at[:, cols], dh_out.at[:, cols], sem_out.at[0]).start()

        rc.run(width // nc // 2, qkv_body)
        if early:
            team.late_along()
        rc.run(width // nc // 2, qkv_body, width // nc // 2)
        for which in range(7):
            if step + 2 < layers:
                load(which, order[step + 2], par).start()

    if fused:
        summed[order[-1], 0:2, :] = team.close()
    for j in range(width // nc):
        cols = pl.ds(j * nc, nc)
        pltpu.make_async_copy(e_buf.at[:, cols], dh_out.at[:, cols], sem_out.at[0]).wait()


def backward(sizes, cot, gain, squares, kept):
    slots, width = cot.shape
    layers, heads = kept[1].shape[:2]
    ff = kept[2].shape[2]
    half = slots // 2
    hbm = pl.BlockSpec(memory_space=pl.ANY)
    vm = pl.BlockSpec(memory_space=pltpu.VMEM)
    ta, tb, tc = min(512, width), min(256, width), min(256, width)
    team = []
    params = {}
    if sizes == KERNEL_MESH:
        plane, line = 2 * sizes[0] * sizes[1], sizes[2]
        team = [
            pltpu.VMEM((layers, 16, width), F32),
            pltpu.VMEM((plane, layers, 16, width // plane), F32),
            pltpu.VMEM((line, layers, 16, width // plane), F32),
            pltpu.VMEM((layers, 16, width // plane), F32),
            pltpu.VMEM((2, width), F32),
            pltpu.VMEM((plane, 2, width), F32),
            pltpu.VMEM((line, 2, width), F32),
            pltpu.SemaphoreType.DMA((5,)),
            pltpu.SemaphoreType.DMA((5,)),
        ]
        params = dict(collective_id=1, has_side_effects=True)
    return pl.pallas_call(
        functools.partial(backward_kernel, layers, sizes),
        out_shape=(
            jax.ShapeDtypeStruct((slots, width), F32),
            jax.ShapeDtypeStruct((layers, 16, width), F32),
        ),
        in_specs=[hbm, vm, vm] + [hbm] * 5 + [vm] * 2 + [hbm] * 4,
        out_specs=(hbm, vm),
        scratch_shapes=[
            pltpu.VMEM((slots, width), F32),
            pltpu.VMEM((slots, width), F32),
            pltpu.VMEM((slots, width), BF),
            pltpu.VMEM((slots, ff), BF),
            pltpu.VMEM((slots, 3 * width), BF),
            pltpu.VMEM((slots, width), BF),
            pltpu.VMEM((slots, width), BF),
        ]
        + [pltpu.VMEM((2, slots, width), BF)] * 3
        + [
            pltpu.VMEM((2, heads, 2, half, half), BF),
            pltpu.VMEM((2, slots, ff), BF),
            pltpu.VMEM((2, slots, width), BF),
            pltpu.VMEM((2, slots, width), BF),
            pltpu.VMEM((3, ta, width), BF),
            pltpu.VMEM((2, tb, ff), BF),
            pltpu.VMEM((2, tc, 3 * width), BF),
            pltpu.SemaphoreType.DMA((3,)),
            pltpu.SemaphoreType.DMA((2,)),
            pltpu.SemaphoreType.DMA((2,)),
            pltpu.SemaphoreType.DMA((2, 7)),
            pltpu.SemaphoreType.DMA((1,)),
        ]
        + team,
        compiler_params=pltpu.CompilerParams(vmem_limit_bytes=67000000, **params),
        name="backward",
    )(cot, gain, squares, *kept)


class Relay:
    def __init__(self, fabric, kinds, per, count, sems):
        self.fab, self.kinds, self.per, self.count = fabric, kinds, per, count
        self.send, self.recv = sems
        at = fabric.at
        self.pair = lax.div(at["z"], 2) * 2
        self.other = 2 - self.pair
        self.mate = self.pair + 1 - lax.rem(at["z"], 2)
        self.inner = jnp.logical_or(at["z"] == 1, at["z"] == 2)

    def wait(self, sem, blocks):
        _, _, _, full, rows, cols = self.kinds[0]
        part = full.at[0, pl.ds(0, blocks * rows), pl.ds(0, cols // 2)]
        pltpu.make_async_copy(part, part, sem).wait()

    def each(self, t, act):
        l = lax.div(t, self.per)
        j = t - l * self.per
        for first, number, own, full, rows, cols in self.kinds:

            @pl.when(jnp.logical_and(j >= first, j < first + number))
            def _(first=first, own=own, full=full, rows=rows, cols=cols):
                for piece in range(2):
                    col = pl.multiple_of((j - first) * cols + piece * (cols // 2), cols // 2)
                    act(l, own, full, rows, pl.ds(col, cols // 2), piece)

    def push(self, t, piece, sem, device, src, dst):
        pltpu.make_async_remote_copy(
            src_ref=src,
            dst_ref=dst,
            send_sem=self.send.at[2 * t + piece, sem],
            recv_sem=self.recv.at[2 * t + piece, sem],
            device_id=device,
            device_id_type=pl.DeviceIdType.MESH,
        ).start()

    def stage(self, s, t):
        fab = self.fab
        at = fab.at
        partner = fab.device(c=1 - at["c"])

        @pl.when(jnp.logical_and(t >= 0, t < self.count))
        def _():
            for piece in range(2):
                if s == 1:
                    self.wait(self.recv.at[2 * t + piece, 0], 1)
                elif s == 2:
                    self.wait(self.recv.at[2 * t + piece, 1], 2)
                elif s == 3:
                    pl.when(self.inner)(lambda piece=piece: self.wait(self.recv.at[2 * t + piece, 2], 4))
                elif s == 4:
                    pl.when(jnp.logical_not(self.inner))(
                        lambda piece=piece: self.wait(self.recv.at[2 * t + piece, 2], 4)
                    )
                    self.wait(self.recv.at[2 * t + piece, 5], 4)
                elif s == 5:
                    self.wait(self.recv.at[2 * t + piece, 3], 4)

            def act(l, own, full, rows, cols, piece):
                u, v = (("x", "y"), ("y", "x"))[piece]

                def view(first, blocks):
                    return full.at[l, pl.ds(pl.multiple_of(first * rows, rows), blocks * rows), cols]

                def out(sem, device, runs):
                    for first, blocks in runs:
                        self.push(t, piece, sem, device, view(first, blocks), view(first, blocks))

                def runs(z, **moved):
                    return [(fab.block(**{u: each, "z": z, **moved}), 2) for each in range(2)]

                across = fab.device(**{v: 1 - at[v]})
                beyond = {v: 1 - at[v]}
                if s == 0:
                    mine = view(fab.block(), 1)
                    self.push(t, piece, 0, fab.device(z=self.mate), own.at[l, :, cols], mine)
                    self.push(t, piece, 4, partner, own.at[l, :, cols], mine)
                elif s == 1:
                    out(1, fab.device(**{u: 1 - at[u]}), [(fab.block(z=self.pair), 2)])
                    out(4, partner, [(fab.block(z=self.mate), 1)])
                elif s == 2:
                    pl.when(self.inner)(lambda: out(2, fab.device(z=3 - at["z"]), runs(self.pair)))
                    out(5, across, runs(self.pair))
                    out(4, partner, [(fab.block(**{u: 1 - at[u], "z": self.pair}), 2)])
                elif s == 3:

                    @pl.when(self.inner)
                    def _():
                        out(2, fab.device(z=self.mate), runs(self.other))
                        out(3, across, runs(self.other))
                        out(4, partner, runs(self.other))

                elif s == 4:

                    @pl.when(jnp.logical_not(self.inner))
                    def _():
                        out(3, across, runs(self.other))
                        out(4, partner, runs(self.other))

                    out(4, partner, runs(self.pair, **beyond))
                else:
                    out(4, partner, runs(self.other, **beyond))

            self.each(t, act)

    def finish(self, t):
        for piece in range(2):
            self.wait(self.recv.at[2 * t + piece, 4], 16)

    def drain(self, t):
        for piece in range(2):
            for sem, blocks in ((0, 1), (1, 2), (3, 4), (4, 16), (5, 4)):
                self.wait(self.send.at[2 * t + piece, sem], blocks)
            pl.when(self.inner)(lambda piece=piece: self.wait(self.send.at[2 * t + piece, 2], 8))


LEADS = (11, 9, 7, 5, 3, 1)


def forward_kernel(layers, sizes, *refs):
    (lens, tok, cot, gain, b_qv, b_out, b_ln, b_up, b_down, s_qkv, s_out, s_up, s_down) = refs[:13]
    (act, squares, back, cot_o, qkv_o, pt_o, sl_o, n1_o, n2_o, r1_o, r2_o, f_qkv, f_out, f_up, f_down) = refs[13:28]
    (
        h_buf, hb_buf, qkv_buf, mix_buf, gu_buf, f_buf, pt_buf, sl_buf, n_buf,
        ring_w, ring_t, own_qkv, own_out, own_up, own_down, turn, vcol, vrow,
        sem_send, sem_recv, sem_own, sem_ring, sem_save,
    ) = refs[28:]
    slots, width = tok.shape
    ff = gu_buf.shape[1]
    heads = pt_buf.shape[0]
    hd = width // heads
    half = slots // 2
    scale = hd ** (-0.5)
    tall = ring_t.shape[2]
    fab = Fabric(sizes)

    shards = ((s_qkv, own_qkv, f_qkv), (s_out, own_out, f_out), (s_up, own_up, f_up), (s_down, own_down, f_down))
    for at, (src, buf, _) in enumerate(shards):
        pltpu.make_async_copy(src, buf, sem_own.at[at]).start()
    pltpu.make_async_copy(cot, mix_buf, sem_save.at[3]).start()
    barrier = pltpu.get_barrier_semaphore()
    around = [fab.device(**{axis: peer}) for axis in ("z", "x", "y", "c") for peer in fab.peers(axis)]
    for device in around:
        pl.semaphore_signal(barrier, inc=1, device_id=device, device_id_type=pl.DeviceIdType.MESH)
    pl.semaphore_wait(barrier, len(around))

    ups, downs = ff // width, width // tall
    kinds = (
        (0, 3, s_qkv, f_qkv, s_qkv.shape[1], width),
        (3, 1, s_out, f_out, s_out.shape[1], width),
        (4, ups, s_up, f_up, s_up.shape[1], width),
        (4 + ups, downs, s_down, f_down, s_down.shape[1], tall),
    )
    per = 4 + ups + downs
    total = layers * per
    relay = Relay(fab, kinds, per, total, (sem_send, sem_recv))

    def save(src, dst, key):
        pltpu.make_async_copy(src, dst, sem_save.at[key]).start()

    def free(src, dst, key, when):
        pl.when(when)(lambda: pltpu.make_async_copy(src, dst, sem_save.at[key]).wait())

    chunk = 32
    steps = slots // chunk

    def rows_of(c):
        return pl.ds(pl.multiple_of(c * chunk, chunk), chunk)

    def tiles(w, lhs, count, body, tile=256):
        def step(j, carry):
            cols = pl.ds(pl.multiple_of(j * tile, tile), tile)
            body(cols, nn(lhs[...], w[:, cols]), j * tile)
            return carry

        lax.fori_loop(0, count // tile, step, 0)

    def norm(l, which, bias_row, base, branch, n_dst, r_dst):
        zero = jnp.zeros((8, width), F32)
        gain_row = gain[l, which : which + 1, :]
        shift_row = b_ln[l, which : which + 1, :]

        def step(c, carry):
            s_h, s_a = carry
            rows = rows_of(c)
            a = branch[rows, :] + bias_row
            h = base[rows, :]
            z = h + a
            mean = jnp.mean(z, axis=1, keepdims=True)
            centred = z - mean
            var = jnp.mean(centred * centred, axis=1, keepdims=True)
            inv = lax.rsqrt(var + 1e-06)
            n = centred * inv
            y = n * gain_row + shift_row
            base[rows, :] = y
            hb_buf[rows, :] = y.astype(BF)
            n_dst[rows, :] = n.astype(BF)
            r_dst[rows, :] = inv
            ok = vcol[rows, :]
            return s_h + fold8(ok * h * h), s_a + fold8(ok * a * a)

        return lax.fori_loop(0, steps, step, (zero, zero))

    def attention():
        lane = lax.broadcasted_iota(jnp.int32, (1, 2 * hd), 1)
        sides = (lane < hd, lane >= hd)

        def pair(hp, carry):
            cols = pl.ds(pl.multiple_of(hp * 2 * hd, 2 * hd), 2 * hd)
            for b in range(2):
                rows = pl.ds(b * half, half)
                q2, k2, v2 = qkv_buf[0, rows, cols], qkv_buf[1, rows, cols], qkv_buf[2, rows, cols]
                mixed = None
                for side in range(2):
                    keep = sides[side]
                    zero = jnp.zeros_like(q2)
                    st = nt(jnp.where(keep, k2, zero), q2) * scale
                    if b == 1:
                        st = jnp.where(vcol[rows, :] == vrow[:, rows], st, -1e30)
                    top = jnp.max(st, axis=0, keepdims=True)
                    ex = jnp.exp(st - top)
                    p = (ex * (1.0 / jnp.sum(ex, axis=0, keepdims=True))).astype(BF)
                    pt_buf[2 * hp + side, b] = p
                    o = tn(p, jnp.where(keep, v2, zero))
                    mixed = o if mixed is None else mixed + o
                mix_buf[rows, cols] = mixed.astype(BF)
            return carry

        lax.fori_loop(0, heads // 2, pair, 0)

    def compute(t):
        l = lax.div(t, per)
        j = t - l * per
        slot = lax.rem(t, 2)
        later = l > 0

        @pl.when(j < 3)
        def _():
            free(qkv_buf.at[j], qkv_o.at[0, j], j, later)
            keep = (j != 1).astype(F32)

            def body(cols, t, first):
                bias = b_qv[l, pl.ds(lax.div(j, 2), 1), cols] * keep
                qkv_buf[j, :, cols] = (t + bias).astype(BF)

            tiles(ring_w.at[slot], hb_buf, width, body)
            save(qkv_buf.at[j], qkv_o.at[l, j], j)

            @pl.when(j == 2)
            def _():
                free(pt_buf, pt_o.at[0], 3, later)
                attention()
                save(pt_buf, pt_o.at[l], 3)

        @pl.when(j == 3)
        def _():
            def body(cols, t, first):
                f_buf[:, cols] = t

            tiles(ring_w.at[slot], mix_buf, width, body)
            free(n_buf.at[0], n1_o.at[0], 4, later)
            s_h, s_a = norm(l, 0, b_out[pl.ds(l, 1), :], h_buf, f_buf, n_buf.at[0], r1_o.at[l])
            squares[pl.ds(3 * l, 1), :] = jnp.sum(s_h, axis=0, keepdims=True)
            squares[pl.ds(3 * l + 1, 1), :] = jnp.sum(s_a, axis=0, keepdims=True)
            save(n_buf.at[0], n1_o.at[l], 4)

        @pl.when(jnp.logical_and(j >= 4, j < 4 + ups))
        def _():
            part = j - 4
            par = lax.rem(part, 2)
            start = pl.multiple_of(part * width, width)
            free(sl_buf.at[par], sl_o.at[0, :, pl.ds(0, width)], 6 + par, jnp.logical_or(later, part >= 2))

            def body(cols, t, first):
                wide = pl.ds(pl.multiple_of(part * width + first, 256), 256)
                u = t + b_up[pl.ds(l, 1), wide]
                phi = 0.5 * (1.0 + lax.erf(u * 0.7071067811865476))
                sl_buf[par, :, cols] = (phi + u * (jnp.exp(-0.5 * u * u) * 0.3989422804014327)).astype(BF)
                gu_buf[:, wide] = (u * phi).astype(BF)

            tiles(ring_w.at[slot], hb_buf, width, body)
            save(sl_buf.at[par], sl_o.at[l, :, pl.ds(start, width)], 6 + par)

        @pl.when(j >= 4 + ups)
        def _():
            part = j - 4 - ups
            f_buf[:, pl.ds(pl.multiple_of(part * tall, tall), tall)] = nn(gu_buf[...], ring_t[slot])

            @pl.when(part == downs - 1)
            def _():
                free(n_buf.at[1], n2_o.at[0], 5, True)
                _, s_f = norm(l, 1, b_down[pl.ds(l, 1), :], h_buf, f_buf, n_buf.at[1], r2_o.at[l])
                squares[pl.ds(3 * l + 2, 1), :] = jnp.sum(s_f, axis=0, keepdims=True)
                save(n_buf.at[1], n2_o.at[l], 5)

    def ring_start(t):
        l = lax.div(t, per)
        j = t - l * per
        slot = lax.rem(t, 2)
        for first, number, _, full, _, cols in kinds:
            buf = ring_t if cols == tall else ring_w

            @pl.when(jnp.logical_and(j >= first, j < first + number))
            def _(first=first, full=full, cols=cols, buf=buf):
                src = full.at[l, :, pl.ds(pl.multiple_of((j - first) * cols, cols), cols)]
                pltpu.make_async_copy(src, buf.at[slot], sem_ring.at[slot]).start()

    def ring_wait(t):
        slot = lax.rem(t, 2)
        pltpu.make_async_copy(f_out.at[0], ring_w.at[slot], sem_ring.at[slot]).wait()

    for t in range(LEADS[0] - LEADS[1]):
        relay.stage(0, jnp.int32(t))
    for at, (src, buf, _) in enumerate(shards):
        pltpu.make_async_copy(src, buf, sem_own.at[at]).wait()
    placed = []
    for at, (_, buf, full) in enumerate(shards):
        rows = buf.shape[1]
        for l in range(layers):
            dst = full.at[l, pl.ds(pl.multiple_of(fab.block() * rows, rows), rows)]
            placed.append(pltpu.make_async_copy(buf.at[l], dst, sem_own.at[4 + at * layers + l]))
            placed[-1].start()

    first, second = lens[0, 0], lens[0, 1]
    shift = jnp.where(first == half, 0, first)
    back[0] = slots - shift

    def source(slot):
        return jnp.where(slot + shift >= slots, slot + shift - slots, slot + shift)

    vcol[...] = (source(lax.broadcasted_iota(jnp.int32, (slots, 1), 0)) < first + second).astype(F32)
    vrow[...] = (source(lax.broadcasted_iota(jnp.int32, (1, slots), 1)) < first + second).astype(F32)

    def turning(c, carry):
        rows = rows_of(c)
        slot = lax.broadcasted_iota(jnp.int32, (chunk, slots), 0) + c * chunk
        turn[rows, :] = (source(slot) == lax.broadcasted_iota(jnp.int32, (chunk, slots), 1)).astype(F32).astype(BF)
        return carry

    lax.fori_loop(0, steps, turning, 0)

    def turned(dst, src):
        def body(j, carry):
            cols = pl.ds(pl.multiple_of(j * 256, 256), 256)
            dst(cols, nn(turn[...], src[:, cols]))
            return carry

        lax.fori_loop(0, width // 256, body, 0)

    def put_tokens(cols, t):
        h_buf[:, cols] = t
        hb_buf[:, cols] = t.astype(BF)

    def put_cotangent(cols, t):
        n_buf[1, :, cols] = (t * vcol[...]).astype(BF)

    turned(put_tokens, tok)
    for copy in placed:
        copy.wait()

    def step(i, carry):
        at = i - LEADS[1]
        for s, lead in enumerate(LEADS):
            relay.stage(s, at + lead)

        @pl.when(i == 4)
        def _():
            pltpu.make_async_copy(cot, mix_buf, sem_save.at[3]).wait()
            turned(put_cotangent, mix_buf)
            save(n_buf.at[1], cot_o, 5)

        pl.when(jnp.logical_and(at >= 1, at <= total))(lambda: ring_wait(at - 1))

        @pl.when(jnp.logical_and(at >= 0, at < total))
        def _():
            relay.finish(at)
            ring_start(at)

        pl.when(at >= 1)(lambda: relay.drain(at - 1))
        pl.when(at >= 1)(lambda: compute(at - 1))
        return carry

    lax.fori_loop(0, total + 1 + LEADS[1], step, 0)
    pltpu.make_async_copy(hb_buf, act, sem_own.at[0]).start()
    here = jnp.sum(vcol[...], axis=0, keepdims=True)
    squares[3 * layers :, :] = jnp.broadcast_to(here, (squares.shape[0] - 3 * layers, width))
    for part in range(3):
        free(qkv_buf.at[part], qkv_o.at[0, part], part, True)
    free(pt_buf, pt_o.at[0], 3, True)
    free(n_buf.at[0], n1_o.at[0], 4, True)
    free(n_buf.at[1], n2_o.at[0], 5, True)
    for par in range(2):
        free(sl_buf.at[par], sl_o.at[0, :, pl.ds(0, width)], 6 + par, True)
    pltpu.make_async_copy(hb_buf, act, sem_own.at[0]).wait()


def forward(sizes, lengths, tokens, cotangent, gain, b_qv, b_out, b_ln, b_up, b_down, s_qkv, s_out, s_up, s_down):
    slots, width = tokens.shape
    layers = s_qkv.shape[0]
    ff = s_up.shape[2]
    half = slots // 2
    tall = width * width // ff
    hbm = pl.BlockSpec(memory_space=pl.ANY)
    vm = pl.BlockSpec(memory_space=pltpu.VMEM)
    chunks = layers * (4 + ff // width + width // tall)
    outs = [
        ((slots, width), BF, hbm),
        ((8, width), F32, vm),
        ((1,), jnp.int32, pl.BlockSpec(memory_space=pltpu.SMEM)),
        ((slots, width), BF, hbm),
        ((layers, 3, slots, width), BF, hbm),
        ((layers, HEADS, 2, half, half), BF, hbm),
        ((layers, slots, ff), BF, hbm),
        ((layers, slots, width), BF, hbm),
        ((layers, slots, width), BF, hbm),
        ((layers, slots, 1), F32, vm),
        ((layers, slots, 1), F32, vm),
        ((layers, width, 3 * width), BF, hbm),
        ((layers, width, width), BF, hbm),
        ((layers, width, ff), BF, hbm),
        ((layers, ff, width), BF, hbm),
    ]
    result = pl.pallas_call(
        functools.partial(forward_kernel, layers, sizes),
        out_shape=tuple(jax.ShapeDtypeStruct(shape, kind) for shape, kind, _ in outs),
        in_specs=[pl.BlockSpec(memory_space=pltpu.SMEM), vm, hbm] + [vm] * 6 + [hbm] * 4,
        out_specs=tuple(spec for _, _, spec in outs),
        scratch_shapes=[
            pltpu.VMEM((slots, width), F32),
            pltpu.VMEM((slots, width), BF),
            pltpu.VMEM((3, slots, width), BF),
            pltpu.VMEM((slots, width), BF),
            pltpu.VMEM((slots, ff), BF),
            pltpu.VMEM((slots, width), F32),
            pltpu.VMEM((HEADS, 2, half, half), BF),
            pltpu.VMEM((2, slots, width), BF),
            pltpu.VMEM((2, slots, width), BF),
            pltpu.VMEM((2, width, width), BF),
            pltpu.VMEM((2, ff, tall), BF),
            pltpu.VMEM(s_qkv.shape, BF),
            pltpu.VMEM(s_out.shape, BF),
            pltpu.VMEM(s_up.shape, BF),
            pltpu.VMEM(s_down.shape, BF),
            pltpu.VMEM((slots, slots), BF),
            pltpu.VMEM((slots, 1), F32),
            pltpu.VMEM((1, slots), F32),
            pltpu.SemaphoreType.DMA((2 * chunks, 6)),
            pltpu.SemaphoreType.DMA((2 * chunks, 6)),
            pltpu.SemaphoreType.DMA((4 + 4 * layers,)),
            pltpu.SemaphoreType.DMA((2,)),
            pltpu.SemaphoreType.DMA((8,)),
        ],
        compiler_params=pltpu.CompilerParams(vmem_limit_bytes=62 << 20, collective_id=0, has_side_effects=True),
        name="forward",
    )(lengths, tokens, cotangent, gain, b_qv, b_out, b_ln, b_up, b_down, s_qkv, s_out, s_up, s_down)
    return result[0], result[1], result[2], result[3], list(result[4:])


def normalize(stream, gain_row, shift_row):
    mean_row = jnp.mean(stream, axis=-1, keepdims=True)
    centred = stream - mean_row
    variance = jnp.mean(centred * centred, axis=-1, keepdims=True)
    inv_std = lax.rsqrt(variance + 1e-06)
    normed = centred * inv_std
    return normed * gain_row + shift_row, normed, inv_std


def turned_by(a, by):
    return lax.dynamic_slice_in_dim(jnp.concatenate([a, a], axis=0), by, a.shape[0], axis=0)


def forward_apart(lengths, tokens, cotangent, gain, b_qv, b_out, b_ln, b_up, b_down, *shards):
    slots, width = tokens.shape
    shift = jnp.where(lengths[0, 0] == slots // 2, 0, lengths[0, 0])
    place = lax.rem(jnp.arange(slots, dtype=jnp.int32) + shift, slots)
    vcol = (place < lengths[0, 0] + lengths[0, 1]).astype(F32)[:, None]
    tokens = turned_by(tokens, shift)
    masked = turned_by(cotangent, shift) * vcol.astype(BF)
    layers = b_out.shape[0]
    half = slots // 2
    hd = width // HEADS
    blocks = vcol.reshape(2, half)
    same = blocks[:, :, None] == blocks[:, None, :]
    stream = tokens.astype(F32)
    kept = []
    squares = []
    for l in range(layers):
        mats = [lax.all_gather(w[l], AXES, axis=0, tiled=True) for w in shards]
        projected = nn(stream.astype(BF), mats[0])
        q = (projected[:, :width] + b_qv[l, 0]).astype(BF)
        k = projected[:, width : 2 * width].astype(BF)
        v = (projected[:, 2 * width :] + b_qv[l, 1]).astype(BF)
        q4, k4, v4 = (a.reshape(2, half, HEADS, hd) for a in (q, k, v))
        st = jnp.einsum("bqhd,bkhd->hbkq", q4, k4, preferred_element_type=F32) * hd ** (-0.5)
        st = jnp.where(same[None], st, -1e30)
        ex = jnp.exp(st - jnp.max(st, axis=2, keepdims=True))
        pt = (ex / jnp.sum(ex, axis=2, keepdims=True)).astype(BF)
        mixed = jnp.einsum("hbkq,bkhd->bqhd", pt, v4, preferred_element_type=F32).reshape(slots, width).astype(BF)
        branch = nn(mixed, mats[1]) + b_out[l]
        x1, n1, r1 = normalize(stream + branch, gain[l, 0], b_ln[l, 0])
        u = nn(x1.astype(BF), mats[2]) + b_up[l]
        phi = 0.5 * (1.0 + lax.erf(u * 0.7071067811865476))
        slope = (phi + u * (jnp.exp(-0.5 * u * u) * 0.3989422804014327)).astype(BF)
        ffn = nn((u * phi).astype(BF), mats[3]) + b_down[l]
        nxt, n2, r2 = normalize(x1 + ffn, gain[l, 1], b_ln[l, 1])
        squares += [jnp.sum(vcol * a * a, axis=0) for a in (stream, branch, ffn)]
        kept.append((jnp.stack([q, k, v]), pt, slope, n1.astype(BF), n2.astype(BF), r1, r2, *mats))
        stream = nxt
    here = jnp.broadcast_to(jnp.sum(vcol), (width,))
    return stream.astype(BF), jnp.stack(squares + [here] * (8 - 3 * layers)), (slots - shift)[None], masked, [jnp.stack(a) for a in zip(*kept)]


def local(
    sizes, tokens, lengths, w_qkv, w_out, w_up, w_down, ln_gain, bias_qv, bias_out, ln_bias, bias_up, bias_down, cotangent
):
    slots, width = tokens.shape
    layers = w_qkv.shape[0]
    run = functools.partial(forward, sizes) if sizes == KERNEL_MESH else forward_apart
    act, squares, back, cot, kept = run(
        lengths, tokens, cotangent, ln_gain, bias_qv, bias_out, ln_bias, bias_up, bias_down, w_qkv, w_out, w_up, w_down
    )
    dh, whole = backward(sizes, cot, ln_gain, squares, kept)
    if sizes != KERNEL_MESH:
        whole = lax.psum(whole, AXES)
    back = back[0].astype(jnp.uint32)
    return (
        turned_by(act, back),
        turned_by(dh, back),
        whole[:, 0:2],
        whole[:, 2],
        whole[:, 3:5],
        whole[:, 5:9].reshape(layers, -1),
        whole[:, 9],
        jnp.sqrt(jnp.sum(whole[:, 10:13], axis=2) / (whole[:, 13, 0:1] * width)),
    )


def solution(mesh):
    pairs = mesh.shape["dp"] // 2
    ny = next(n for n in range(math.isqrt(pairs), 0, -1) if pairs % n == 0)
    sizes = (ny, pairs // ny, mesh.shape["shard"])
    rows = P(AXES, None)
    weight = P(None, AXES, None)
    in_specs = (rows, rows, weight, weight, weight, weight, P(), P(), P(), P(), P(), P(), rows)
    out_specs = (rows, rows, P(), P(), P(), P(), P(), P())
    return jax.shard_map(
        functools.partial(local, sizes), mesh=mesh, in_specs=in_specs, out_specs=out_specs, check_vma=False
    )
```

```python
import functools
import math

import jax
import jax.numpy as jnp
from jax import lax
from jax.experimental import pallas as pl
from jax.experimental.pallas import tpu as pltpu
from jax.sharding import PartitionSpec as P

BF = jnp.bfloat16
F32 = jnp.float32
HEADS = 16
AXES = ("dp", "shard")
KERNEL_MESH = (2, 2, 4)


def nt(a, b):
    return lax.dot_general(a, b, (((1,), (1,)), ((), ())), preferred_element_type=F32)


def nn(a, b):
    return lax.dot_general(a, b, (((1,), (0,)), ((), ())), preferred_element_type=F32)


def tn(a, b):
    return lax.dot_general(a, b, (((0,), (0,)), ((), ())), preferred_element_type=F32)


def fold8(t):
    return jnp.sum(t.reshape(t.shape[0] // 8, 8, t.shape[1]), axis=0)


class Ring:
    def __init__(self, buf, sem, segments):
        self.buf, self.sem, self.segments = buf, sem, segments
        self.slots, self.rows = buf.shape[0], buf.shape[1]
        self.base = 0

    def fetch(self, at):
        slot = lax.rem(at, self.slots)
        first = 0
        for ref, count in self.segments:
            if isinstance(at, int):
                if first <= at < first + count:
                    row = (at - first) * self.rows
                    pltpu.make_async_copy(ref.at[pl.ds(row, self.rows)], self.buf.at[slot], self.sem.at[slot]).start()
            else:

                @pl.when(jnp.logical_and(at >= first, at < first + count))
                def _(ref=ref, first=first):
                    row = pl.multiple_of((at - first) * self.rows, self.rows)
                    pltpu.make_async_copy(ref.at[pl.ds(row, self.rows)], self.buf.at[slot], self.sem.at[slot]).start()

            first += count

    def prime(self):
        for at in range(self.slots):
            self.fetch(at)

    def run(self, count, body, first=0):
        base = self.base

        def step(j, carry):
            at = base + j
            slot = lax.rem(at, self.slots)
            pltpu.make_async_copy(self.segments[0][0].at[pl.ds(0, self.rows)], self.buf.at[slot], self.sem.at[slot]).wait()
            body(first + j, self.buf[slot])
            self.fetch(at + self.slots)
            return carry

        lax.fori_loop(0, count, step, 0)
        self.base = base + count


class Fabric:
    def __init__(self, sizes):
        ny, nx, nz = sizes
        dp = lax.axis_index("dp")
        self.size = {"y": ny, "x": nx, "z": nz, "c": 2}
        self.at = {"z": lax.axis_index("shard"), "c": lax.rem(dp, 2), "x": lax.rem(dp // 2, nx), "y": dp // (2 * nx)}

    def device(self, **moved):
        at = {**self.at, **moved}
        return ((at["y"] * self.size["x"] + at["x"]) * 2 + at["c"], at["z"])

    def peers(self, axis):
        n = self.size[axis]
        return [lax.rem(self.at[axis] + step, n) for step in range(1, n)]

    def block(self, **moved):
        at = {**self.at, **moved}
        return ((at["y"] * self.size["x"] + at["x"]) * 2 + at["c"]) * self.size["z"] + at["z"]


class Total:
    def __init__(self, fabric, rest):
        (self.plane, self.line, self.mine, self.late, self.late_plane, self.late_line, self.send, self.recv) = rest
        self.fab = fabric
        self.me = lax.axis_index("dp")
        self.z = fabric.at["z"]
        self.n, self.nz = self.plane.shape[0], fabric.size["z"]
        self.mates = [(lax.rem(self.me + step, self.n), self.z) for step in range(1, self.n)]
        self.others = [(self.me, lax.rem(self.z + step, self.nz)) for step in range(1, self.nz)]

    def greet(self):
        barrier = pltpu.get_barrier_semaphore()
        for device in self.mates + self.others:
            pl.semaphore_signal(barrier, inc=1, device_id=device, device_id_type=pl.DeviceIdType.MESH)

    def met(self):
        pl.semaphore_wait(pltpu.get_barrier_semaphore(), len(self.mates) + len(self.others))

    def push(self, src, dst, sem, device):
        pltpu.make_async_remote_copy(
            src_ref=src,
            dst_ref=dst,
            send_sem=self.send.at[sem],
            recv_sem=self.recv.at[sem],
            device_id=device,
            device_id_type=pl.DeviceIdType.MESH,
        ).start()

    def wait(self, part, sems):
        for sem in sems:
            pltpu.make_async_copy(part, part, sem).wait()

    def share(self, ref, at):
        cols = ref.shape[2] // self.n
        return ref.at[:, :, pl.ds(pl.multiple_of(at * cols, cols), cols)]

    def spread(self, part):
        self.plane[self.me] = self.share(part, self.me)[...]
        for device in self.mates:
            self.push(self.share(part, device[0]), self.plane.at[self.me], 0, device)

    def along(self):
        self.wait(self.plane.at[pl.ds(0, self.n - 1)], (self.send.at[0], self.recv.at[0]))
        self.line[self.z] = self.added(self.plane)
        for device in self.others:
            self.push(self.line.at[self.z], self.line.at[self.z], 1, device)

    def back(self, out):
        self.wait(self.line.at[pl.ds(0, self.nz - 1)], (self.send.at[1], self.recv.at[1]))
        total = self.added(self.line)
        self.mine[...] = total
        self.share(out, self.me)[...] = total
        for device in self.mates:
            self.push(self.mine, self.share(out, self.me), 2, device)

    def late_spread(self):
        self.late_plane[self.me] = self.late[...]
        for device in self.mates:
            self.push(self.late, self.late_plane.at[self.me], 3, device)

    def late_along(self):
        self.wait(self.late_plane.at[pl.ds(0, self.n - 1)], (self.send.at[3], self.recv.at[3]))
        self.late_line[self.z] = self.added(self.late_plane)
        for device in self.others:
            self.push(self.late_line.at[self.z], self.late_line.at[self.z], 4, device)

    def close(self):
        self.wait(self.late_line.at[pl.ds(0, self.nz - 1)], (self.send.at[4], self.recv.at[4]))
        self.wait(self.plane.at[pl.ds(0, self.n - 1)], (self.send.at[2], self.recv.at[2]))
        return self.added(self.late_line)

    def added(self, ref):
        total = ref[0]
        for at in range(1, ref.shape[0]):
            total = total + ref[at]
        return total


def backward_kernel(layers, sizes, *refs):
    cot, gain, squares = refs[:3]
    qkv, pt, slope, n1, n2, r1, r2, wqkv, wout, wup, wdown = [
        [ref.at[l] for l in range(layers)] for ref in refs[3:14]
    ]
    q, k, v = [[ref.at[part] for ref in qkv] for part in range(3)]
    backward_body(
        layers, sizes, cot, gain, squares, q, k, v, pt, slope, n1, n2, r1, r2, wqkv, wout, wup, wdown, *refs[14:]
    )


def backward_body(
    layers, sizes, cot, gain, squares, q, k, v, pt, slope, n1, n2, r1, r2, wqkv, wout, wup, wdown,
    dh_out, summed,
    e_buf, x_buf, z_buf, du_buf, dp_buf, do_buf, cot_buf,
    q_buf, k_buf, v_buf, pt_buf, sl_buf, n1_buf, n2_buf,
    ring_a, ring_b, ring_c, sem_a, sem_b, sem_c, sem_in, sem_out, *rest,
):
    slots, width = e_buf.shape
    ff = du_buf.shape[1]
    heads = pt[0].shape[0]
    hd = width // heads
    half = slots // 2
    scale = hd ** (-0.5)
    order = list(reversed(range(layers)))
    fused = len(rest) > 0
    grads = rest[0] if fused else summed
    team = None
    if fused:
        team = Total(Fabric(sizes), rest[1:])
        team.greet()

    sources = (n2, slope, n1, q, k, v, pt)
    buffers = (n2_buf, sl_buf, n1_buf, q_buf, k_buf, v_buf, pt_buf)

    def load(which, layer, par):
        return pltpu.make_async_copy(sources[which][layer], buffers[which].at[par], sem_in.at[par, which])

    cot_copy = pltpu.make_async_copy(cot, cot_buf, sem_out.at[0])
    cot_copy.start()
    load(0, order[0], 0).start()
    seg_a = []
    seg_b = []
    seg_c = []
    for l in order:
        seg_a += [(wdown[l], ff // ring_a.shape[1]), (wout[l], width // ring_a.shape[1])]
        seg_b += [(wup[l], width // ring_b.shape[1])]
        seg_c += [(wqkv[l], width // ring_c.shape[1])]
    ra, rb, rc = Ring(ring_a, sem_a, seg_a), Ring(ring_b, sem_b, seg_b), Ring(ring_c, sem_c, seg_c)
    ra.prime()
    load(1, order[0], 0).start()

    chunk = 32
    cot_copy.wait()

    def widen(c, carry):
        rows = pl.ds(pl.multiple_of(c * chunk, chunk), chunk)
        e_buf[rows, :] = cot_buf[rows, :].astype(F32)
        return carry

    lax.fori_loop(0, slots // chunk, widen, 0)

    def norm_back(src, dst, gain_row, n_ref, r_ref):
        def step(c, carry):
            s_in, s_out = carry
            rows = pl.ds(pl.multiple_of(c * chunk, chunk), chunk)
            g = src[rows, :]
            n = n_ref[rows, :].astype(F32)
            ge = g * gain_row
            m1 = jnp.mean(ge, axis=1, keepdims=True)
            m2 = jnp.mean(ge * n, axis=1, keepdims=True)
            dz = r_ref[rows, :] * (ge - m1 - n * m2)
            dst[rows, :] = dz
            z_buf[rows, :] = dz.astype(BF)
            return (s_in + fold8(g), s_out + fold8(dz))

        zero = jnp.zeros((8, width), F32)
        s_in, s_out = lax.fori_loop(0, slots // chunk, step, (zero, zero))
        return jnp.sum(s_in, axis=0, keepdims=True), jnp.sum(s_out, axis=0, keepdims=True)

    for l in range(layers):
        grads[l, 10:13, :] = squares[3 * l : 3 * l + 3, :]
        grads[l, 13:14, :] = squares[3 * layers : 3 * layers + 1, :]
        grads[l, 14:16, :] = jnp.zeros((2, width), F32)
    if fused:
        grads[order[-1], 0:2, :] = jnp.zeros((2, width), F32)

    for step, l in enumerate(order):
        par = step % 2
        last = step == layers - 1
        early = fused and last

        load(0, l, par).wait()
        s_in, s_out = norm_back(e_buf, x_buf, gain[l, 1:2, :], n2_buf.at[par], r2[l])
        grads[l, 4:5, :] = s_in
        grads[l, 9:10, :] = s_out

        if step == 0:
            rb.prime()
            load(2, l, par).start()
        load(1, l, par).wait()
        wide = ring_a.shape[1]

        def down_body(j, w):
            cols = pl.ds(pl.multiple_of(j * wide, wide), wide)
            du = nt(z_buf[...], w) * sl_buf[par, :, cols].astype(F32)
            du_buf[:, cols] = du.astype(BF)
            part = jnp.sum(fold8(du), axis=0, keepdims=True)
            per = width // wide
            grads[l, pl.ds(5 + j // per, 1), pl.ds(pl.multiple_of(lax.rem(j, per) * wide, wide), wide)] = part

        ra.run(ff // wide, down_body)
        if step == 0:
            for which in range(3, 7):
                load(which, l, par).start()
            rc.prime()
        nb = ring_b.shape[1]

        def up_body(j, w):
            cols = pl.ds(pl.multiple_of(j * nb, nb), nb)
            x_buf[:, cols] = x_buf[:, cols] + nt(du_buf[...], w)

        rb.run(width // nb, up_body)
        if step + 1 < layers:
            for which in range(7):
                load(which, order[step + 1], 1 - par).start()

        load(2, l, par).wait()
        s_in, s_out = norm_back(x_buf, x_buf, gain[l, 0:1, :], n1_buf.at[par], r1[l])
        grads[l, 3:4, :] = s_in
        grads[l, 2:3, :] = s_out

        def out_body(j, w):
            cols = pl.ds(pl.multiple_of(j * wide, wide), wide)
            do_buf[:, cols] = nt(z_buf[...], w).astype(BF)

        ra.run(width // wide, out_body)

        for which in range(3, 7):
            load(which, l, par).wait()
        lane = lax.broadcasted_iota(jnp.int32, (1, 2 * hd), 1)
        sides = (lane < hd, lane >= hd)

        def pair(hp, carry):
            cols = pl.ds(pl.multiple_of(hp * 2 * hd, 2 * hd), 2 * hd)
            sum_q = jnp.zeros((8, 2 * hd), F32)
            sum_v = jnp.zeros((8, 2 * hd), F32)
            for b in range(2):
                rows = pl.ds(b * half, half)
                q2, k2, v2, do2 = (r[rows, cols] for r in (q_buf.at[par], k_buf.at[par], v_buf.at[par], do_buf))
                dq = dk = dv = None
                for side in range(2):
                    keep = sides[side]
                    zero = jnp.zeros_like(q2)
                    pb = pt_buf[par, 2 * hp + side, b]
                    dpt = nt(jnp.where(keep, v2, zero), do2)
                    p32 = pb.astype(F32)
                    t = p32 * dpt
                    inner = jnp.sum(fold8(t), axis=0, keepdims=True)
                    ds = (t - p32 * inner).astype(BF)
                    a_v = nn(pb, jnp.where(keep, do2, zero))
                    a_k = nn(ds, jnp.where(keep, q2, zero))
                    a_q = tn(ds, jnp.where(keep, k2, zero))
                    dv = a_v if dv is None else dv + a_v
                    dk = a_k if dk is None else dk + a_k
                    dq = a_q if dq is None else dq + a_q
                dq = dq * scale
                dk = dk * scale
                dp_buf[rows, cols] = dq.astype(BF)
                dp_buf[rows, pl.ds(pl.multiple_of(width + hp * 2 * hd, 2 * hd), 2 * hd)] = dk.astype(BF)
                dp_buf[rows, pl.ds(pl.multiple_of(2 * width + hp * 2 * hd, 2 * hd), 2 * hd)] = dv.astype(BF)
                sum_q = sum_q + fold8(dq)
                sum_v = sum_v + fold8(dv)
            terms = team.late if early else grads.at[l]
            terms[0:1, cols] = jnp.sum(sum_q, axis=0, keepdims=True)
            terms[1:2, cols] = jnp.sum(sum_v, axis=0, keepdims=True)
            return carry

        if early:
            team.met()
            team.spread(grads)
            lax.fori_loop(0, 3, pair, 0)
            team.along()
            lax.fori_loop(3, 6, pair, 0)
            team.back(summed)
            lax.fori_loop(6, heads // 2, pair, 0)
            team.late_spread()
        else:
            lax.fori_loop(0, heads // 2, pair, 0)
        nc = ring_c.shape[1]

        def qkv_body(j, w):
            cols = pl.ds(pl.multiple_of(j * nc, nc), nc)
            e_buf[:, cols] = x_buf[:, cols] + nt(dp_buf[...], w)
            if last:
                pltpu.make_async_copy(e_buf.at[:, cols], dh_out.at[:, cols], sem_out.at[0]).start()

        rc.run(width // nc // 2, qkv_body)
        if early:
            team.late_along()
        rc.run(width // nc // 2, qkv_body, width // nc // 2)

    if fused:
        summed[order[-1], 0:2, :] = team.close()
    for j in range(width // nc):
        cols = pl.ds(j * nc, nc)
        pltpu.make_async_copy(e_buf.at[:, cols], dh_out.at[:, cols], sem_out.at[0]).wait()


def backward(sizes, cot, gain, squares, kept):
    slots, width = cot.shape
    layers, heads = kept[1].shape[:2]
    ff = kept[2].shape[2]
    half = slots // 2
    hbm = pl.BlockSpec(memory_space=pl.ANY)
    vm = pl.BlockSpec(memory_space=pltpu.VMEM)
    ta, tb, tc = min(512, width), min(256, width), min(256, width)
    team = []
    params = {}
    if sizes == KERNEL_MESH:
        plane, line = 2 * sizes[0] * sizes[1], sizes[2]
        team = [
            pltpu.VMEM((layers, 16, width), F32),
            pltpu.VMEM((plane, layers, 16, width // plane), F32),
            pltpu.VMEM((line, layers, 16, width // plane), F32),
            pltpu.VMEM((layers, 16, width // plane), F32),
            pltpu.VMEM((2, width), F32),
            pltpu.VMEM((plane, 2, width), F32),
            pltpu.VMEM((line, 2, width), F32),
            pltpu.SemaphoreType.DMA((5,)),
            pltpu.SemaphoreType.DMA((5,)),
        ]
        params = dict(collective_id=1, has_side_effects=True)
    return pl.pallas_call(
        functools.partial(backward_kernel, layers, sizes),
        out_shape=(
            jax.ShapeDtypeStruct((slots, width), F32),
            jax.ShapeDtypeStruct((layers, 16, width), F32),
        ),
        in_specs=[hbm, vm, vm] + [hbm] * 5 + [vm] * 2 + [hbm] * 4,
        out_specs=(hbm, vm),
        scratch_shapes=[
            pltpu.VMEM((slots, width), F32),
            pltpu.VMEM((slots, width), F32),
            pltpu.VMEM((slots, width), BF),
            pltpu.VMEM((slots, ff), BF),
            pltpu.VMEM((slots, 3 * width), BF),
            pltpu.VMEM((slots, width), BF),
            pltpu.VMEM((slots, width), BF),
        ]
        + [pltpu.VMEM((2, slots, width), BF)] * 3
        + [
            pltpu.VMEM((2, heads, 2, half, half), BF),
            pltpu.VMEM((2, slots, ff), BF),
            pltpu.VMEM((2, slots, width), BF),
            pltpu.VMEM((2, slots, width), BF),
            pltpu.VMEM((4, ta, width), BF),
            pltpu.VMEM((3, tb, ff), BF),
            pltpu.VMEM((3, tc, 3 * width), BF),
            pltpu.SemaphoreType.DMA((4,)),
            pltpu.SemaphoreType.DMA((3,)),
            pltpu.SemaphoreType.DMA((3,)),
            pltpu.SemaphoreType.DMA((2, 7)),
            pltpu.SemaphoreType.DMA((1,)),
        ]
        + team,
        compiler_params=pltpu.CompilerParams(vmem_limit_bytes=67000000, **params),
        name="backward",
    )(cot, gain, squares, *kept)


class Relay:
    def __init__(self, fabric, kinds, per, count, sems):
        self.fab, self.kinds, self.per, self.count = fabric, kinds, per, count
        self.send, self.recv = sems
        at = fabric.at
        self.pair = lax.div(at["z"], 2) * 2
        self.other = 2 - self.pair
        self.mate = self.pair + 1 - lax.rem(at["z"], 2)
        self.inner = jnp.logical_or(at["z"] == 1, at["z"] == 2)

    def wait(self, sem, blocks):
        _, _, _, full, rows, cols = self.kinds[0]
        part = full.at[0, pl.ds(0, blocks * rows), pl.ds(0, cols // 2)]
        pltpu.make_async_copy(part, part, sem).wait()

    def each(self, t, act):
        l = lax.div(t, self.per)
        j = t - l * self.per
        for first, number, own, full, rows, cols in self.kinds:

            @pl.when(jnp.logical_and(j >= first, j < first + number))
            def _(first=first, own=own, full=full, rows=rows, cols=cols):
                for piece in range(2):
                    col = pl.multiple_of((j - first) * cols + piece * (cols // 2), cols // 2)
                    act(l, own, full, rows, pl.ds(col, cols // 2), piece)

    def push(self, t, piece, sem, device, src, dst):
        pltpu.make_async_remote_copy(
            src_ref=src,
            dst_ref=dst,
            send_sem=self.send.at[2 * t + piece, sem],
            recv_sem=self.recv.at[2 * t + piece, sem],
            device_id=device,
            device_id_type=pl.DeviceIdType.MESH,
        ).start()

    def stage(self, s, t):
        fab = self.fab
        at = fab.at
        partner = fab.device(c=1 - at["c"])

        @pl.when(jnp.logical_and(t >= 0, t < self.count))
        def _():
            for piece in range(2):
                if s == 1:
                    self.wait(self.recv.at[2 * t + piece, 0], 1)
                elif s == 2:
                    self.wait(self.recv.at[2 * t + piece, 1], 2)
                elif s == 3:
                    pl.when(self.inner)(lambda piece=piece: self.wait(self.recv.at[2 * t + piece, 2], 4))
                elif s == 4:
                    pl.when(jnp.logical_not(self.inner))(
                        lambda piece=piece: self.wait(self.recv.at[2 * t + piece, 2], 4)
                    )
                    self.wait(self.recv.at[2 * t + piece, 5], 4)
                elif s == 5:
                    self.wait(self.recv.at[2 * t + piece, 3], 4)

            def act(l, own, full, rows, cols, piece):
                u, v = (("x", "y"), ("y", "x"))[piece]

                def view(first, blocks):
                    return full.at[l, pl.ds(pl.multiple_of(first * rows, rows), blocks * rows), cols]

                def out(sem, device, runs):
                    for first, blocks in runs:
                        self.push(t, piece, sem, device, view(first, blocks), view(first, blocks))

                def runs(z, **moved):
                    return [(fab.block(**{u: each, "z": z, **moved}), 2) for each in range(2)]

                across = fab.device(**{v: 1 - at[v]})
                beyond = {v: 1 - at[v]}
                if s == 0:
                    mine = view(fab.block(), 1)
                    self.push(t, piece, 0, fab.device(z=self.mate), own.at[l, :, cols], mine)
                    self.push(t, piece, 4, partner, own.at[l, :, cols], mine)
                elif s == 1:
                    out(1, fab.device(**{u: 1 - at[u]}), [(fab.block(z=self.pair), 2)])
                    out(4, partner, [(fab.block(z=self.mate), 1)])
                elif s == 2:
                    pl.when(self.inner)(lambda: out(2, fab.device(z=3 - at["z"]), runs(self.pair)))
                    out(5, across, runs(self.pair))
                    out(4, partner, [(fab.block(**{u: 1 - at[u], "z": self.pair}), 2)])
                elif s == 3:

                    @pl.when(self.inner)
                    def _():
                        out(2, fab.device(z=self.mate), runs(self.other))
                        out(3, across, runs(self.other))
                        out(4, partner, runs(self.other))

                elif s == 4:

                    @pl.when(jnp.logical_not(self.inner))
                    def _():
                        out(3, across, runs(self.other))
                        out(4, partner, runs(self.other))

                    out(4, partner, runs(self.pair, **beyond))
                else:
                    out(4, partner, runs(self.other, **beyond))

            self.each(t, act)

    def finish(self, t):
        for piece in range(2):
            self.wait(self.recv.at[2 * t + piece, 4], 16)

    def drain(self, t):
        for piece in range(2):
            for sem, blocks in ((0, 1), (1, 2), (3, 4), (4, 16), (5, 4)):
                self.wait(self.send.at[2 * t + piece, sem], blocks)
            pl.when(self.inner)(lambda piece=piece: self.wait(self.send.at[2 * t + piece, 2], 8))


LEADS = (11, 9, 7, 5, 3, 1)


def forward_kernel(layers, sizes, *refs):
    (lens, tok, cot, gain, b_qv, b_out, b_ln, b_up, b_down, s_qkv, s_out, s_up, s_down) = refs[:13]
    (act, squares, back, cot_o, qkv_o, pt_o, sl_o, n1_o, n2_o, r1_o, r2_o, f_qkv, f_out, f_up, f_down) = refs[13:28]
    (
        h_buf, hb_buf, qkv_buf, mix_buf, gu_buf, f_buf, pt_buf, sl_buf, n_buf,
        ring_w, ring_t, own_qkv, own_out, own_up, own_down, turn, vcol, vrow,
        sem_send, sem_recv, sem_own, sem_ring, sem_save,
    ) = refs[28:]
    slots, width = tok.shape
    ff = gu_buf.shape[1]
    heads = pt_buf.shape[0]
    hd = width // heads
    half = slots // 2
    scale = hd ** (-0.5)
    tall = ring_t.shape[2]
    fab = Fabric(sizes)

    shards = ((s_qkv, own_qkv, f_qkv), (s_out, own_out, f_out), (s_up, own_up, f_up), (s_down, own_down, f_down))
    for at, (src, buf, _) in enumerate(shards):
        pltpu.make_async_copy(src, buf, sem_own.at[at]).start()
    pltpu.make_async_copy(cot, mix_buf, sem_save.at[3]).start()
    barrier = pltpu.get_barrier_semaphore()
    around = [fab.device(**{axis: peer}) for axis in ("z", "x", "y", "c") for peer in fab.peers(axis)]
    for device in around:
        pl.semaphore_signal(barrier, inc=1, device_id=device, device_id_type=pl.DeviceIdType.MESH)
    pl.semaphore_wait(barrier, len(around))

    ups, downs = ff // width, width // tall
    kinds = (
        (0, 3, s_qkv, f_qkv, s_qkv.shape[1], width),
        (3, 1, s_out, f_out, s_out.shape[1], width),
        (4, ups, s_up, f_up, s_up.shape[1], width),
        (4 + ups, downs, s_down, f_down, s_down.shape[1], tall),
    )
    per = 4 + ups + downs
    total = layers * per
    relay = Relay(fab, kinds, per, total, (sem_send, sem_recv))

    def save(src, dst, key):
        pltpu.make_async_copy(src, dst, sem_save.at[key]).start()

    def free(src, dst, key, when):
        pl.when(when)(lambda: pltpu.make_async_copy(src, dst, sem_save.at[key]).wait())

    chunk = 32
    steps = slots // chunk

    def rows_of(c):
        return pl.ds(pl.multiple_of(c * chunk, chunk), chunk)

    def tiles(w, lhs, count, body, tile=256):
        def step(j, carry):
            cols = pl.ds(pl.multiple_of(j * tile, tile), tile)
            body(cols, nn(lhs[...], w[:, cols]), j * tile)
            return carry

        lax.fori_loop(0, count // tile, step, 0)

    def norm(l, which, bias_row, base, branch, n_dst, r_dst):
        zero = jnp.zeros((8, width), F32)
        gain_row = gain[l, which : which + 1, :]
        shift_row = b_ln[l, which : which + 1, :]

        def step(c, carry):
            s_h, s_a = carry
            rows = rows_of(c)
            a = branch[rows, :] + bias_row
            h = base[rows, :]
            z = h + a
            mean = jnp.mean(z, axis=1, keepdims=True)
            centred = z - mean
            var = jnp.mean(centred * centred, axis=1, keepdims=True)
            inv = lax.rsqrt(var + 1e-06)
            n = centred * inv
            y = n * gain_row + shift_row
            base[rows, :] = y
            hb_buf[rows, :] = y.astype(BF)
            n_dst[rows, :] = n.astype(BF)
            r_dst[rows, :] = inv
            ok = vcol[rows, :]
            return s_h + fold8(ok * h * h), s_a + fold8(ok * a * a)

        return lax.fori_loop(0, steps, step, (zero, zero))

    def attention():
        lane = lax.broadcasted_iota(jnp.int32, (1, 2 * hd), 1)
        sides = (lane < hd, lane >= hd)

        def pair(hp, carry):
            cols = pl.ds(pl.multiple_of(hp * 2 * hd, 2 * hd), 2 * hd)
            for b in range(2):
                rows = pl.ds(b * half, half)
                q2, k2, v2 = qkv_buf[0, rows, cols], qkv_buf[1, rows, cols], qkv_buf[2, rows, cols]
                mixed = None
                for side in range(2):
                    keep = sides[side]
                    zero = jnp.zeros_like(q2)
                    st = nt(jnp.where(keep, k2, zero), q2) * scale
                    if b == 1:
                        st = jnp.where(vcol[rows, :] == vrow[:, rows], st, -1e30)
                    top = jnp.max(st, axis=0, keepdims=True)
                    ex = jnp.exp(st - top)
                    p = (ex * (1.0 / jnp.sum(ex, axis=0, keepdims=True))).astype(BF)
                    pt_buf[2 * hp + side, b] = p
                    o = tn(p, jnp.where(keep, v2, zero))
                    mixed = o if mixed is None else mixed + o
                mix_buf[rows, cols] = mixed.astype(BF)
            return carry

        lax.fori_loop(0, heads // 2, pair, 0)

    def compute(t):
        l = lax.div(t, per)
        j = t - l * per
        slot = lax.rem(t, 2)
        later = l > 0

        @pl.when(j < 3)
        def _():
            free(qkv_buf.at[j], qkv_o.at[0, j], j, later)
            keep = (j != 1).astype(F32)

            def body(cols, t, first):
                bias = b_qv[l, pl.ds(lax.div(j, 2), 1), cols] * keep
                qkv_buf[j, :, cols] = (t + bias).astype(BF)

            tiles(ring_w.at[slot], hb_buf, width, body)
            save(qkv_buf.at[j], qkv_o.at[l, j], j)

            @pl.when(j == 2)
            def _():
                free(pt_buf, pt_o.at[0], 3, later)
                attention()
                save(pt_buf, pt_o.at[l], 3)

        @pl.when(j == 3)
        def _():
            def body(cols, t, first):
                f_buf[:, cols] = t

            tiles(ring_w.at[slot], mix_buf, width, body)
            free(n_buf.at[0], n1_o.at[0], 4, later)
            s_h, s_a = norm(l, 0, b_out[pl.ds(l, 1), :], h_buf, f_buf, n_buf.at[0], r1_o.at[l])
            squares[pl.ds(3 * l, 1), :] = jnp.sum(s_h, axis=0, keepdims=True)
            squares[pl.ds(3 * l + 1, 1), :] = jnp.sum(s_a, axis=0, keepdims=True)
            save(n_buf.at[0], n1_o.at[l], 4)

        @pl.when(jnp.logical_and(j >= 4, j < 4 + ups))
        def _():
            part = j - 4
            par = lax.rem(part, 2)
            start = pl.multiple_of(part * width, width)
            free(sl_buf.at[par], sl_o.at[0, :, pl.ds(0, width)], 6 + par, jnp.logical_or(later, part >= 2))

            def body(cols, t, first):
                wide = pl.ds(pl.multiple_of(part * width + first, 256), 256)
                u = t + b_up[pl.ds(l, 1), wide]
                phi = 0.5 * (1.0 + lax.erf(u * 0.7071067811865476))
                sl_buf[par, :, cols] = (phi + u * (jnp.exp(-0.5 * u * u) * 0.3989422804014327)).astype(BF)
                gu_buf[:, wide] = (u * phi).astype(BF)

            tiles(ring_w.at[slot], hb_buf, width, body)
            save(sl_buf.at[par], sl_o.at[l, :, pl.ds(start, width)], 6 + par)

        @pl.when(j >= 4 + ups)
        def _():
            part = j - 4 - ups
            f_buf[:, pl.ds(pl.multiple_of(part * tall, tall), tall)] = nn(gu_buf[...], ring_t[slot])

            @pl.when(part == downs - 1)
            def _():
                free(n_buf.at[1], n2_o.at[0], 5, True)
                _, s_f = norm(l, 1, b_down[pl.ds(l, 1), :], h_buf, f_buf, n_buf.at[1], r2_o.at[l])
                squares[pl.ds(3 * l + 2, 1), :] = jnp.sum(s_f, axis=0, keepdims=True)
                save(n_buf.at[1], n2_o.at[l], 5)

    def ring_start(t):
        l = lax.div(t, per)
        j = t - l * per
        slot = lax.rem(t, 2)
        for first, number, _, full, _, cols in kinds:
            buf = ring_t if cols == tall else ring_w

            @pl.when(jnp.logical_and(j >= first, j < first + number))
            def _(first=first, full=full, cols=cols, buf=buf):
                src = full.at[l, :, pl.ds(pl.multiple_of((j - first) * cols, cols), cols)]
                pltpu.make_async_copy(src, buf.at[slot], sem_ring.at[slot]).start()

    def ring_wait(t):
        slot = lax.rem(t, 2)
        pltpu.make_async_copy(f_out.at[0], ring_w.at[slot], sem_ring.at[slot]).wait()

    for t in range(LEADS[0] - LEADS[1]):
        relay.stage(0, jnp.int32(t))
    for at, (src, buf, _) in enumerate(shards):
        pltpu.make_async_copy(src, buf, sem_own.at[at]).wait()
    placed = []
    for at, (_, buf, full) in enumerate(shards):
        rows = buf.shape[1]
        for l in range(layers):
            dst = full.at[l, pl.ds(pl.multiple_of(fab.block() * rows, rows), rows)]
            placed.append(pltpu.make_async_copy(buf.at[l], dst, sem_own.at[4 + at * layers + l]))
            placed[-1].start()

    first, second = lens[0, 0], lens[0, 1]
    shift = jnp.where(first == half, 0, first)
    back[0] = slots - shift

    def source(slot):
        return jnp.where(slot + shift >= slots, slot + shift - slots, slot + shift)

    vcol[...] = (source(lax.broadcasted_iota(jnp.int32, (slots, 1), 0)) < first + second).astype(F32)
    vrow[...] = (source(lax.broadcasted_iota(jnp.int32, (1, slots), 1)) < first + second).astype(F32)

    def turning(c, carry):
        rows = rows_of(c)
        slot = lax.broadcasted_iota(jnp.int32, (chunk, slots), 0) + c * chunk
        turn[rows, :] = (source(slot) == lax.broadcasted_iota(jnp.int32, (chunk, slots), 1)).astype(F32).astype(BF)
        return carry

    lax.fori_loop(0, steps, turning, 0)

    def turned(dst, src):
        def body(j, carry):
            cols = pl.ds(pl.multiple_of(j * 256, 256), 256)
            dst(cols, nn(turn[...], src[:, cols]))
            return carry

        lax.fori_loop(0, width // 256, body, 0)

    def put_tokens(cols, t):
        h_buf[:, cols] = t
        hb_buf[:, cols] = t.astype(BF)

    def put_cotangent(cols, t):
        n_buf[1, :, cols] = (t * vcol[...]).astype(BF)

    turned(put_tokens, tok)
    for copy in placed:
        copy.wait()

    def step(i, carry):
        at = i - LEADS[1]
        for s, lead in enumerate(LEADS):
            relay.stage(s, at + lead)

        @pl.when(i == 4)
        def _():
            pltpu.make_async_copy(cot, mix_buf, sem_save.at[3]).wait()
            turned(put_cotangent, mix_buf)
            save(n_buf.at[1], cot_o, 5)

        pl.when(jnp.logical_and(at >= 1, at <= total))(lambda: ring_wait(at - 1))

        @pl.when(jnp.logical_and(at >= 0, at < total))
        def _():
            relay.finish(at)
            ring_start(at)

        pl.when(at >= 1)(lambda: relay.drain(at - 1))
        pl.when(at >= 1)(lambda: compute(at - 1))
        return carry

    lax.fori_loop(0, total + 1 + LEADS[1], step, 0)
    pltpu.make_async_copy(hb_buf, act, sem_own.at[0]).start()
    here = jnp.sum(vcol[...], axis=0, keepdims=True)
    squares[3 * layers :, :] = jnp.broadcast_to(here, (squares.shape[0] - 3 * layers, width))
    for part in range(3):
        free(qkv_buf.at[part], qkv_o.at[0, part], part, True)
    free(pt_buf, pt_o.at[0], 3, True)
    free(n_buf.at[0], n1_o.at[0], 4, True)
    free(n_buf.at[1], n2_o.at[0], 5, True)
    for par in range(2):
        free(sl_buf.at[par], sl_o.at[0, :, pl.ds(0, width)], 6 + par, True)
    pltpu.make_async_copy(hb_buf, act, sem_own.at[0]).wait()


def forward(sizes, lengths, tokens, cotangent, gain, b_qv, b_out, b_ln, b_up, b_down, s_qkv, s_out, s_up, s_down):
    slots, width = tokens.shape
    layers = s_qkv.shape[0]
    ff = s_up.shape[2]
    half = slots // 2
    tall = width * width // ff
    hbm = pl.BlockSpec(memory_space=pl.ANY)
    vm = pl.BlockSpec(memory_space=pltpu.VMEM)
    chunks = layers * (4 + ff // width + width // tall)
    outs = [
        ((slots, width), BF, hbm),
        ((8, width), F32, vm),
        ((1,), jnp.int32, pl.BlockSpec(memory_space=pltpu.SMEM)),
        ((slots, width), BF, hbm),
        ((layers, 3, slots, width), BF, hbm),
        ((layers, HEADS, 2, half, half), BF, hbm),
        ((layers, slots, ff), BF, hbm),
        ((layers, slots, width), BF, hbm),
        ((layers, slots, width), BF, hbm),
        ((layers, slots, 1), F32, vm),
        ((layers, slots, 1), F32, vm),
        ((layers, width, 3 * width), BF, hbm),
        ((layers, width, width), BF, hbm),
        ((layers, width, ff), BF, hbm),
        ((layers, ff, width), BF, hbm),
    ]
    result = pl.pallas_call(
        functools.partial(forward_kernel, layers, sizes),
        out_shape=tuple(jax.ShapeDtypeStruct(shape, kind) for shape, kind, _ in outs),
        in_specs=[pl.BlockSpec(memory_space=pltpu.SMEM), vm, hbm] + [vm] * 6 + [hbm] * 4,
        out_specs=tuple(spec for _, _, spec in outs),
        scratch_shapes=[
            pltpu.VMEM((slots, width), F32),
            pltpu.VMEM((slots, width), BF),
            pltpu.VMEM((3, slots, width), BF),
            pltpu.VMEM((slots, width), BF),
            pltpu.VMEM((slots, ff), BF),
            pltpu.VMEM((slots, width), F32),
            pltpu.VMEM((HEADS, 2, half, half), BF),
            pltpu.VMEM((2, slots, width), BF),
            pltpu.VMEM((2, slots, width), BF),
            pltpu.VMEM((2, width, width), BF),
            pltpu.VMEM((2, ff, tall), BF),
            pltpu.VMEM(s_qkv.shape, BF),
            pltpu.VMEM(s_out.shape, BF),
            pltpu.VMEM(s_up.shape, BF),
            pltpu.VMEM(s_down.shape, BF),
            pltpu.VMEM((slots, slots), BF),
            pltpu.VMEM((slots, 1), F32),
            pltpu.VMEM((1, slots), F32),
            pltpu.SemaphoreType.DMA((2 * chunks, 6)),
            pltpu.SemaphoreType.DMA((2 * chunks, 6)),
            pltpu.SemaphoreType.DMA((4 + 4 * layers,)),
            pltpu.SemaphoreType.DMA((2,)),
            pltpu.SemaphoreType.DMA((8,)),
        ],
        compiler_params=pltpu.CompilerParams(vmem_limit_bytes=62 << 20, collective_id=0, has_side_effects=True),
        name="forward",
    )(lengths, tokens, cotangent, gain, b_qv, b_out, b_ln, b_up, b_down, s_qkv, s_out, s_up, s_down)
    return result[0], result[1], result[2], result[3], list(result[4:])


def normalize(stream, gain_row, shift_row):
    mean_row = jnp.mean(stream, axis=-1, keepdims=True)
    centred = stream - mean_row
    variance = jnp.mean(centred * centred, axis=-1, keepdims=True)
    inv_std = lax.rsqrt(variance + 1e-06)
    normed = centred * inv_std
    return normed * gain_row + shift_row, normed, inv_std


def turned_by(a, by):
    return lax.dynamic_slice_in_dim(jnp.concatenate([a, a], axis=0), by, a.shape[0], axis=0)


def forward_apart(lengths, tokens, cotangent, gain, b_qv, b_out, b_ln, b_up, b_down, *shards):
    slots, width = tokens.shape
    shift = jnp.where(lengths[0, 0] == slots // 2, 0, lengths[0, 0])
    place = lax.rem(jnp.arange(slots, dtype=jnp.int32) + shift, slots)
    vcol = (place < lengths[0, 0] + lengths[0, 1]).astype(F32)[:, None]
    tokens = turned_by(tokens, shift)
    masked = turned_by(cotangent, shift) * vcol.astype(BF)
    layers = b_out.shape[0]
    half = slots // 2
    hd = width // HEADS
    blocks = vcol.reshape(2, half)
    same = blocks[:, :, None] == blocks[:, None, :]
    stream = tokens.astype(F32)
    kept = []
    squares = []
    for l in range(layers):
        mats = [lax.all_gather(w[l], AXES, axis=0, tiled=True) for w in shards]
        projected = nn(stream.astype(BF), mats[0])
        q = (projected[:, :width] + b_qv[l, 0]).astype(BF)
        k = projected[:, width : 2 * width].astype(BF)
        v = (projected[:, 2 * width :] + b_qv[l, 1]).astype(BF)
        q4, k4, v4 = (a.reshape(2, half, HEADS, hd) for a in (q, k, v))
        st = jnp.einsum("bqhd,bkhd->hbkq", q4, k4, preferred_element_type=F32) * hd ** (-0.5)
        st = jnp.where(same[None], st, -1e30)
        ex = jnp.exp(st - jnp.max(st, axis=2, keepdims=True))
        pt = (ex / jnp.sum(ex, axis=2, keepdims=True)).astype(BF)
        mixed = jnp.einsum("hbkq,bkhd->bqhd", pt, v4, preferred_element_type=F32).reshape(slots, width).astype(BF)
        branch = nn(mixed, mats[1]) + b_out[l]
        x1, n1, r1 = normalize(stream + branch, gain[l, 0], b_ln[l, 0])
        u = nn(x1.astype(BF), mats[2]) + b_up[l]
        phi = 0.5 * (1.0 + lax.erf(u * 0.7071067811865476))
        slope = (phi + u * (jnp.exp(-0.5 * u * u) * 0.3989422804014327)).astype(BF)
        ffn = nn((u * phi).astype(BF), mats[3]) + b_down[l]
        nxt, n2, r2 = normalize(x1 + ffn, gain[l, 1], b_ln[l, 1])
        squares += [jnp.sum(vcol * a * a, axis=0) for a in (stream, branch, ffn)]
        kept.append((jnp.stack([q, k, v]), pt, slope, n1.astype(BF), n2.astype(BF), r1, r2, *mats))
        stream = nxt
    here = jnp.broadcast_to(jnp.sum(vcol), (width,))
    return stream.astype(BF), jnp.stack(squares + [here] * (8 - 3 * layers)), (slots - shift)[None], masked, [jnp.stack(a) for a in zip(*kept)]


def local(
    sizes, tokens, lengths, w_qkv, w_out, w_up, w_down, ln_gain, bias_qv, bias_out, ln_bias, bias_up, bias_down, cotangent
):
    slots, width = tokens.shape
    layers = w_qkv.shape[0]
    run = functools.partial(forward, sizes) if sizes == KERNEL_MESH else forward_apart
    act, squares, back, cot, kept = run(
        lengths, tokens, cotangent, ln_gain, bias_qv, bias_out, ln_bias, bias_up, bias_down, w_qkv, w_out, w_up, w_down
    )
    dh, whole = backward(sizes, cot, ln_gain, squares, kept)
    if sizes != KERNEL_MESH:
        whole = lax.psum(whole, AXES)
    back = back[0].astype(jnp.uint32)
    return (
        turned_by(act, back),
        turned_by(dh, back),
        whole[:, 0:2],
        whole[:, 2],
        whole[:, 3:5],
        whole[:, 5:9].reshape(layers, -1),
        whole[:, 9],
        jnp.sqrt(jnp.sum(whole[:, 10:13], axis=2) / (whole[:, 13, 0:1] * width)),
    )


def solution(mesh):
    pairs = mesh.shape["dp"] // 2
    ny = next(n for n in range(math.isqrt(pairs), 0, -1) if pairs % n == 0)
    sizes = (ny, pairs // ny, mesh.shape["shard"])
    rows = P(AXES, None)
    weight = P(None, AXES, None)
    in_specs = (rows, rows, weight, weight, weight, weight, P(), P(), P(), P(), P(), P(), rows)
    out_specs = (rows, rows, P(), P(), P(), P(), P(), P())
    return jax.shard_map(
        functools.partial(local, sizes), mesh=mesh, in_specs=in_specs, out_specs=out_specs, check_vma=False
    )
```

```python
import functools
import math

import jax
import jax.numpy as jnp
from jax import lax
from jax.experimental import pallas as pl
from jax.experimental.pallas import tpu as pltpu
from jax.sharding import PartitionSpec as P

BF = jnp.bfloat16
F32 = jnp.float32
HEADS = 16
AXES = ("dp", "shard")
KERNEL_MESH = (2, 2, 4)


def nt(a, b):
    return lax.dot_general(a, b, (((1,), (1,)), ((), ())), preferred_element_type=F32)


def nn(a, b):
    return lax.dot_general(a, b, (((1,), (0,)), ((), ())), preferred_element_type=F32)


def tn(a, b):
    return lax.dot_general(a, b, (((0,), (0,)), ((), ())), preferred_element_type=F32)


def fold8(t):
    return jnp.sum(t.reshape(t.shape[0] // 8, 8, t.shape[1]), axis=0)


class Ring:
    def __init__(self, buf, sem, segments):
        self.buf, self.sem, self.segments = buf, sem, segments
        self.slots, self.rows = buf.shape[0], buf.shape[1]
        self.base = 0

    def fetch(self, at):
        slot = lax.rem(at, self.slots)
        first = 0
        for ref, count in self.segments:
            if isinstance(at, int):
                if first <= at < first + count:
                    row = (at - first) * self.rows
                    pltpu.make_async_copy(ref.at[pl.ds(row, self.rows)], self.buf.at[slot], self.sem.at[slot]).start()
            else:

                @pl.when(jnp.logical_and(at >= first, at < first + count))
                def _(ref=ref, first=first):
                    row = pl.multiple_of((at - first) * self.rows, self.rows)
                    pltpu.make_async_copy(ref.at[pl.ds(row, self.rows)], self.buf.at[slot], self.sem.at[slot]).start()

            first += count

    def prime(self):
        for at in range(self.slots):
            self.fetch(at)

    def run(self, count, body, first=0):
        base = self.base

        def step(j, carry):
            at = base + j
            slot = lax.rem(at, self.slots)
            pltpu.make_async_copy(self.segments[0][0].at[pl.ds(0, self.rows)], self.buf.at[slot], self.sem.at[slot]).wait()
            body(first + j, self.buf[slot])
            self.fetch(at + self.slots)
            return carry

        lax.fori_loop(0, count, step, 0)
        self.base = base + count


class Fabric:
    def __init__(self, sizes):
        ny, nx, nz = sizes
        dp = lax.axis_index("dp")
        self.size = {"y": ny, "x": nx, "z": nz, "c": 2}
        self.at = {"z": lax.axis_index("shard"), "c": lax.rem(dp, 2), "x": lax.rem(dp // 2, nx), "y": dp // (2 * nx)}

    def device(self, **moved):
        at = {**self.at, **moved}
        return ((at["y"] * self.size["x"] + at["x"]) * 2 + at["c"], at["z"])

    def peers(self, axis):
        n = self.size[axis]
        return [lax.rem(self.at[axis] + step, n) for step in range(1, n)]

    def block(self, **moved):
        at = {**self.at, **moved}
        return ((at["y"] * self.size["x"] + at["x"]) * 2 + at["c"]) * self.size["z"] + at["z"]


class Total:
    def __init__(self, fabric, rest):
        (self.plane, self.line, self.mine, self.late, self.late_plane, self.late_line, self.send, self.recv) = rest
        self.fab = fabric
        self.me = lax.axis_index("dp")
        self.z = fabric.at["z"]
        self.n, self.nz = self.plane.shape[0], fabric.size["z"]
        self.mates = [(lax.rem(self.me + step, self.n), self.z) for step in range(1, self.n)]
        self.others = [(self.me, lax.rem(self.z + step, self.nz)) for step in range(1, self.nz)]

    def greet(self):
        barrier = pltpu.get_barrier_semaphore()
        for device in self.mates + self.others:
            pl.semaphore_signal(barrier, inc=1, device_id=device, device_id_type=pl.DeviceIdType.MESH)

    def met(self):
        pl.semaphore_wait(pltpu.get_barrier_semaphore(), len(self.mates) + len(self.others))

    def push(self, src, dst, sem, device):
        pltpu.make_async_remote_copy(
            src_ref=src,
            dst_ref=dst,
            send_sem=self.send.at[sem],
            recv_sem=self.recv.at[sem],
            device_id=device,
            device_id_type=pl.DeviceIdType.MESH,
        ).start()

    def wait(self, part, sems):
        for sem in sems:
            pltpu.make_async_copy(part, part, sem).wait()

    def share(self, ref, at):
        cols = ref.shape[2] // self.n
        return ref.at[:, :, pl.ds(pl.multiple_of(at * cols, cols), cols)]

    def spread(self, part):
        self.plane[self.me] = self.share(part, self.me)[...]
        for device in self.mates:
            self.push(self.share(part, device[0]), self.plane.at[self.me], 0, device)

    def along(self):
        self.wait(self.plane.at[pl.ds(0, self.n - 1)], (self.send.at[0], self.recv.at[0]))
        self.line[self.z] = self.added(self.plane)
        for device in self.others:
            self.push(self.line.at[self.z], self.line.at[self.z], 1, device)

    def back(self, out):
        self.wait(self.line.at[pl.ds(0, self.nz - 1)], (self.send.at[1], self.recv.at[1]))
        total = self.added(self.line)
        self.mine[...] = total
        self.share(out, self.me)[...] = total
        for device in self.mates:
            self.push(self.mine, self.share(out, self.me), 2, device)

    def late_spread(self):
        self.late_plane[self.me] = self.late[...]
        for device in self.mates:
            self.push(self.late, self.late_plane.at[self.me], 3, device)

    def late_along(self):
        self.wait(self.late_plane.at[pl.ds(0, self.n - 1)], (self.send.at[3], self.recv.at[3]))
        self.late_line[self.z] = self.added(self.late_plane)
        for device in self.others:
            self.push(self.late_line.at[self.z], self.late_line.at[self.z], 4, device)

    def close(self):
        self.wait(self.late_line.at[pl.ds(0, self.nz - 1)], (self.send.at[4], self.recv.at[4]))
        self.wait(self.plane.at[pl.ds(0, self.n - 1)], (self.send.at[2], self.recv.at[2]))
        return self.added(self.late_line)

    def added(self, ref):
        total = ref[0]
        for at in range(1, ref.shape[0]):
            total = total + ref[at]
        return total


def backward_kernel(layers, sizes, *refs):
    cot, gain, squares = refs[:3]
    qkv, pt, slope, n1, n2, r1, r2, wqkv, wout, wup, wdown = [
        [ref.at[l] for l in range(layers)] for ref in refs[3:14]
    ]
    q, k, v = [[ref.at[part] for ref in qkv] for part in range(3)]
    backward_body(
        layers, sizes, cot, gain, squares, q, k, v, pt, slope, n1, n2, r1, r2, wqkv, wout, wup, wdown, *refs[14:]
    )


def backward_body(
    layers, sizes, cot, gain, squares, q, k, v, pt, slope, n1, n2, r1, r2, wqkv, wout, wup, wdown,
    dh_out, summed,
    e_buf, x_buf, z_buf, du_buf, dp_buf, do_buf, cot_buf,
    q_buf, k_buf, v_buf, pt_buf, sl_buf, n1_buf, n2_buf,
    ring_a, ring_b, ring_c, sem_a, sem_b, sem_c, sem_in, sem_out, *rest,
):
    slots, width = e_buf.shape
    ff = du_buf.shape[1]
    heads = pt[0].shape[0]
    hd = width // heads
    half = slots // 2
    scale = hd ** (-0.5)
    order = list(reversed(range(layers)))
    fused = len(rest) > 0
    grads = rest[0] if fused else summed
    team = None
    if fused:
        team = Total(Fabric(sizes), rest[1:])
        team.greet()

    sources = (n2, slope, n1, q, k, v, pt)
    buffers = (n2_buf, sl_buf, n1_buf, q_buf, k_buf, v_buf, pt_buf)

    def load(which, layer, par):
        return pltpu.make_async_copy(sources[which][layer], buffers[which].at[par], sem_in.at[par, which])

    cot_copy = pltpu.make_async_copy(cot, cot_buf, sem_out.at[0])
    cot_copy.start()
    load(0, order[0], 0).start()
    seg_a = []
    seg_b = []
    seg_c = []
    for l in order:
        seg_a += [(wdown[l], ff // ring_a.shape[1]), (wout[l], width // ring_a.shape[1])]
        seg_b += [(wup[l], width // ring_b.shape[1])]
        seg_c += [(wqkv[l], width // ring_c.shape[1])]
    ra, rb, rc = Ring(ring_a, sem_a, seg_a), Ring(ring_b, sem_b, seg_b), Ring(ring_c, sem_c, seg_c)
    ra.prime()
    load(1, order[0], 0).start()

    chunk = 64
    cot_copy.wait()

    def widen(c, carry):
        rows = pl.ds(pl.multiple_of(c * chunk, chunk), chunk)
        e_buf[rows, :] = cot_buf[rows, :].astype(F32)
        return carry

    lax.fori_loop(0, slots // chunk, widen, 0)

    def norm_back(src, dst, gain_row, n_ref, r_ref):
        def step(c, carry):
            s_in, s_out = carry
            rows = pl.ds(pl.multiple_of(c * chunk, chunk), chunk)
            g = src[rows, :]
            n = n_ref[rows, :].astype(F32)
            ge = g * gain_row
            m1 = jnp.mean(ge, axis=1, keepdims=True)
            m2 = jnp.mean(ge * n, axis=1, keepdims=True)
            dz = r_ref[rows, :] * (ge - m1 - n * m2)
            dst[rows, :] = dz
            z_buf[rows, :] = dz.astype(BF)
            return (s_in + fold8(g), s_out + fold8(dz))

        zero = jnp.zeros((8, width), F32)
        s_in, s_out = lax.fori_loop(0, slots // chunk, step, (zero, zero))
        return jnp.sum(s_in, axis=0, keepdims=True), jnp.sum(s_out, axis=0, keepdims=True)

    for l in range(layers):
        grads[l, 10:13, :] = squares[3 * l : 3 * l + 3, :]
        grads[l, 13:14, :] = squares[3 * layers : 3 * layers + 1, :]
        grads[l, 14:16, :] = jnp.zeros((2, width), F32)
    if fused:
        grads[order[-1], 0:2, :] = jnp.zeros((2, width), F32)

    for step, l in enumerate(order):
        par = step % 2
        last = step == layers - 1
        early = fused and last

        load(0, l, par).wait()
        s_in, s_out = norm_back(e_buf, x_buf, gain[l, 1:2, :], n2_buf.at[par], r2[l])
        grads[l, 4:5, :] = s_in
        grads[l, 9:10, :] = s_out

        if step == 0:
            rb.prime()
            load(2, l, par).start()
        load(1, l, par).wait()
        wide = ring_a.shape[1]

        def down_body(j, w):
            cols = pl.ds(pl.multiple_of(j * wide, wide), wide)
            du = nt(z_buf[...], w) * sl_buf[par, :, cols].astype(F32)
            du_buf[:, cols] = du.astype(BF)
            part = jnp.sum(fold8(du), axis=0, keepdims=True)
            per = width // wide
            grads[l, pl.ds(5 + j // per, 1), pl.ds(pl.multiple_of(lax.rem(j, per) * wide, wide), wide)] = part

        ra.run(ff // wide, down_body)
        if step == 0:
            for which in range(3, 7):
                load(which, l, par).start()
            rc.prime()
        nb = ring_b.shape[1]

        def up_body(j, w):
            cols = pl.ds(pl.multiple_of(j * nb, nb), nb)
            x_buf[:, cols] = x_buf[:, cols] + nt(du_buf[...], w)

        rb.run(width // nb, up_body)
        if step + 1 < layers:
            for which in range(7):
                load(which, order[step + 1], 1 - par).start()

        load(2, l, par).wait()
        s_in, s_out = norm_back(x_buf, x_buf, gain[l, 0:1, :], n1_buf.at[par], r1[l])
        grads[l, 3:4, :] = s_in
        grads[l, 2:3, :] = s_out

        def out_body(j, w):
            cols = pl.ds(pl.multiple_of(j * wide, wide), wide)
            do_buf[:, cols] = nt(z_buf[...], w).astype(BF)

        ra.run(width // wide, out_body)

        for which in range(3, 7):
            load(which, l, par).wait()
        lane = lax.broadcasted_iota(jnp.int32, (1, 2 * hd), 1)
        sides = (lane < hd, lane >= hd)

        def pair(hp, carry):
            cols = pl.ds(pl.multiple_of(hp * 2 * hd, 2 * hd), 2 * hd)
            sum_q = jnp.zeros((8, 2 * hd), F32)
            sum_v = jnp.zeros((8, 2 * hd), F32)
            for b in range(2):
                rows = pl.ds(b * half, half)
                q2, k2, v2, do2 = (r[rows, cols] for r in (q_buf.at[par], k_buf.at[par], v_buf.at[par], do_buf))
                dq = dk = dv = None
                for side in range(2):
                    keep = sides[side]
                    zero = jnp.zeros_like(q2)
                    pb = pt_buf[par, 2 * hp + side, b]
                    dpt = nt(jnp.where(keep, v2, zero), do2)
                    p32 = pb.astype(F32)
                    t = p32 * dpt
                    inner = jnp.sum(fold8(t), axis=0, keepdims=True)
                    ds = (t - p32 * inner).astype(BF)
                    a_v = nn(pb, jnp.where(keep, do2, zero))
                    a_k = nn(ds, jnp.where(keep, q2, zero))
                    a_q = tn(ds, jnp.where(keep, k2, zero))
                    dv = a_v if dv is None else dv + a_v
                    dk = a_k if dk is None else dk + a_k
                    dq = a_q if dq is None else dq + a_q
                dq = dq * scale
                dk = dk * scale
                dp_buf[rows, cols] = dq.astype(BF)
                dp_buf[rows, pl.ds(pl.multiple_of(width + hp * 2 * hd, 2 * hd), 2 * hd)] = dk.astype(BF)
                dp_buf[rows, pl.ds(pl.multiple_of(2 * width + hp * 2 * hd, 2 * hd), 2 * hd)] = dv.astype(BF)
                sum_q = sum_q + fold8(dq)
                sum_v = sum_v + fold8(dv)
            terms = team.late if early else grads.at[l]
            terms[0:1, cols] = jnp.sum(sum_q, axis=0, keepdims=True)
            terms[1:2, cols] = jnp.sum(sum_v, axis=0, keepdims=True)
            return carry

        if early:
            team.met()
            team.spread(grads)
            lax.fori_loop(0, 3, pair, 0)
            team.along()
            lax.fori_loop(3, 6, pair, 0)
            team.back(summed)
            lax.fori_loop(6, heads // 2, pair, 0)
            team.late_spread()
        else:
            lax.fori_loop(0, heads // 2, pair, 0)
        nc = ring_c.shape[1]

        def qkv_body(j, w):
            cols = pl.ds(pl.multiple_of(j * nc, nc), nc)
            e_buf[:, cols] = x_buf[:, cols] + nt(dp_buf[...], w)
            if last:
                pltpu.make_async_copy(e_buf.at[:, cols], dh_out.at[:, cols], sem_out.at[0]).start()

        rc.run(width // nc // 2, qkv_body)
        if early:
            team.late_along()
        rc.run(width // nc // 2, qkv_body, width // nc // 2)

    if fused:
        summed[order[-1], 0:2, :] = team.close()
    for j in range(width // nc):
        cols = pl.ds(j * nc, nc)
        pltpu.make_async_copy(e_buf.at[:, cols], dh_out.at[:, cols], sem_out.at[0]).wait()


def backward(sizes, cot, gain, squares, kept):
    slots, width = cot.shape
    layers, heads = kept[1].shape[:2]
    ff = kept[2].shape[2]
    half = slots // 2
    hbm = pl.BlockSpec(memory_space=pl.ANY)
    vm = pl.BlockSpec(memory_space=pltpu.VMEM)
    ta, tb, tc = min(512, width), min(256, width), min(256, width)
    team = []
    params = {}
    if sizes == KERNEL_MESH:
        plane, line = 2 * sizes[0] * sizes[1], sizes[2]
        team = [
            pltpu.VMEM((layers, 16, width), F32),
            pltpu.VMEM((plane, layers, 16, width // plane), F32),
            pltpu.VMEM((line, layers, 16, width // plane), F32),
            pltpu.VMEM((layers, 16, width // plane), F32),
            pltpu.VMEM((2, width), F32),
            pltpu.VMEM((plane, 2, width), F32),
            pltpu.VMEM((line, 2, width), F32),
            pltpu.SemaphoreType.DMA((5,)),
            pltpu.SemaphoreType.DMA((5,)),
        ]
        params = dict(collective_id=1, has_side_effects=True)
    return pl.pallas_call(
        functools.partial(backward_kernel, layers, sizes),
        out_shape=(
            jax.ShapeDtypeStruct((slots, width), F32),
            jax.ShapeDtypeStruct((layers, 16, width), F32),
        ),
        in_specs=[hbm, vm, vm] + [hbm] * 5 + [vm] * 2 + [hbm] * 4,
        out_specs=(hbm, vm),
        scratch_shapes=[
            pltpu.VMEM((slots, width), F32),
            pltpu.VMEM((slots, width), F32),
            pltpu.VMEM((slots, width), BF),
            pltpu.VMEM((slots, ff), BF),
            pltpu.VMEM((slots, 3 * width), BF),
            pltpu.VMEM((slots, width), BF),
            pltpu.VMEM((slots, width), BF),
        ]
        + [pltpu.VMEM((2, slots, width), BF)] * 3
        + [
            pltpu.VMEM((2, heads, 2, half, half), BF),
            pltpu.VMEM((2, slots, ff), BF),
            pltpu.VMEM((2, slots, width), BF),
            pltpu.VMEM((2, slots, width), BF),
            pltpu.VMEM((4, ta, width), BF),
            pltpu.VMEM((3, tb, ff), BF),
            pltpu.VMEM((3, tc, 3 * width), BF),
            pltpu.SemaphoreType.DMA((4,)),
            pltpu.SemaphoreType.DMA((3,)),
            pltpu.SemaphoreType.DMA((3,)),
            pltpu.SemaphoreType.DMA((2, 7)),
            pltpu.SemaphoreType.DMA((1,)),
        ]
        + team,
        compiler_params=pltpu.CompilerParams(vmem_limit_bytes=67000000, **params),
        name="backward",
    )(cot, gain, squares, *kept)


class Relay:
    def __init__(self, fabric, kinds, per, count, sems):
        self.fab, self.kinds, self.per, self.count = fabric, kinds, per, count
        self.send, self.recv = sems
        at = fabric.at
        self.pair = lax.div(at["z"], 2) * 2
        self.other = 2 - self.pair
        self.mate = self.pair + 1 - lax.rem(at["z"], 2)
        self.inner = jnp.logical_or(at["z"] == 1, at["z"] == 2)

    def wait(self, sem, blocks):
        _, _, _, full, rows, cols = self.kinds[0]
        part = full.at[0, pl.ds(0, blocks * rows), pl.ds(0, cols // 2)]
        pltpu.make_async_copy(part, part, sem).wait()

    def each(self, t, act):
        l = lax.div(t, self.per)
        j = t - l * self.per
        for first, number, own, full, rows, cols in self.kinds:

            @pl.when(jnp.logical_and(j >= first, j < first + number))
            def _(first=first, own=own, full=full, rows=rows, cols=cols):
                for piece in range(2):
                    col = pl.multiple_of((j - first) * cols + piece * (cols // 2), cols // 2)
                    act(l, own, full, rows, pl.ds(col, cols // 2), piece)

    def push(self, t, piece, sem, device, src, dst):
        pltpu.make_async_remote_copy(
            src_ref=src,
            dst_ref=dst,
            send_sem=self.send.at[2 * t + piece, sem],
            recv_sem=self.recv.at[2 * t + piece, sem],
            device_id=device,
            device_id_type=pl.DeviceIdType.MESH,
        ).start()

    def stage(self, s, t):
        fab = self.fab
        at = fab.at
        partner = fab.device(c=1 - at["c"])

        @pl.when(jnp.logical_and(t >= 0, t < self.count))
        def _():
            for piece in range(2):
                if s == 1:
                    self.wait(self.recv.at[2 * t + piece, 0], 1)
                elif s == 2:
                    self.wait(self.recv.at[2 * t + piece, 1], 2)
                elif s == 3:
                    pl.when(self.inner)(lambda piece=piece: self.wait(self.recv.at[2 * t + piece, 2], 4))
                elif s == 4:
                    pl.when(jnp.logical_not(self.inner))(
                        lambda piece=piece: self.wait(self.recv.at[2 * t + piece, 2], 4)
                    )
                    self.wait(self.recv.at[2 * t + piece, 5], 4)
                elif s == 5:
                    self.wait(self.recv.at[2 * t + piece, 3], 4)

            def act(l, own, full, rows, cols, piece):
                u, v = (("x", "y"), ("y", "x"))[piece]

                def view(first, blocks):
                    return full.at[l, pl.ds(pl.multiple_of(first * rows, rows), blocks * rows), cols]

                def out(sem, device, runs):
                    for first, blocks in runs:
                        self.push(t, piece, sem, device, view(first, blocks), view(first, blocks))

                def runs(z, **moved):
                    return [(fab.block(**{u: each, "z": z, **moved}), 2) for each in range(2)]

                across = fab.device(**{v: 1 - at[v]})
                beyond = {v: 1 - at[v]}
                if s == 0:
                    mine = view(fab.block(), 1)
                    self.push(t, piece, 0, fab.device(z=self.mate), own.at[l, :, cols], mine)
                    self.push(t, piece, 4, partner, own.at[l, :, cols], mine)
                elif s == 1:
                    out(1, fab.device(**{u: 1 - at[u]}), [(fab.block(z=self.pair), 2)])
                    out(4, partner, [(fab.block(z=self.mate), 1)])
                elif s == 2:
                    pl.when(self.inner)(lambda: out(2, fab.device(z=3 - at["z"]), runs(self.pair)))
                    out(5, across, runs(self.pair))
                    out(4, partner, [(fab.block(**{u: 1 - at[u], "z": self.pair}), 2)])
                elif s == 3:

                    @pl.when(self.inner)
                    def _():
                        out(2, fab.device(z=self.mate), runs(self.other))
                        out(3, across, runs(self.other))
                        out(4, partner, runs(self.other))

                elif s == 4:

                    @pl.when(jnp.logical_not(self.inner))
                    def _():
                        out(3, across, runs(self.other))
                        out(4, partner, runs(self.other))

                    out(4, partner, runs(self.pair, **beyond))
                else:
                    out(4, partner, runs(self.other, **beyond))

            self.each(t, act)

    def finish(self, t):
        for piece in range(2):
            self.wait(self.recv.at[2 * t + piece, 4], 16)

    def drain(self, t):
        for piece in range(2):
            for sem, blocks in ((0, 1), (1, 2), (3, 4), (4, 16), (5, 4)):
                self.wait(self.send.at[2 * t + piece, sem], blocks)
            pl.when(self.inner)(lambda piece=piece: self.wait(self.send.at[2 * t + piece, 2], 8))


LEADS = (11, 9, 7, 5, 3, 1)


def forward_kernel(layers, sizes, *refs):
    (lens, tok, cot, gain, b_qv, b_out, b_ln, b_up, b_down, s_qkv, s_out, s_up, s_down) = refs[:13]
    (act, squares, back, cot_o, qkv_o, pt_o, sl_o, n1_o, n2_o, r1_o, r2_o, f_qkv, f_out, f_up, f_down) = refs[13:28]
    (
        h_buf, hb_buf, qkv_buf, mix_buf, gu_buf, f_buf, pt_buf, sl_buf, n_buf,
        ring_w, ring_t, own_qkv, own_out, own_up, own_down, turn, vcol, vrow,
        sem_send, sem_recv, sem_own, sem_ring, sem_save,
    ) = refs[28:]
    slots, width = tok.shape
    ff = gu_buf.shape[1]
    heads = pt_buf.shape[0]
    hd = width // heads
    half = slots // 2
    scale = hd ** (-0.5)
    tall = ring_t.shape[2]
    fab = Fabric(sizes)

    shards = ((s_qkv, own_qkv, f_qkv), (s_out, own_out, f_out), (s_up, own_up, f_up), (s_down, own_down, f_down))
    for at, (src, buf, _) in enumerate(shards):
        pltpu.make_async_copy(src, buf, sem_own.at[at]).start()
    pltpu.make_async_copy(cot, mix_buf, sem_save.at[3]).start()
    barrier = pltpu.get_barrier_semaphore()
    around = [fab.device(**{axis: peer}) for axis in ("z", "x", "y", "c") for peer in fab.peers(axis)]
    for device in around:
        pl.semaphore_signal(barrier, inc=1, device_id=device, device_id_type=pl.DeviceIdType.MESH)
    pl.semaphore_wait(barrier, len(around))

    ups, downs = ff // width, width // tall
    kinds = (
        (0, 3, s_qkv, f_qkv, s_qkv.shape[1], width),
        (3, 1, s_out, f_out, s_out.shape[1], width),
        (4, ups, s_up, f_up, s_up.shape[1], width),
        (4 + ups, downs, s_down, f_down, s_down.shape[1], tall),
    )
    per = 4 + ups + downs
    total = layers * per
    relay = Relay(fab, kinds, per, total, (sem_send, sem_recv))

    def save(src, dst, key):
        pltpu.make_async_copy(src, dst, sem_save.at[key]).start()

    def free(src, dst, key, when):
        pl.when(when)(lambda: pltpu.make_async_copy(src, dst, sem_save.at[key]).wait())

    chunk = 64
    steps = slots // chunk

    def rows_of(c):
        return pl.ds(pl.multiple_of(c * chunk, chunk), chunk)

    def tiles(w, lhs, count, body, tile=256):
        def step(j, carry):
            cols = pl.ds(pl.multiple_of(j * tile, tile), tile)
            body(cols, nn(lhs[...], w[:, cols]), j * tile)
            return carry

        lax.fori_loop(0, count // tile, step, 0)

    def norm(l, which, bias_row, base, branch, n_dst, r_dst):
        zero = jnp.zeros((8, width), F32)
        gain_row = gain[l, which : which + 1, :]
        shift_row = b_ln[l, which : which + 1, :]

        def step(c, carry):
            s_h, s_a = carry
            rows = rows_of(c)
            a = branch[rows, :] + bias_row
            h = base[rows, :]
            z = h + a
            mean = jnp.mean(z, axis=1, keepdims=True)
            centred = z - mean
            var = jnp.mean(centred * centred, axis=1, keepdims=True)
            inv = lax.rsqrt(var + 1e-06)
            n = centred * inv
            y = n * gain_row + shift_row
            base[rows, :] = y
            hb_buf[rows, :] = y.astype(BF)
            n_dst[rows, :] = n.astype(BF)
            r_dst[rows, :] = inv
            ok = vcol[rows, :]
            return s_h + fold8(ok * h * h), s_a + fold8(ok * a * a)

        return lax.fori_loop(0, steps, step, (zero, zero))

    def attention():
        lane = lax.broadcasted_iota(jnp.int32, (1, 2 * hd), 1)
        sides = (lane < hd, lane >= hd)

        def pair(hp, carry):
            cols = pl.ds(pl.multiple_of(hp * 2 * hd, 2 * hd), 2 * hd)
            for b in range(2):
                rows = pl.ds(b * half, half)
                q2, k2, v2 = qkv_buf[0, rows, cols], qkv_buf[1, rows, cols], qkv_buf[2, rows, cols]
                mixed = None
                for side in range(2):
                    keep = sides[side]
                    zero = jnp.zeros_like(q2)
                    st = nt(jnp.where(keep, k2, zero), q2) * scale
                    if b == 1:
                        st = jnp.where(vcol[rows, :] == vrow[:, rows], st, -1e30)
                    top = jnp.max(st, axis=0, keepdims=True)
                    ex = jnp.exp(st - top)
                    p = (ex * (1.0 / jnp.sum(ex, axis=0, keepdims=True))).astype(BF)
                    pt_buf[2 * hp + side, b] = p
                    o = tn(p, jnp.where(keep, v2, zero))
                    mixed = o if mixed is None else mixed + o
                mix_buf[rows, cols] = mixed.astype(BF)
            return carry

        lax.fori_loop(0, heads // 2, pair, 0)

    def compute(t):
        l = lax.div(t, per)
        j = t - l * per
        slot = lax.rem(t, 2)
        later = l > 0

        @pl.when(j < 3)
        def _():
            free(qkv_buf.at[j], qkv_o.at[0, j], j, later)
            keep = (j != 1).astype(F32)

            def body(cols, t, first):
                bias = b_qv[l, pl.ds(lax.div(j, 2), 1), cols] * keep
                qkv_buf[j, :, cols] = (t + bias).astype(BF)

            tiles(ring_w.at[slot], hb_buf, width, body)
            save(qkv_buf.at[j], qkv_o.at[l, j], j)

            @pl.when(j == 2)
            def _():
                free(pt_buf, pt_o.at[0], 3, later)
                attention()
                save(pt_buf, pt_o.at[l], 3)

        @pl.when(j == 3)
        def _():
            def body(cols, t, first):
                f_buf[:, cols] = t

            tiles(ring_w.at[slot], mix_buf, width, body)
            free(n_buf.at[0], n1_o.at[0], 4, later)
            s_h, s_a = norm(l, 0, b_out[pl.ds(l, 1), :], h_buf, f_buf, n_buf.at[0], r1_o.at[l])
            squares[pl.ds(3 * l, 1), :] = jnp.sum(s_h, axis=0, keepdims=True)
            squares[pl.ds(3 * l + 1, 1), :] = jnp.sum(s_a, axis=0, keepdims=True)
            save(n_buf.at[0], n1_o.at[l], 4)

        @pl.when(jnp.logical_and(j >= 4, j < 4 + ups))
        def _():
            part = j - 4
            par = lax.rem(part, 2)
            start = pl.multiple_of(part * width, width)
            free(sl_buf.at[par], sl_o.at[0, :, pl.ds(0, width)], 6 + par, jnp.logical_or(later, part >= 2))

            def body(cols, t, first):
                wide = pl.ds(pl.multiple_of(part * width + first, 256), 256)
                u = t + b_up[pl.ds(l, 1), wide]
                phi = 0.5 * (1.0 + lax.erf(u * 0.7071067811865476))
                sl_buf[par, :, cols] = (phi + u * (jnp.exp(-0.5 * u * u) * 0.3989422804014327)).astype(BF)
                gu_buf[:, wide] = (u * phi).astype(BF)

            tiles(ring_w.at[slot], hb_buf, width, body)
            save(sl_buf.at[par], sl_o.at[l, :, pl.ds(start, width)], 6 + par)

        @pl.when(j >= 4 + ups)
        def _():
            part = j - 4 - ups
            f_buf[:, pl.ds(pl.multiple_of(part * tall, tall), tall)] = nn(gu_buf[...], ring_t[slot])

            @pl.when(part == downs - 1)
            def _():
                free(n_buf.at[1], n2_o.at[0], 5, True)
                _, s_f = norm(l, 1, b_down[pl.ds(l, 1), :], h_buf, f_buf, n_buf.at[1], r2_o.at[l])
                squares[pl.ds(3 * l + 2, 1), :] = jnp.sum(s_f, axis=0, keepdims=True)
                save(n_buf.at[1], n2_o.at[l], 5)

    def ring_start(t):
        l = lax.div(t, per)
        j = t - l * per
        slot = lax.rem(t, 2)
        for first, number, _, full, _, cols in kinds:
            buf = ring_t if cols == tall else ring_w

            @pl.when(jnp.logical_and(j >= first, j < first + number))
            def _(first=first, full=full, cols=cols, buf=buf):
                src = full.at[l, :, pl.ds(pl.multiple_of((j - first) * cols, cols), cols)]
                pltpu.make_async_copy(src, buf.at[slot], sem_ring.at[slot]).start()

    def ring_wait(t):
        slot = lax.rem(t, 2)
        pltpu.make_async_copy(f_out.at[0], ring_w.at[slot], sem_ring.at[slot]).wait()

    for t in range(LEADS[0] - LEADS[1]):
        relay.stage(0, jnp.int32(t))
    for at, (src, buf, _) in enumerate(shards):
        pltpu.make_async_copy(src, buf, sem_own.at[at]).wait()
    placed = []
    for at, (_, buf, full) in enumerate(shards):
        rows = buf.shape[1]
        for l in range(layers):
            dst = full.at[l, pl.ds(pl.multiple_of(fab.block() * rows, rows), rows)]
            placed.append(pltpu.make_async_copy(buf.at[l], dst, sem_own.at[4 + at * layers + l]))
            placed[-1].start()

    first, second = lens[0, 0], lens[0, 1]
    shift = jnp.where(first == half, 0, first)
    back[0] = slots - shift

    def source(slot):
        return jnp.where(slot + shift >= slots, slot + shift - slots, slot + shift)

    vcol[...] = (source(lax.broadcasted_iota(jnp.int32, (slots, 1), 0)) < first + second).astype(F32)
    vrow[...] = (source(lax.broadcasted_iota(jnp.int32, (1, slots), 1)) < first + second).astype(F32)

    def turning(c, carry):
        rows = rows_of(c)
        slot = lax.broadcasted_iota(jnp.int32, (chunk, slots), 0) + c * chunk
        turn[rows, :] = (source(slot) == lax.broadcasted_iota(jnp.int32, (chunk, slots), 1)).astype(F32).astype(BF)
        return carry

    lax.fori_loop(0, steps, turning, 0)

    def turned(dst, src):
        def body(j, carry):
            cols = pl.ds(pl.multiple_of(j * 256, 256), 256)
            dst(cols, nn(turn[...], src[:, cols]))
            return carry

        lax.fori_loop(0, width // 256, body, 0)

    def put_tokens(cols, t):
        h_buf[:, cols] = t
        hb_buf[:, cols] = t.astype(BF)

    def put_cotangent(cols, t):
        n_buf[1, :, cols] = (t * vcol[...]).astype(BF)

    turned(put_tokens, tok)
    for copy in placed:
        copy.wait()

    def step(i, carry):
        at = i - LEADS[1]
        for s, lead in enumerate(LEADS):
            relay.stage(s, at + lead)

        @pl.when(i == 4)
        def _():
            pltpu.make_async_copy(cot, mix_buf, sem_save.at[3]).wait()
            turned(put_cotangent, mix_buf)
            save(n_buf.at[1], cot_o, 5)

        pl.when(jnp.logical_and(at >= 1, at <= total))(lambda: ring_wait(at - 1))

        @pl.when(jnp.logical_and(at >= 0, at < total))
        def _():
            relay.finish(at)
            ring_start(at)

        pl.when(at >= 1)(lambda: relay.drain(at - 1))
        pl.when(at >= 1)(lambda: compute(at - 1))
        return carry

    lax.fori_loop(0, total + 1 + LEADS[1], step, 0)
    pltpu.make_async_copy(hb_buf, act, sem_own.at[0]).start()
    here = jnp.sum(vcol[...], axis=0, keepdims=True)
    squares[3 * layers :, :] = jnp.broadcast_to(here, (squares.shape[0] - 3 * layers, width))
    for part in range(3):
        free(qkv_buf.at[part], qkv_o.at[0, part], part, True)
    free(pt_buf, pt_o.at[0], 3, True)
    free(n_buf.at[0], n1_o.at[0], 4, True)
    free(n_buf.at[1], n2_o.at[0], 5, True)
    for par in range(2):
        free(sl_buf.at[par], sl_o.at[0, :, pl.ds(0, width)], 6 + par, True)
    pltpu.make_async_copy(hb_buf, act, sem_own.at[0]).wait()


def forward(sizes, lengths, tokens, cotangent, gain, b_qv, b_out, b_ln, b_up, b_down, s_qkv, s_out, s_up, s_down):
    slots, width = tokens.shape
    layers = s_qkv.shape[0]
    ff = s_up.shape[2]
    half = slots // 2
    tall = width * width // ff
    hbm = pl.BlockSpec(memory_space=pl.ANY)
    vm = pl.BlockSpec(memory_space=pltpu.VMEM)
    chunks = layers * (4 + ff // width + width // tall)
    outs = [
        ((slots, width), BF, hbm),
        ((8, width), F32, vm),
        ((1,), jnp.int32, pl.BlockSpec(memory_space=pltpu.SMEM)),
        ((slots, width), BF, hbm),
        ((layers, 3, slots, width), BF, hbm),
        ((layers, HEADS, 2, half, half), BF, hbm),
        ((layers, slots, ff), BF, hbm),
        ((layers, slots, width), BF, hbm),
        ((layers, slots, width), BF, hbm),
        ((layers, slots, 1), F32, vm),
        ((layers, slots, 1), F32, vm),
        ((layers, width, 3 * width), BF, hbm),
        ((layers, width, width), BF, hbm),
        ((layers, width, ff), BF, hbm),
        ((layers, ff, width), BF, hbm),
    ]
    result = pl.pallas_call(
        functools.partial(forward_kernel, layers, sizes),
        out_shape=tuple(jax.ShapeDtypeStruct(shape, kind) for shape, kind, _ in outs),
        in_specs=[pl.BlockSpec(memory_space=pltpu.SMEM), vm, hbm] + [vm] * 6 + [hbm] * 4,
        out_specs=tuple(spec for _, _, spec in outs),
        scratch_shapes=[
            pltpu.VMEM((slots, width), F32),
            pltpu.VMEM((slots, width), BF),
            pltpu.VMEM((3, slots, width), BF),
            pltpu.VMEM((slots, width), BF),
            pltpu.VMEM((slots, ff), BF),
            pltpu.VMEM((slots, width), F32),
            pltpu.VMEM((HEADS, 2, half, half), BF),
            pltpu.VMEM((2, slots, width), BF),
            pltpu.VMEM((2, slots, width), BF),
            pltpu.VMEM((2, width, width), BF),
            pltpu.VMEM((2, ff, tall), BF),
            pltpu.VMEM(s_qkv.shape, BF),
            pltpu.VMEM(s_out.shape, BF),
            pltpu.VMEM(s_up.shape, BF),
            pltpu.VMEM(s_down.shape, BF),
            pltpu.VMEM((slots, slots), BF),
            pltpu.VMEM((slots, 1), F32),
            pltpu.VMEM((1, slots), F32),
            pltpu.SemaphoreType.DMA((2 * chunks, 6)),
            pltpu.SemaphoreType.DMA((2 * chunks, 6)),
            pltpu.SemaphoreType.DMA((4 + 4 * layers,)),
            pltpu.SemaphoreType.DMA((2,)),
            pltpu.SemaphoreType.DMA((8,)),
        ],
        compiler_params=pltpu.CompilerParams(vmem_limit_bytes=62 << 20, collective_id=0, has_side_effects=True),
        name="forward",
    )(lengths, tokens, cotangent, gain, b_qv, b_out, b_ln, b_up, b_down, s_qkv, s_out, s_up, s_down)
    return result[0], result[1], result[2], result[3], list(result[4:])


def normalize(stream, gain_row, shift_row):
    mean_row = jnp.mean(stream, axis=-1, keepdims=True)
    centred = stream - mean_row
    variance = jnp.mean(centred * centred, axis=-1, keepdims=True)
    inv_std = lax.rsqrt(variance + 1e-06)
    normed = centred * inv_std
    return normed * gain_row + shift_row, normed, inv_std


def turned_by(a, by):
    return lax.dynamic_slice_in_dim(jnp.concatenate([a, a], axis=0), by, a.shape[0], axis=0)


def forward_apart(lengths, tokens, cotangent, gain, b_qv, b_out, b_ln, b_up, b_down, *shards):
    slots, width = tokens.shape
    shift = jnp.where(lengths[0, 0] == slots // 2, 0, lengths[0, 0])
    place = lax.rem(jnp.arange(slots, dtype=jnp.int32) + shift, slots)
    vcol = (place < lengths[0, 0] + lengths[0, 1]).astype(F32)[:, None]
    tokens = turned_by(tokens, shift)
    masked = turned_by(cotangent, shift) * vcol.astype(BF)
    layers = b_out.shape[0]
    half = slots // 2
    hd = width // HEADS
    blocks = vcol.reshape(2, half)
    same = blocks[:, :, None] == blocks[:, None, :]
    stream = tokens.astype(F32)
    kept = []
    squares = []
    for l in range(layers):
        mats = [lax.all_gather(w[l], AXES, axis=0, tiled=True) for w in shards]
        projected = nn(stream.astype(BF), mats[0])
        q = (projected[:, :width] + b_qv[l, 0]).astype(BF)
        k = projected[:, width : 2 * width].astype(BF)
        v = (projected[:, 2 * width :] + b_qv[l, 1]).astype(BF)
        q4, k4, v4 = (a.reshape(2, half, HEADS, hd) for a in (q, k, v))
        st = jnp.einsum("bqhd,bkhd->hbkq", q4, k4, preferred_element_type=F32) * hd ** (-0.5)
        st = jnp.where(same[None], st, -1e30)
        ex = jnp.exp(st - jnp.max(st, axis=2, keepdims=True))
        pt = (ex / jnp.sum(ex, axis=2, keepdims=True)).astype(BF)
        mixed = jnp.einsum("hbkq,bkhd->bqhd", pt, v4, preferred_element_type=F32).reshape(slots, width).astype(BF)
        branch = nn(mixed, mats[1]) + b_out[l]
        x1, n1, r1 = normalize(stream + branch, gain[l, 0], b_ln[l, 0])
        u = nn(x1.astype(BF), mats[2]) + b_up[l]
        phi = 0.5 * (1.0 + lax.erf(u * 0.7071067811865476))
        slope = (phi + u * (jnp.exp(-0.5 * u * u) * 0.3989422804014327)).astype(BF)
        ffn = nn((u * phi).astype(BF), mats[3]) + b_down[l]
        nxt, n2, r2 = normalize(x1 + ffn, gain[l, 1], b_ln[l, 1])
        squares += [jnp.sum(vcol * a * a, axis=0) for a in (stream, branch, ffn)]
        kept.append((jnp.stack([q, k, v]), pt, slope, n1.astype(BF), n2.astype(BF), r1, r2, *mats))
        stream = nxt
    here = jnp.broadcast_to(jnp.sum(vcol), (width,))
    return stream.astype(BF), jnp.stack(squares + [here] * (8 - 3 * layers)), (slots - shift)[None], masked, [jnp.stack(a) for a in zip(*kept)]


def local(
    sizes, tokens, lengths, w_qkv, w_out, w_up, w_down, ln_gain, bias_qv, bias_out, ln_bias, bias_up, bias_down, cotangent
):
    slots, width = tokens.shape
    layers = w_qkv.shape[0]
    run = functools.partial(forward, sizes) if sizes == KERNEL_MESH else forward_apart
    act, squares, back, cot, kept = run(
        lengths, tokens, cotangent, ln_gain, bias_qv, bias_out, ln_bias, bias_up, bias_down, w_qkv, w_out, w_up, w_down
    )
    dh, whole = backward(sizes, cot, ln_gain, squares, kept)
    if sizes != KERNEL_MESH:
        whole = lax.psum(whole, AXES)
    back = back[0].astype(jnp.uint32)
    return (
        turned_by(act, back),
        turned_by(dh, back),
        whole[:, 0:2],
        whole[:, 2],
        whole[:, 3:5],
        whole[:, 5:9].reshape(layers, -1),
        whole[:, 9],
        jnp.sqrt(jnp.sum(whole[:, 10:13], axis=2) / (whole[:, 13, 0:1] * width)),
    )


def solution(mesh):
    pairs = mesh.shape["dp"] // 2
    ny = next(n for n in range(math.isqrt(pairs), 0, -1) if pairs % n == 0)
    sizes = (ny, pairs // ny, mesh.shape["shard"])
    rows = P(AXES, None)
    weight = P(None, AXES, None)
    in_specs = (rows, rows, weight, weight, weight, weight, P(), P(), P(), P(), P(), P(), rows)
    out_specs = (rows, rows, P(), P(), P(), P(), P(), P())
    return jax.shard_map(
        functools.partial(local, sizes), mesh=mesh, in_specs=in_specs, out_specs=out_specs, check_vma=False
    )
```
